32 devices in a mesh: groups: 2 (over y), ctx: 4 (over z), mp: 4 (over x, core).
Axes of the slice: x: 2, y: 2, z: 4, core: 2. Of those that a mesh axis runs over, the one named last changes fastest.
Arguments:
- streams: bfloat16 [3, 2048, 4096], P(None, ('groups', 'ctx'), 'mp'), parts along dimension 1, may hold values from -6 to 6
- short_filter: float32 [3, 3, 4096], P(None, None, 'mp'), may hold values from -3 to 3
- mode_params: float32 [2, 4096, 8], P(None, 'mp'), may hold values from -2 to 2, as said below
- out_weight: bfloat16 [4096, 4096], P('mp', 'ctx'), may hold values from -0.09375 to 0.09375
- norm_gain: float32 [4096], P('mp'), may hold values from 0.5 to 1.5
- unembed: bfloat16 [4096, 512], P('mp'), may hold values from -40 to 40
- native: int32 [2048], P(('groups', 'ctx')), parts along dimension 0, may hold values from 0 to 511
- mut_pos: int32 [512], P('groups'), parts along dimension 0, may hold values from 0 to 1023
- mut_ids: int32 [512], P('groups'), parts along dimension 0, may hold values from 0 to 511
Outputs:
- loglik: float32 [2048], P(('groups', 'ctx')), parts along dimension 0
- scores: float32 [512], P('groups'), parts along dimension 0
The draws below stay inside these ranges and needn't reach their ends.
There are 2 independent parts, one for each index of `groups`. The reference program is written for one: setup_inputs(seed, part) draws one part's arguments, and reference() takes and returns one part's arrays. A program takes and returns all parts, laid end to end along the dimension named above; an argument that names none is the same for every part. Nothing has to cross between parts.
Inputs may be any that keep to these rules, and one draw needn't show every extreme that they name: mode_params[0] holds positive decay rates, mode_params[1] residues.
All inputs are finite; a program needn't handle non-finite values.
Results may differ from the reference program's by a relative error of at most 0.0065.
Values may be sent and summed in bfloat16 or wider, within the bound.
No kernel may reach another device: no remote copies, remote signals or barrier semaphores. Data moves between devices by JAX's collectives and lax.ppermute only.
A program may use at most 192 MiB of HBM per device.

```python
import math
import jax
import jax.numpy as jnp
from jax import lax

D = 4096
VOCAB = 512
MODES = 8
KERNEL = 3
NMUT = 256
LENGTH = 1024


def draw_mode_params(key, part):
    key_a, key_b, key_c = jax.random.split(key, 3)
    placing = jax.random.uniform(key_a, (D, MODES), jnp.float32)
    chooser = jax.random.uniform(key_b, (D, MODES), jnp.float32)
    share = 0.5
    noise = jnp.clip(jax.random.normal(key_c, (D, MODES), jnp.float32), -4.0, 4.0)
    slow_low = math.log(0.1 / LENGTH)
    slow_high = math.log(2.0 / LENGTH)
    slow = jnp.exp(slow_low + placing * (slow_high - slow_low))
    fast_low = math.log(1.0 / 50.0)
    fast_high = math.log(1.0 / 30.0)
    fast = jnp.exp(fast_low + placing * (fast_high - fast_low))
    decays = jnp.where(chooser < share, slow, fast)
    residue = noise * jnp.sqrt(2.0 * decays)
    return jnp.stack([decays, residue])


def draw_unembed(key, part):
    key_a = jax.random.fold_in(key, 0)
    base = jax.random.normal(key_a, (D, VOCAB), jnp.float32) * (3.0 / math.sqrt(D))
    return jnp.clip(base, -40.0, 40.0).astype(jnp.bfloat16)


def place_ends(drawn, own_key, least, top_value):
    longest = drawn.shape.index(max(drawn.shape))
    spots = []
    for shift in (0, 1):
        where = [jax.random.randint(jax.random.fold_in(own_key, axis), (), 0, length) for axis, length in enumerate(drawn.shape)]
        where[longest] = (where[longest] + shift) % drawn.shape[longest]
        spots.append(tuple(where))
    return drawn.at[spots[0]].set(least).at[spots[1]].set(top_value)


def level_of(rng, extent, cuts, low, top_value):
    level = 1.0
    for position, shards_of in cuts:
        draws = jax.random.uniform(jax.random.fold_in(jax.random.fold_in(rng, 6), position), (shards_of,), jnp.float32, low / len(cuts), top_value / len(cuts))
        level = level * jnp.repeat(jnp.exp(draws), extent[position] // shards_of).reshape((-1,) + (1,) * (len(extent) - 1 - position))
    return level


def centred(own_key, extent, scale, reach, shards=(), held_as=jnp.bfloat16):
    array = jax.random.normal(own_key, extent, jnp.float32) * scale
    if len(shards) > 0:
        array = level_of(own_key, extent, shards, -0.22, 0.18) * array
    return jnp.clip(array, min=-reach, max=reach).astype(held_as)


def setup_inputs(seed: int = 0, part: int = 0) -> dict:
    key_list = jax.random.split(jax.random.key(seed), 10)
    own_keys = jax.random.split(jax.random.fold_in(key_list[9], part), 10)
    return {
        "streams": centred(own_keys[0], (3, LENGTH, D), 1.0, 6.0, ((1, 4), (2, 4))),
        "short_filter": centred(key_list[1], (3, KERNEL, D), 0.5, 3.0, ((2, 4),), jnp.float32),
        "mode_params": draw_mode_params(jax.random.fold_in(key_list[9], 71), part),
        "out_weight": centred(key_list[3], (D, D), D ** -0.5, 0.09375, ((0, 4), (1, 4))),
        "norm_gain": jnp.clip(1.0 + 0.1 * jax.random.normal(key_list[4], (D,), jnp.float32), 0.5, 1.5),
        "unembed": draw_unembed(jax.random.fold_in(key_list[9], 71), part),
        "native": place_ends(jax.random.randint(own_keys[6], (LENGTH,), 0, VOCAB), jax.random.fold_in(own_keys[6], 1), 0, VOCAB - 1).astype(jnp.int32),
        "mut_pos": place_ends(jax.random.randint(own_keys[7], (NMUT,), 0, LENGTH), jax.random.fold_in(own_keys[7], 1), 0, LENGTH - 1).astype(jnp.int32),
        "mut_ids": place_ends(jax.random.randint(own_keys[8], (NMUT,), 0, VOCAB), jax.random.fold_in(own_keys[8], 1), 0, VOCAB - 1).astype(jnp.int32),
    }


PRECISE = lax.Precision.HIGHEST

def short_mix(padded, short_filter, seq_rows):
    return short_filter[:, 0, None, :] * padded[:, 2:, :] + short_filter[:, 1, None, :] * padded[:, 1:seq_rows + 1, :] + short_filter[:, 2, None, :] * padded[:, 0:seq_rows, :]

def carry_terms(starts, decays, residue, span_len):
    lag_steps = jnp.arange(span_len, dtype=jnp.float32)
    weights = residue[None] * jnp.exp(-decays[None] * (lag_steps + 1.0)[:, None, None])
    return jnp.einsum('ncm,tcm->ntc', starts, weights, precision=PRECISE)

def span_conv(values, decays, residue, span_len):
    seq_all, channels = values.shape
    spans = seq_all // span_len
    lag_steps = jnp.arange(span_len, dtype=jnp.float32)
    powers = jnp.exp(-decays[None] * lag_steps[:, None, None])
    kernel = lax.optimization_barrier(jnp.sum(residue[None] * powers, axis=2))
    offsets = jnp.arange(span_len, dtype=jnp.int32)
    spread = offsets[:, None] - offsets[None, :]
    toeplitz = jnp.where((spread >= 0)[:, :, None], kernel[jnp.clip(spread, 0, span_len - 1)], 0.0)
    blocked = values.reshape(spans, span_len, channels)
    inside = jnp.einsum('tsc,nsc->ntc', toeplitz, blocked, precision=PRECISE)
    tail_pows = jnp.exp(-decays[None] * (span_len - 1.0 - lag_steps)[:, None, None])
    own_states = jnp.einsum('nsc,scm->ncm', blocked, tail_pows, precision=PRECISE)
    factor = jnp.exp(-decays * span_len)

    def advance(carried, own_part):
        return (factor * carried + own_part, carried)
    end_state, starts = lax.scan(advance, jnp.zeros_like(factor), own_states)
    result = inside + carry_terms(starts, decays, residue, span_len)
    return (result.reshape(seq_all, channels), end_state)

def reference(streams, short_filter, mode_params, out_weight, norm_gain, unembed, native, mut_pos, mut_ids):
    seq_rows = streams.shape[1]
    padded = jnp.pad(streams.astype(jnp.float32), ((0, 0), (2, 0), (0, 0)))
    mixed = short_mix(padded, short_filter, seq_rows)
    gate_bf = lax.optimization_barrier(mixed[0].astype(jnp.bfloat16))
    product = (mixed[1] * mixed[2]).astype(jnp.bfloat16)
    span_len = min(64, seq_rows)
    conv_sum, unused = span_conv(product.astype(jnp.float32), mode_params[0], mode_params[1], span_len)
    conv_bf = lax.optimization_barrier(conv_sum.astype(jnp.bfloat16))
    gated = (gate_bf.astype(jnp.float32) * conv_bf.astype(jnp.float32)).astype(jnp.bfloat16)
    output = jnp.dot(gated, out_weight, preferred_element_type=jnp.float32)
    squares = lax.optimization_barrier(jnp.sum(output * output, axis=1, keepdims=True))
    normed = (output * lax.rsqrt(squares / D + 1e-05) * norm_gain).astype(jnp.bfloat16)
    logits = jnp.dot(normed, unembed, preferred_element_type=jnp.float32)
    totals = jax.nn.logsumexp(logits, axis=1)
    picked = jnp.take_along_axis(logits, native[:, None], axis=1)[:, 0]
    loglik = picked - totals
    chosen = jnp.take_along_axis(logits[mut_pos], mut_ids[:, None], axis=1)[:, 0]
    scores = chosen - picked[mut_pos]
    return (loglik, scores)
```

```python
import functools

import jax
import jax.numpy as jnp
from jax import lax
from jax.experimental import pallas as pl
from jax.experimental.pallas import tpu as pltpu
from jax.sharding import PartitionSpec as P

F32 = jnp.float32
BF16 = jnp.bfloat16
LANES = 128
SUBS = 8
EPS = 1e-05


def swap(value, axis, bit):
    count = lax.axis_size(axis)
    return lax.ppermute(value, axis, [(i, i ^ bit) for i in range(count)])


def rows_of(ref, start, size):
    return ref[pl.ds(pl.multiple_of(start, size), size), :]


def mix(taps, now, back1, back2):
    return taps[0] * now + taps[1] * back1 + taps[2] * back2


def rounded(value):
    return value.astype(BF16).astype(F32)


def taps_of(filt_ref, stream, cols):
    return [filt_ref[stream, j : j + 1, cols] for j in range(3)]


def local_kernel(steps, modes, x_ref, filt_ref, mode_ref, nat_ref, y_ref, gate_ref, start_ref, msg_ref, xs, gs):
    rows = steps * SUBS
    for tile in range(x_ref.shape[2] // LANES):
        cols = slice(tile * LANES, (tile + 1) * LANES)
        sub = lax.broadcasted_iota(jnp.int32, (SUBS, LANES), 0)
        for i in range(3):
            xs[i] = x_ref[i, :, cols].astype(F32)
        decay = [jnp.broadcast_to(mode_ref[0, m : m + 1, cols], (SUBS, LANES)) for m in range(modes)]
        res = [jnp.broadcast_to(mode_ref[1, m : m + 1, cols], (SUBS, LANES)) for m in range(modes)]
        fall = [jnp.exp(-d) for d in decay]
        taps = [taps_of(filt_ref, i, cols) for i in range(3)]

        def at(i, t):
            return xs[i, pl.ds(t, SUBS, stride=steps), :]

        def behind(value):
            return jnp.where(sub == 0, 0.0, pltpu.roll(value, 1, 0))

        back2 = [behind(at(i, steps - 2)) for i in range(3)]
        back1 = [behind(at(i, steps - 1)) for i in range(3)]
        state = [jnp.zeros((SUBS, LANES), F32) for _ in range(modes)]
        for t in range(steps):
            now = [at(i, t) for i in range(3)]
            mixed = [mix(taps[i], now[i], back1[i], back2[i]) for i in range(3)]
            back2, back1 = back1, now
            gs[pl.ds(t, SUBS, stride=steps), :] = mixed[0]
            prod = rounded(mixed[1] * mixed[2])
            if t < 2:
                prod = jnp.where(sub == 0, 0.0, prod)
            state = [f * s + prod for f, s in zip(fall, state)]
            y_ref[t * SUBS : (t + 1) * SUBS, cols] = functools.reduce(
                lambda p, q: p + q, [r * s for r, s in zip(res, state)]
            )
        gate_ref[:, cols] = gs[...].astype(BF16)
        ends = []
        for m in range(modes):
            total = state[m]
            for reach in (1, 2, 4):
                power = jnp.exp(-decay[m] * float(steps * reach))
                total = total + jnp.where(sub < reach, 0.0, power * pltpu.roll(total, reach, 0))
            start_ref[m * SUBS : (m + 1) * SUBS, cols] = behind(total)
            ends.append(total[SUBS - 1 : SUBS, :])
        end = jnp.concatenate(ends, axis=0)
        high = rounded(end)
        first = [xs[i, 0:2, :] for i in range(3)]
        last = [xs[i, rows - 2 : rows, :] for i in range(3)]
        edge = jnp.concatenate([first[1], first[2], last[1], last[2]], axis=0)
        other = jnp.concatenate(
            [last[0], first[0], nat_ref[0:1, cols], jnp.zeros((3, LANES), F32)], axis=0
        )
        msg_ref[:, cols] = jnp.concatenate([high, end - high, edge, other], axis=0).astype(BF16)


def local_part(streams, filt, modes_t, nat_row):
    rows, width = streams.shape[1:]
    modes = modes_t.shape[1]
    steps = rows // SUBS
    block = 2 * LANES
    msg_rows = 2 * modes + 16
    return pl.pallas_call(
        functools.partial(local_kernel, steps, modes),
        grid=(width // block,),
        in_specs=[
            pl.BlockSpec((3, rows, block), lambda c: (0, 0, c)),
            pl.BlockSpec((3, 3, block), lambda c: (0, 0, c)),
            pl.BlockSpec((2, modes, block), lambda c: (0, 0, c)),
            pl.BlockSpec((1, block), lambda c: (0, c)),
        ],
        out_specs=[
            pl.BlockSpec((rows, block), lambda c: (0, c)),
            pl.BlockSpec((rows, block), lambda c: (0, c)),
            pl.BlockSpec((modes * SUBS, block), lambda c: (0, c)),
            pl.BlockSpec((msg_rows, block), lambda c: (0, c)),
        ],
        out_shape=[
            jax.ShapeDtypeStruct((rows, width), F32),
            jax.ShapeDtypeStruct((rows, width), BF16),
            jax.ShapeDtypeStruct((modes * SUBS, width), F32),
            jax.ShapeDtypeStruct((msg_rows, width), BF16),
        ],
        scratch_shapes=[pltpu.VMEM((3, rows, LANES), F32), pltpu.VMEM((rows, LANES), F32)],
        compiler_params=pltpu.CompilerParams(vmem_limit_bytes=24 * 2**20),
        cost_estimate=pl.CostEstimate(flops=rows * width * 64, bytes_accessed=rows * width * 12, transcendentals=0),
        name="local_part",
    )(streams, filt, modes_t, nat_row)


def carry_kernel(steps, modes, stacked, count, where_ref, filt_ref, mode_ref, y_ref, gate_ref, start_ref, *rest):
    msg_refs, (out_ref, held, conv) = rest[:-3], rest[-3:]
    me = where_ref[0]
    rows = steps * SUBS
    base = 2 * modes
    for tile in range(y_ref.shape[1] // LANES):
        cols = slice(tile * LANES, (tile + 1) * LANES)
        sub = lax.broadcasted_iota(jnp.int32, (SUBS, LANES), 0)
        for k in range(count):
            if stacked:
                held[k] = msg_refs[0][k, :, cols].astype(F32)
            else:
                held[me ^ k] = msg_refs[k][:, cols].astype(F32)
        decay = mode_ref[0, :, cols]
        taps = [taps_of(filt_ref, i, cols) for i in range(3)]

        def firsts(own, prior, keep):
            pair = []
            for i, lane in ((1, 0), (2, 2)):
                f0 = own[base + lane : base + lane + 1, :]
                f1 = own[base + lane + 1 : base + lane + 2, :]
                l2 = jnp.where(keep, prior[base + lane + 4 : base + lane + 5, :], 0.0)
                l1 = jnp.where(keep, prior[base + lane + 5 : base + lane + 6, :], 0.0)
                pair.append((mix(taps[i], f0, l1, l2), mix(taps[i], f1, f0, l1)))
            return rounded(pair[0][0] * pair[1][0]), rounded(pair[0][1] * pair[1][1])

        full = jnp.exp(-decay * float(rows))
        near0 = jnp.exp(-decay * float(rows - 1))
        near1 = jnp.exp(-decay * float(rows - 2))

        def advance(b, entering):
            own = held[b]
            p0, p1 = firsts(own, held[jnp.maximum(b - 1, 0)], b > 0)
            end = own[0:modes, :] + own[modes : 2 * modes, :] + near0 * p0 + near1 * p1
            return jnp.where(b < me, full * entering + end, entering)

        entering = jnp.zeros((modes, LANES), F32)
        if count <= 8:
            for b in range(count - 1):
                entering = advance(b, entering)
        else:
            entering = lax.fori_loop(0, count - 1, advance, entering)
        own = held[me]
        prior = held[jnp.maximum(me - 1, 0)]
        p0, p1 = firsts(own, prior, me > 0)
        later = (
            jnp.exp(-decay * float(steps)) * entering
            + jnp.exp(-decay * float(steps - 1)) * p0
            + jnp.exp(-decay * float(steps - 2)) * p1
        )
        shift = float(steps) * jnp.maximum(sub - 1, 0).astype(F32)
        fall, res, flow = [], [], []
        for m in range(modes):
            d = jnp.broadcast_to(decay[m : m + 1, :], (SUBS, LANES))
            r = jnp.broadcast_to(mode_ref[1, m : m + 1, cols], (SUBS, LANES))
            fall.append(jnp.exp(-d))
            res.append(r)
            begin = jnp.where(sub == 0, entering[m : m + 1, :], jnp.exp(-d * shift) * later[m : m + 1, :])
            flow.append(r * (start_ref[m * SUBS : (m + 1) * SUBS, cols] + begin))
        inject = (p0, p1)
        for t in range(steps):
            flow = [f * v for f, v in zip(fall, flow)]
            if t < 2:
                extra = jnp.where(sub == 0, inject[t], 0.0)
                flow = [v + r * extra for v, r in zip(flow, res)]
            conv[pl.ds(t, SUBS, stride=steps), :] = functools.reduce(
                lambda p, q: p + q, flow, y_ref[t * SUBS : (t + 1) * SUBS, cols]
            )
        g0 = own[base + 10 : base + 11, :]
        g1 = own[base + 11 : base + 12, :]
        l2 = jnp.where(me > 0, prior[base + 8 : base + 9, :], 0.0)
        l1 = jnp.where(me > 0, prior[base + 9 : base + 10, :], 0.0)
        head0 = mix(taps[0], g0, l1, l2)
        head1 = mix(taps[0], g1, g0, l1)
        gate = gate_ref[:, cols].astype(F32)
        line = lax.broadcasted_iota(jnp.int32, (16, LANES), 0)
        head = jnp.where(line == 0, rounded(head0), jnp.where(line == 1, rounded(head1), gate[0:16, :]))
        out_ref[0:16, cols] = (head * rounded(conv[0:16, :])).astype(BF16)
        out_ref[16:rows, cols] = (gate[16:rows, :] * rounded(conv[16:rows, :])).astype(BF16)


def carry_part(me, filt, modes_t, y, gate, start, msgs, stacked):
    rows, width = y.shape
    modes = modes_t.shape[1]
    steps = rows // SUBS
    block = 2 * LANES
    count = msgs[0].shape[0] if stacked else len(msgs)
    msg_rows = msgs[0].shape[-2]
    if stacked:
        msg_specs = [pl.BlockSpec((count, msg_rows, block), lambda c, w: (0, 0, c))]
    else:
        msg_specs = [pl.BlockSpec((msg_rows, block), lambda c, w: (0, c))] * count
    return pl.pallas_call(
        functools.partial(carry_kernel, steps, modes, stacked, count),
        grid_spec=pltpu.PrefetchScalarGridSpec(
            num_scalar_prefetch=1,
            grid=(width // block,),
            in_specs=[
                pl.BlockSpec((3, 3, block), lambda c, w: (0, 0, c)),
                pl.BlockSpec((2, modes, block), lambda c, w: (0, 0, c)),
                pl.BlockSpec((rows, block), lambda c, w: (0, c)),
                pl.BlockSpec((rows, block), lambda c, w: (0, c)),
                pl.BlockSpec((modes * SUBS, block), lambda c, w: (0, c)),
            ]
            + msg_specs,
            out_specs=pl.BlockSpec((rows, block), lambda c, w: (0, c)),
            scratch_shapes=[pltpu.VMEM((count, msg_rows, LANES), F32), pltpu.VMEM((rows, LANES), F32)],
        ),
        out_shape=jax.ShapeDtypeStruct((rows, width), BF16),
        compiler_params=pltpu.CompilerParams(vmem_limit_bytes=24 * 2**20),
        cost_estimate=pl.CostEstimate(flops=rows * width * 32, bytes_accessed=rows * width * 8, transcendentals=0),
        name="carry_part",
    )(me, filt, modes_t, y, gate, start, *msgs)


def as_row(col, width):
    rows = col.shape[0]
    r = lax.broadcasted_iota(jnp.int32, (rows, width), 0)
    c = lax.broadcasted_iota(jnp.int32, (rows, width), 1)
    return jnp.sum(jnp.where(r == c, col, 0.0), axis=0, keepdims=True)


def exact_dot(onehot, values):
    high = values.astype(BF16)
    low = (values - high.astype(F32)).astype(BF16)
    return jnp.dot(onehot, high, preferred_element_type=F32) + jnp.dot(onehot, low, preferred_element_type=F32)


def logit_kernel(share, where_ref, un_ref, row_ref, id_ref, nat_ref, *rest):
    slots = where_ref.shape[0]
    slot_refs, (part_ref, square_ref, score_ref, acc) = rest[:slots], rest[slots:]
    for k in range(slots):
        acc[pl.ds(pl.multiple_of(where_ref[k] * share, share), share), :] = slot_refs[k][...]
    values = acc[...]
    total = values.shape[0]
    square_ref[...] = as_row(jnp.sum(values * values, axis=1, keepdims=True), total)
    part = jnp.dot(values.astype(BF16), un_ref[...], preferred_element_type=F32)
    part_ref[...] = part
    muts = row_ref.shape[0]
    vocab = part.shape[1]
    spots = lax.broadcasted_iota(jnp.int32, (muts, total), 1)
    picked = exact_dot((spots == row_ref[...]).astype(BF16), part)
    words = lax.broadcasted_iota(jnp.int32, (muts, vocab), 1)
    gain = jnp.where(words == id_ref[...], picked, 0.0) - jnp.where(words == nat_ref[...], picked, 0.0)
    score_ref[...] = as_row(jnp.sum(gain, axis=1, keepdims=True), muts)


def logit_part(where, slots, un, mut_row, mut_id, mut_nat):
    share, wide = slots[0].shape
    total = share * len(slots)
    vocab = un.shape[1]
    muts = mut_row.shape[0]
    whole = pl.BlockSpec(memory_space=pltpu.VMEM)
    return pl.pallas_call(
        functools.partial(logit_kernel, share),
        in_specs=[pl.BlockSpec(memory_space=pltpu.SMEM)] + [whole] * (4 + len(slots)),
        out_specs=[whole] * 3,
        out_shape=[
            jax.ShapeDtypeStruct((total, vocab), F32),
            jax.ShapeDtypeStruct((1, total), F32),
            jax.ShapeDtypeStruct((1, muts), F32),
        ],
        scratch_shapes=[pltpu.VMEM((total, wide), F32)],
        compiler_params=pltpu.CompilerParams(vmem_limit_bytes=40 * 2**20),
        name="logit_part",
    )(where, un, mut_row, mut_id, mut_nat, *slots)


def final_kernel(feats, where_ref, log_ref, square_ref, score_ref, nat_ref, row_ref, out_ref):
    me, piece = where_ref[0], where_ref[1]
    share, vocab = log_ref.shape
    total = square_ref.shape[1]
    muts = score_ref.shape[1]
    width = out_ref.shape[1]
    scale_row = lax.rsqrt(square_ref[...] / feats + EPS)
    r = lax.broadcasted_iota(jnp.int32, (share, total), 0)
    c = lax.broadcasted_iota(jnp.int32, (share, total), 1)
    scale = jnp.sum(jnp.where(c == r + me * share, scale_row, 0.0), axis=1, keepdims=True)
    logits = log_ref[...] * scale
    top = jnp.max(logits, axis=1, keepdims=True)
    norm = top + jnp.log(jnp.sum(jnp.exp(logits - top), axis=1, keepdims=True))
    words = lax.broadcasted_iota(jnp.int32, (share, vocab), 1)
    like = jnp.sum(jnp.where(words == nat_ref[...], logits, 0.0), axis=1, keepdims=True) - norm
    r = lax.broadcasted_iota(jnp.int32, (share, width), 0)
    c = lax.broadcasted_iota(jnp.int32, (share, width), 1)
    out_ref[0:1, :] = jnp.sum(jnp.where(c == r + piece * share, like, 0.0), axis=0, keepdims=True)
    r = lax.broadcasted_iota(jnp.int32, (muts, total), 0)
    c = lax.broadcasted_iota(jnp.int32, (muts, total), 1)
    at_mut = jnp.sum(jnp.where(c == row_ref[...], scale_row, 0.0), axis=1, keepdims=True)
    out_ref[1:2, 0:muts] = score_ref[...] * as_row(at_mut, muts)


def final_part(feats, where, logits, squares, scores, nat, mut_row, width):
    whole = pl.BlockSpec(memory_space=pltpu.VMEM)
    return pl.pallas_call(
        functools.partial(final_kernel, float(feats)),
        in_specs=[pl.BlockSpec(memory_space=pltpu.SMEM)] + [whole] * 5,
        out_specs=whole,
        out_shape=jax.ShapeDtypeStruct((2, width), F32),
        name="final_part",
    )(where, logits, squares, scores, nat, mut_row)


def spread_unembed(unembed, norm_gain, rows_wanted):
    count, shards = lax.axis_size("ctx"), lax.axis_size("mp")
    scaled = (unembed.astype(F32) * norm_gain[:, None]).astype(BF16)
    held = unembed.shape[0]
    z, m = lax.axis_index("ctx"), lax.axis_index("mp")
    if held % rows_wanted != 0:
        every = lax.all_gather(scaled, "mp", axis=0, tiled=True)
        return lax.dynamic_slice_in_dim(every, z * rows_wanted, rows_wanted, 0)
    ratio = held // rows_wanted
    owner = [i // ratio for i in range(count)]
    piece = lax.dynamic_slice_in_dim(scaled, (z % ratio) * rows_wanted, rows_wanted, 0)
    value = jnp.where(m == z // ratio, piece, jnp.zeros_like(piece))
    bit, holders = shards // 2, [0]
    while bit:
        pairs = [
            (i * shards + (owner[i] ^ h), i * shards + (owner[i] ^ h ^ bit)) for i in range(count) for h in holders
        ]
        value = value + lax.ppermute(value, ("ctx", "mp"), pairs)
        holders = holders + [h ^ bit for h in holders]
        bit //= 2
    return value


def split_half(value, upper):
    half = value.shape[0] // 2
    keep = lax.dynamic_slice_in_dim(value, upper * half, half, 0)
    send = lax.dynamic_slice_in_dim(value, (1 - upper) * half, half, 0)
    return keep, send


def project(gated, weight):
    shards = lax.axis_size("mp")
    m = lax.axis_index("mp")
    bit = 1
    value = None
    while bit < shards:
        upper = (m // bit) % 2
        keep, send = split_half(gated if value is None else value, upper)
        if value is None:
            sent = jnp.dot(send, weight, preferred_element_type=F32).astype(BF16)
            keep = jnp.dot(keep, weight, preferred_element_type=F32)
        else:
            sent = send.astype(BF16)
        value = keep + swap(sent, "mp", bit).astype(F32)
        bit *= 2
    return jnp.dot(gated, weight, preferred_element_type=F32) if value is None else value


def row_piece():
    shards = lax.axis_size("mp")
    m = lax.axis_index("mp")
    piece, bit = 0, 1
    while bit < shards:
        piece = piece * 2 + (m // bit) % 2
        bit *= 2
    return piece


def body(streams, short_filter, mode_params, out_weight, norm_gain, unembed, native, mut_pos, mut_ids):
    rows, width = streams.shape[1:]
    count, shards = lax.axis_size("ctx"), lax.axis_size("mp")
    z = lax.axis_index("ctx")
    quick = count == 4
    modes_t = jnp.swapaxes(mode_params, 1, 2)
    me = z.astype(jnp.int32)[None]
    high = native // 256
    nat_row = jnp.concatenate([high, native - high * 256]).astype(F32)
    nat_row = jnp.pad(nat_row, (0, width - 2 * rows))[None, :]
    y, gate, start, msg = local_part(streams, short_filter, modes_t, nat_row)
    nat_at = 2 * mode_params.shape[2] + 12
    if quick:
        msgs = [msg] + [swap(msg, "ctx", k) for k in range(1, count)]
        gated = carry_part(me, short_filter, modes_t, y, gate, start, msgs, False)
        nat_rows = jnp.stack([msgs[k][nat_at, : 2 * rows] for k in range(count)])
        nat_rows = nat_rows[z ^ jnp.arange(count)]
    else:
        every = lax.all_gather(msg, "ctx")
        gated = carry_part(me, short_filter, modes_t, y, gate, start, [every], True)
        nat_rows = every[:, nat_at, : 2 * rows]
    nat_rows = nat_rows.astype(jnp.int32)
    nat_all = (nat_rows[:, :rows] * 256 + nat_rows[:, rows:]).reshape(-1)

    un = spread_unembed(unembed, norm_gain, out_weight.shape[1])
    piece = row_piece()
    share = rows // shards
    block, inner = mut_pos // rows, mut_pos % rows
    mut_row = jnp.where(inner // share == piece, block * share + inner % share, -1)[:, None]
    mut_nat = nat_all[mut_pos][:, None]

    if quick:
        middle = [(1, 2), (2, 1)]
        beside = swap(gated, "ctx", 1)
        mid_a = lax.ppermute(gated, "ctx", middle)
        mid_b = lax.ppermute(beside, "ctx", middle)
        far_a = swap(mid_a, "ctx", 1)
        far_b = swap(mid_b, "ctx", 1)
        blocks = [gated, beside, mid_a + far_a, mid_b + far_b]
        low = z < 2
        where = jnp.stack([z, z ^ 1, jnp.where(low, 2, 1), jnp.where(low, 3, 0)]).astype(jnp.int32)
    else:
        every = lax.all_gather(gated, "ctx")
        blocks = [every[b] for b in range(count)]
        where = jnp.arange(count, dtype=jnp.int32)
    slots = [project(part, out_weight) for part in blocks]
    part, squares, scores = logit_part(where, slots, un, mut_row, mut_ids[:, None], mut_nat)

    if quick:
        vocab = part.shape[1]
        own = lax.dynamic_slice_in_dim(part, z * share, share, 0)

        def wide(value):
            first = value.astype(BF16)
            second = (value - first.astype(F32)).astype(BF16)
            both = jnp.concatenate([first, second], axis=0)
            return jnp.pad(both, ((0, 0), (0, vocab - both.shape[1])))

        extra = jnp.concatenate([wide(squares), wide(scores)], axis=0)
        logits = own
        for k in range(1, count):
            theirs = lax.dynamic_slice_in_dim(part, (z ^ k) * share, share, 0).astype(BF16)
            got = swap(jnp.concatenate([theirs, extra], axis=0), "ctx", k).astype(F32)
            logits = logits + got[:share]
            squares = squares + (got[share : share + 1] + got[share + 1 : share + 2])[:, : squares.shape[1]]
            scores = scores + (got[share + 2 : share + 3] + got[share + 3 : share + 4])[:, : scores.shape[1]]
    else:
        logits = lax.psum_scatter(part, "ctx", scatter_dimension=0, tiled=True)
        squares = lax.psum(squares, "ctx")
        scores = lax.psum(scores, "ctx")

    own_nat = lax.dynamic_slice_in_dim(native, piece * share, share, 0)[:, None]
    spot = jnp.stack([z, piece]).astype(jnp.int32)
    feats = norm_gain.shape[0] * shards
    span = max(rows, mut_pos.shape[0])
    result = final_part(feats, spot, logits, squares, scores, own_nat, mut_row, span)
    total = result
    for k in range(1, shards):
        total = total + swap(result, "mp", k)
    return total[0, :rows], total[1, : mut_pos.shape[0]]


def solution(mesh):
    in_specs = (
        P(None, ("groups", "ctx"), "mp"),
        P(None, None, "mp"),
        P(None, "mp", None),
        P("mp", "ctx"),
        P("mp"),
        P("mp", None),
        P(("groups", "ctx")),
        P("groups"),
        P("groups"),
    )
    out_specs = (P(("groups", "ctx")), P("groups"))
    return jax.shard_map(body, mesh=mesh, in_specs=in_specs, out_specs=out_specs, check_vma=False)
```

```python
import functools

import jax
import jax.numpy as jnp
from jax import lax
from jax.experimental import pallas as pl
from jax.experimental.pallas import tpu as pltpu
from jax.sharding import PartitionSpec as P


F32 = jnp.float32
BF16 = jnp.bfloat16
LANES = 128
SUBS = 8
EPS = 1e-05


def swap(value, axis, bit):
    count = lax.axis_size(axis)
    return lax.ppermute(value, axis, [(i, i ^ bit) for i in range(count)])


def mix(taps, now, back1, back2):
    return taps[0] * now + taps[1] * back1 + taps[2] * back2


def rounded(value):
    return value.astype(BF16).astype(F32)


def taps_of(filt_ref, stream, cols):
    return [filt_ref[stream, j : j + 1, cols] for j in range(3)]


def local_kernel(steps, modes, spread, x_ref, filt_ref, mode_ref, nat_ref, y_ref, gate_ref, start_ref, msg_ref, xs, gs):
    rows = steps * SUBS
    turn = pl.program_id(0)
    ids = nat_ref[...]
    ids = jnp.where(turn < spread, ids // 256, jnp.where(turn < 2 * spread, ids % 256, 0)).astype(F32)
    for tile in range(x_ref.shape[2] // LANES):
        cols = slice(tile * LANES, (tile + 1) * LANES)
        sub = lax.broadcasted_iota(jnp.int32, (SUBS, LANES), 0)
        for i in range(3):
            xs[i] = x_ref[i, :, cols].astype(F32)
        decay = [jnp.broadcast_to(mode_ref[0, m : m + 1, cols], (SUBS, LANES)) for m in range(modes)]
        res = [jnp.broadcast_to(mode_ref[1, m : m + 1, cols], (SUBS, LANES)) for m in range(modes)]
        fall = [jnp.exp(-d) for d in decay]
        taps = [taps_of(filt_ref, i, cols) for i in range(3)]

        def at(i, t):
            return xs[i, pl.ds(t, SUBS, stride=steps), :]

        def behind(value):
            return jnp.where(sub == 0, 0.0, pltpu.roll(value, 1, 0))

        back2 = [behind(at(i, steps - 2)) for i in range(3)]
        back1 = [behind(at(i, steps - 1)) for i in range(3)]
        state = [jnp.zeros((SUBS, LANES), F32) for _ in range(modes)]
        for t in range(steps):
            now = [at(i, t) for i in range(3)]
            mixed = [mix(taps[i], now[i], back1[i], back2[i]) for i in range(3)]
            back2, back1 = back1, now
            gs[pl.ds(t, SUBS, stride=steps), :] = mixed[0]
            prod = rounded(mixed[1] * mixed[2])
            if t < 2:
                prod = jnp.where(sub == 0, 0.0, prod)
            state = [f * s + prod for f, s in zip(fall, state)]
            y_ref[t * SUBS : (t + 1) * SUBS, cols] = functools.reduce(
                lambda p, q: p + q, [r * s for r, s in zip(res, state)]
            )
        gate_ref[:, cols] = gs[...].astype(BF16)
        ends = []
        for m in range(modes):
            total = state[m]
            for reach in (1, 2, 4):
                power = jnp.exp(-decay[m] * float(steps * reach))
                total = total + jnp.where(sub < reach, 0.0, power * pltpu.roll(total, reach, 0))
            start_ref[m * SUBS : (m + 1) * SUBS, cols] = behind(total)
            ends.append(total[SUBS - 1 : SUBS, :])
        end = jnp.concatenate(ends, axis=0)
        high = rounded(end)
        first = [xs[i, 0:2, :] for i in range(3)]
        last = [xs[i, rows - 2 : rows, :] for i in range(3)]
        edge = jnp.concatenate([first[1], first[2], last[1], last[2]], axis=0)
        other = jnp.concatenate(
            [last[0], first[0], ids[:, cols], jnp.zeros((3, LANES), F32)], axis=0
        )
        msg_ref[:, cols] = jnp.concatenate([high, end - high, edge, other], axis=0).astype(BF16)


def local_part(streams, filt, modes_t, native):
    rows, width = streams.shape[1:]
    modes = modes_t.shape[1]
    steps = rows // SUBS
    block = 2 * LANES
    msg_rows = 2 * modes + 16
    return pl.pallas_call(
        functools.partial(local_kernel, steps, modes, rows // block),
        grid=(width // block,),
        in_specs=[
            pl.BlockSpec((3, rows, block), lambda c: (0, 0, c)),
            pl.BlockSpec((3, 3, block), lambda c: (0, 0, c)),
            pl.BlockSpec((2, modes, block), lambda c: (0, 0, c)),
            pl.BlockSpec((1, block), lambda c: (0, c % (rows // block))),
        ],
        out_specs=[
            pl.BlockSpec((rows, block), lambda c: (0, c)),
            pl.BlockSpec((rows, block), lambda c: (0, c)),
            pl.BlockSpec((modes * SUBS, block), lambda c: (0, c)),
            pl.BlockSpec((msg_rows, block), lambda c: (0, c)),
        ],
        out_shape=[
            jax.ShapeDtypeStruct((rows, width), F32),
            jax.ShapeDtypeStruct((rows, width), BF16),
            jax.ShapeDtypeStruct((modes * SUBS, width), F32),
            jax.ShapeDtypeStruct((msg_rows, width), BF16),
        ],
        scratch_shapes=[pltpu.VMEM((3, rows, LANES), F32), pltpu.VMEM((rows, LANES), F32)],
        cost_estimate=pl.CostEstimate(flops=rows * width * 64, bytes_accessed=rows * width * 12, transcendentals=0),
        name="local_part",
    )(streams, filt, modes_t, native[None, :])


def carry_kernel(steps, modes, stacked, count, where_ref, filt_ref, mode_ref, y_ref, gate_ref, start_ref, *rest):
    msg_refs, (out_ref, held, conv) = rest[:-3], rest[-3:]
    me = where_ref[0]
    rows = steps * SUBS
    base = 2 * modes
    for tile in range(y_ref.shape[1] // LANES):
        cols = slice(tile * LANES, (tile + 1) * LANES)
        sub = lax.broadcasted_iota(jnp.int32, (SUBS, LANES), 0)
        for k in range(count):
            if stacked:
                held[k] = msg_refs[0][k, :, cols].astype(F32)
            else:
                held[me ^ k] = msg_refs[k][:, cols].astype(F32)
        decay = mode_ref[0, :, cols]
        taps = [taps_of(filt_ref, i, cols) for i in range(3)]

        def firsts(own, prior, keep):
            pair = []
            for i, lane in ((1, 0), (2, 2)):
                f0 = own[base + lane : base + lane + 1, :]
                f1 = own[base + lane + 1 : base + lane + 2, :]
                l2 = jnp.where(keep, prior[base + lane + 4 : base + lane + 5, :], 0.0)
                l1 = jnp.where(keep, prior[base + lane + 5 : base + lane + 6, :], 0.0)
                pair.append((mix(taps[i], f0, l1, l2), mix(taps[i], f1, f0, l1)))
            return rounded(pair[0][0] * pair[1][0]), rounded(pair[0][1] * pair[1][1])

        full = jnp.exp(-decay * float(rows))
        near0 = jnp.exp(-decay * float(rows - 1))
        near1 = jnp.exp(-decay * float(rows - 2))

        def advance(b, entering):
            own = held[b]
            p0, p1 = firsts(own, held[jnp.maximum(b - 1, 0)], b > 0)
            end = own[0:modes, :] + own[modes : 2 * modes, :] + near0 * p0 + near1 * p1
            return jnp.where(b < me, full * entering + end, entering)

        entering = jnp.zeros((modes, LANES), F32)
        if count <= 8:
            for b in range(count - 1):
                entering = advance(b, entering)
        else:
            entering = lax.fori_loop(0, count - 1, advance, entering)
        own = held[me]
        prior = held[jnp.maximum(me - 1, 0)]
        p0, p1 = firsts(own, prior, me > 0)
        later = (
            jnp.exp(-decay * float(steps)) * entering
            + jnp.exp(-decay * float(steps - 1)) * p0
            + jnp.exp(-decay * float(steps - 2)) * p1
        )
        shift = float(steps) * jnp.maximum(sub - 1, 0).astype(F32)
        fall, res, flow = [], [], []
        for m in range(modes):
            d = jnp.broadcast_to(decay[m : m + 1, :], (SUBS, LANES))
            r = jnp.broadcast_to(mode_ref[1, m : m + 1, cols], (SUBS, LANES))
            fall.append(jnp.exp(-d))
            res.append(r)
            begin = jnp.where(sub == 0, entering[m : m + 1, :], jnp.exp(-d * shift) * later[m : m + 1, :])
            flow.append(r * (start_ref[m * SUBS : (m + 1) * SUBS, cols] + begin))
        inject = (p0, p1)
        for t in range(steps):
            flow = [f * v for f, v in zip(fall, flow)]
            if t < 2:
                extra = jnp.where(sub == 0, inject[t], 0.0)
                flow = [v + r * extra for v, r in zip(flow, res)]
            conv[pl.ds(t, SUBS, stride=steps), :] = functools.reduce(
                lambda p, q: p + q, flow, y_ref[t * SUBS : (t + 1) * SUBS, cols]
            )
        g0 = own[base + 10 : base + 11, :]
        g1 = own[base + 11 : base + 12, :]
        l2 = jnp.where(me > 0, prior[base + 8 : base + 9, :], 0.0)
        l1 = jnp.where(me > 0, prior[base + 9 : base + 10, :], 0.0)
        head0 = mix(taps[0], g0, l1, l2)
        head1 = mix(taps[0], g1, g0, l1)
        gate = gate_ref[:, cols].astype(F32)
        line = lax.broadcasted_iota(jnp.int32, (16, LANES), 0)
        head = jnp.where(line == 0, rounded(head0), jnp.where(line == 1, rounded(head1), gate[0:16, :]))
        out_ref[0:16, cols] = (head * rounded(conv[0:16, :])).astype(BF16)
        out_ref[16:rows, cols] = (gate[16:rows, :] * rounded(conv[16:rows, :])).astype(BF16)


def carry_part(me, filt, modes_t, y, gate, start, msgs, stacked):
    rows, width = y.shape
    modes = modes_t.shape[1]
    steps = rows // SUBS
    block = 2 * LANES
    count = msgs[0].shape[0] if stacked else len(msgs)
    msg_rows = msgs[0].shape[-2]
    if stacked:
        msg_specs = [pl.BlockSpec((count, msg_rows, block), lambda c, w: (0, 0, c))]
    else:
        msg_specs = [pl.BlockSpec((msg_rows, block), lambda c, w: (0, c))] * count
    return pl.pallas_call(
        functools.partial(carry_kernel, steps, modes, stacked, count),
        grid_spec=pltpu.PrefetchScalarGridSpec(
            num_scalar_prefetch=1,
            grid=(width // block,),
            in_specs=[
                pl.BlockSpec((3, 3, block), lambda c, w: (0, 0, c)),
                pl.BlockSpec((2, modes, block), lambda c, w: (0, 0, c)),
                pl.BlockSpec((rows, block), lambda c, w: (0, c)),
                pl.BlockSpec((rows, block), lambda c, w: (0, c)),
                pl.BlockSpec((modes * SUBS, block), lambda c, w: (0, c)),
            ]
            + msg_specs,
            out_specs=pl.BlockSpec((rows, block), lambda c, w: (0, c)),
            scratch_shapes=[pltpu.VMEM((count, msg_rows, LANES), F32), pltpu.VMEM((rows, LANES), F32)],
        ),
        out_shape=jax.ShapeDtypeStruct((rows, width), BF16),
        cost_estimate=pl.CostEstimate(flops=rows * width * 32, bytes_accessed=rows * width * 8, transcendentals=0),
        name="carry_part",
    )(me, filt, modes_t, y, gate, start, *msgs)


def as_row(col, width):
    rows = col.shape[0]
    r = lax.broadcasted_iota(jnp.int32, (rows, width), 0)
    c = lax.broadcasted_iota(jnp.int32, (rows, width), 1)
    return jnp.sum(jnp.where(r == c, col, 0.0), axis=0, keepdims=True)


def exact_dot(onehot, values):
    high = values.astype(BF16)
    low = (values - high.astype(F32)).astype(BF16)
    return jnp.dot(onehot, high, preferred_element_type=F32) + jnp.dot(onehot, low, preferred_element_type=F32)


def two_rows(row, width):
    high = rounded(row)
    both = jnp.concatenate([high, row - high], axis=0)
    return jnp.concatenate([both, jnp.zeros((2, width - row.shape[1]), F32)], axis=1)


def logit_kernel(share, peers, where_ref, un_ref, row_ref, id_ref, nat_ref, *rest):
    slots = where_ref.shape[0] - 1
    slot_refs, rest = rest[:slots], rest[slots:]
    part_ref, square_ref, score_ref = rest[:3]
    msg_refs, acc = rest[3 : 3 + peers], rest[-1]
    for k in range(slots):
        acc[pl.ds(pl.multiple_of(where_ref[k] * share, share), share), :] = slot_refs[k][...]
    values = acc[...]
    total = values.shape[0]
    square = as_row(jnp.sum(values * values, axis=1, keepdims=True), total)
    square_ref[...] = square
    part = jnp.dot(values.astype(BF16), un_ref[...], preferred_element_type=F32)
    part_ref[...] = part
    muts = row_ref.shape[0]
    vocab = part.shape[1]
    spots = lax.broadcasted_iota(jnp.int32, (muts, total), 1)
    picked = exact_dot((spots == row_ref[...]).astype(BF16), part)
    words = lax.broadcasted_iota(jnp.int32, (muts, vocab), 1)
    gain = jnp.where(words == id_ref[...], picked, 0.0) - jnp.where(words == nat_ref[...], picked, 0.0)
    score = as_row(jnp.sum(gain, axis=1, keepdims=True), muts)
    score_ref[...] = score
    if peers:
        me = where_ref[slots]
        extra = jnp.concatenate(
            [two_rows(square, vocab), two_rows(score, vocab), jnp.zeros((4, vocab), F32)], axis=0
        ).astype(BF16)
        for k in range(1, peers + 1):
            their = part_ref[pl.ds(pl.multiple_of((me ^ k) * share, share), share), :]
            msg_refs[k - 1][0:share, :] = their.astype(BF16)
            msg_refs[k - 1][share : share + 8, :] = extra


def logit_part(where, slots, un, mut_row, mut_id, mut_nat, peers):
    share, wide = slots[0].shape
    total = share * len(slots)
    vocab = un.shape[1]
    muts = mut_row.shape[0]
    whole = pl.BlockSpec(memory_space=pltpu.VMEM)
    return pl.pallas_call(
        functools.partial(logit_kernel, share, peers),
        in_specs=[pl.BlockSpec(memory_space=pltpu.SMEM)] + [whole] * (4 + len(slots)),
        out_specs=[whole] * (3 + peers),
        out_shape=[
            jax.ShapeDtypeStruct((total, vocab), F32),
            jax.ShapeDtypeStruct((1, total), F32),
            jax.ShapeDtypeStruct((1, muts), F32),
        ]
        + [jax.ShapeDtypeStruct((share + 8, vocab), BF16)] * peers,
        scratch_shapes=[pltpu.VMEM((total, wide), F32)],
        name="logit_part",
    )(where, un, mut_row, mut_id, mut_nat, *slots)


def final_kernel(feats, where_ref, log_ref, square_ref, score_ref, nat_ref, row_ref, *rest):
    msg_refs, out_ref = rest[:-1], rest[-1]
    me, piece = where_ref[0], where_ref[1]
    share = nat_ref.shape[0]
    vocab = log_ref.shape[1]
    total = square_ref.shape[1]
    muts = score_ref.shape[1]
    width = out_ref.shape[1]
    if msg_refs:
        logits = log_ref[pl.ds(pl.multiple_of(me * share, share), share), :]
    else:
        logits = log_ref[...]
    square, score = square_ref[...], score_ref[...]
    for msg_ref in msg_refs:
        logits = logits + msg_ref[0:share, :].astype(F32)
        extra = msg_ref[share : share + 8, :].astype(F32)
        square = square + (extra[0:1, 0:total] + extra[1:2, 0:total])
        score = score + (extra[2:3, 0:muts] + extra[3:4, 0:muts])
    scale_row = lax.rsqrt(square / feats + EPS)
    r = lax.broadcasted_iota(jnp.int32, (share, total), 0)
    c = lax.broadcasted_iota(jnp.int32, (share, total), 1)
    scale = jnp.sum(jnp.where(c == r + me * share, scale_row, 0.0), axis=1, keepdims=True)
    logits = logits * scale
    top = jnp.max(logits, axis=1, keepdims=True)
    norm = top + jnp.log(jnp.sum(jnp.exp(logits - top), axis=1, keepdims=True))
    words = lax.broadcasted_iota(jnp.int32, (share, vocab), 1)
    like = jnp.sum(jnp.where(words == nat_ref[...], logits, 0.0), axis=1, keepdims=True) - norm
    r = lax.broadcasted_iota(jnp.int32, (share, width), 0)
    c = lax.broadcasted_iota(jnp.int32, (share, width), 1)
    out_ref[0:1, :] = jnp.sum(jnp.where(c == r + piece * share, like, 0.0), axis=0, keepdims=True)
    r = lax.broadcasted_iota(jnp.int32, (muts, total), 0)
    c = lax.broadcasted_iota(jnp.int32, (muts, total), 1)
    at_mut = jnp.sum(jnp.where(c == row_ref[...], scale_row, 0.0), axis=1, keepdims=True)
    out_ref[1:2, 0:muts] = score * as_row(at_mut, muts)


def final_part(feats, where, logits, squares, scores, nat, mut_row, msgs, width):
    whole = pl.BlockSpec(memory_space=pltpu.VMEM)
    return pl.pallas_call(
        functools.partial(final_kernel, float(feats)),
        in_specs=[pl.BlockSpec(memory_space=pltpu.SMEM)] + [whole] * (5 + len(msgs)),
        out_specs=whole,
        out_shape=jax.ShapeDtypeStruct((2, width), F32),
        name="final_part",
    )(where, logits, squares, scores, nat, mut_row, *msgs)


def total_kernel(*refs):
    like_ref, score_ref = refs[-2:]
    total = functools.reduce(lambda p, q: p + q, [ref[...] for ref in refs[:-2]])
    like_ref[...] = total[0:1, 0 : like_ref.shape[1]]
    score_ref[...] = total[1:2, 0 : score_ref.shape[1]]


def total_part(pieces, rows, muts):
    whole = pl.BlockSpec(memory_space=pltpu.VMEM)
    return pl.pallas_call(
        total_kernel,
        in_specs=[whole] * len(pieces),
        out_specs=[whole] * 2,
        out_shape=[jax.ShapeDtypeStruct((1, rows), F32), jax.ShapeDtypeStruct((1, muts), F32)],
        name="total_part",
    )(*pieces)


def spread_unembed(unembed, norm_gain, rows_wanted):
    count, shards = lax.axis_size("ctx"), lax.axis_size("mp")
    scaled = (unembed.astype(F32) * norm_gain[:, None]).astype(BF16)
    held = unembed.shape[0]
    z, m = lax.axis_index("ctx"), lax.axis_index("mp")
    if held % rows_wanted != 0:
        every = lax.all_gather(scaled, "mp", axis=0, tiled=True)
        return lax.dynamic_slice_in_dim(every, z * rows_wanted, rows_wanted, 0)
    ratio = held // rows_wanted
    owner = [i // ratio for i in range(count)]
    piece = lax.dynamic_slice_in_dim(scaled, (z % ratio) * rows_wanted, rows_wanted, 0)
    value = jnp.where(m == z // ratio, piece, jnp.zeros_like(piece))
    bit, holders = shards // 2, [0]
    while bit:
        pairs = [
            (i * shards + (owner[i] ^ h), i * shards + (owner[i] ^ h ^ bit)) for i in range(count) for h in holders
        ]
        moved = lax.ppermute(value, ("ctx", "mp"), pairs)
        value = value + moved
        holders = holders + [h ^ bit for h in holders]
        bit //= 2
    return value


def split_half(value, upper):
    half = value.shape[0] // 2
    keep = lax.dynamic_slice_in_dim(value, upper * half, half, 0)
    send = lax.dynamic_slice_in_dim(value, (1 - upper) * half, half, 0)
    return keep, send


def project(gated, weight):
    shards = lax.axis_size("mp")
    m = lax.axis_index("mp")
    bit = 1
    value = None
    while bit < shards:
        upper = (m // bit) % 2
        keep, send = split_half(gated if value is None else value, upper)
        if value is None:
            sent = jnp.dot(send, weight, preferred_element_type=F32).astype(BF16)
            keep = jnp.dot(keep, weight, preferred_element_type=F32)
        else:
            sent = send.astype(BF16)
        value = keep + swap(sent, "mp", bit).astype(F32)
        bit *= 2
    return jnp.dot(gated, weight, preferred_element_type=F32) if value is None else value


def row_piece():
    shards = lax.axis_size("mp")
    m = lax.axis_index("mp")
    piece, bit = 0, 1
    while bit < shards:
        piece = piece * 2 + (m // bit) % 2
        bit *= 2
    return piece


def body(streams, short_filter, mode_params, out_weight, norm_gain, unembed, native, mut_pos, mut_ids):
    rows, _ = streams.shape[1:]
    count, shards = lax.axis_size("ctx"), lax.axis_size("mp")
    z = lax.axis_index("ctx")
    quick = count == 4
    modes_t = jnp.swapaxes(mode_params, 1, 2)
    me = z.astype(jnp.int32)[None]
    y, gate, start, msg = local_part(streams, short_filter, modes_t, native)
    nat_at = 2 * mode_params.shape[2] + 12
    if quick:
        msgs = [msg] + [swap(msg, "ctx", k) for k in range(1, count)]
        gated = carry_part(me, short_filter, modes_t, y, gate, start, msgs, False)
        nat_rows = jnp.stack([msgs[k][nat_at, : 2 * rows] for k in range(count)])
        nat_rows = nat_rows[z ^ jnp.arange(count)]
    else:
        every = lax.all_gather(msg, "ctx")
        gated = carry_part(me, short_filter, modes_t, y, gate, start, [every], True)
        nat_rows = every[:, nat_at, : 2 * rows]
    nat_rows = nat_rows.astype(jnp.int32)
    nat_all = (nat_rows[:, :rows] * 256 + nat_rows[:, rows:]).reshape(-1)

    held, unembed, norm_gain = lax.optimization_barrier((gated, unembed, norm_gain)) if quick else (gated, unembed, norm_gain)
    gated = held
    un = spread_unembed(unembed, norm_gain, out_weight.shape[1])
    piece = row_piece()
    share = rows // shards
    block, inner = mut_pos // rows, mut_pos % rows
    mut_row = jnp.where(inner // share == piece, block * share + inner % share, -1)[:, None]
    mut_nat = nat_all[mut_pos][:, None]

    if quick:
        middle = [(1, 2), (2, 1)]
        beside = swap(gated, "ctx", 1)
        mid_a = lax.ppermute(gated, "ctx", middle)
        mid_b = lax.ppermute(beside, "ctx", middle)
        far_a = swap(mid_a, "ctx", 1)
        far_b = swap(mid_b, "ctx", 1)
        third = mid_a + far_a
        fourth = mid_b + far_b
        blocks = [gated, beside, third, fourth]
        low = z < 2
        where = [z, z ^ 1, jnp.where(low, 2, 1), jnp.where(low, 3, 0)]
    else:
        every = lax.all_gather(gated, "ctx")
        blocks = [every[b] for b in range(count)]
        where = list(range(count))
    where = jnp.stack([jnp.asarray(w, jnp.int32) for w in where + [z]])
    slots = []
    for part in blocks:
        slots.append(project(part, out_weight))
    peers = count - 1 if quick else 0
    part, squares, scores, *msgs = logit_part(where, slots, un, mut_row, mut_ids[:, None], mut_nat, peers)
    if quick:
        msgs = [swap(msgs[k - 1], "ctx", k) for k in range(1, count)]
    else:
        part = lax.psum_scatter(part, "ctx", scatter_dimension=0, tiled=True)
        squares = lax.psum(squares, "ctx")
        scores = lax.psum(scores, "ctx")

    own_nat = lax.dynamic_slice_in_dim(native, piece * share, share, 0)[:, None]
    spot = jnp.stack([z, piece]).astype(jnp.int32)
    feats = norm_gain.shape[0] * shards
    span = max(rows, mut_pos.shape[0])
    result = final_part(feats, spot, part, squares, scores, own_nat, mut_row, msgs, span)
    pieces = [result] + [swap(result, "mp", k) for k in range(1, shards)]
    like, score = total_part(pieces, rows, mut_pos.shape[0])
    return like[0], score[0]


def solution(mesh):
    in_specs = (
        P(None, ("groups", "ctx"), "mp"),
        P(None, None, "mp"),
        P(None, "mp", None),
        P("mp", "ctx"),
        P("mp"),
        P("mp", None),
        P(("groups", "ctx")),
        P("groups"),
        P("groups"),
    )
    out_specs = (P(("groups", "ctx")), P("groups"))
    return jax.shard_map(body, mesh=mesh, in_specs=in_specs, out_specs=out_specs, check_vma=False)
```

```python
import functools

import jax
import jax.numpy as jnp
from jax import lax
from jax.experimental import pallas as pl
from jax.experimental.pallas import tpu as pltpu
from jax.sharding import PartitionSpec as P


F32 = jnp.float32
BF16 = jnp.bfloat16
LANES = 128
SUBS = 8
EPS = 1e-05


def swap(value, axis, bit):
    count = lax.axis_size(axis)
    return lax.ppermute(value, axis, [(i, i ^ bit) for i in range(count)])


def mix(taps, now, back1, back2):
    return taps[0] * now + taps[1] * back1 + taps[2] * back2


def rounded(value):
    return value.astype(BF16).astype(F32)


def taps_of(filt_ref, stream, cols):
    return [filt_ref[stream, j : j + 1, cols] for j in range(3)]


def lane_slice(tile):
    return pl.ds(pl.multiple_of(tile * LANES, LANES), LANES)


def local_kernel(
    steps, modes, x_any, filt_any, mode_any, nat_any, y_ref, gate_ref, start_ref, msg_ref,
    filt_ref, mode_ref, held, nat_ref, xs, gs, sems, side_sems
):
    rows = steps * SUBS
    tiles = held.shape[0]
    spread = rows // LANES

    def fetch(tile):
        return pltpu.make_async_copy(x_any.at[:, :, lane_slice(tile)], held.at[tile], sems.at[tile])

    sides = [
        pltpu.make_async_copy(src, dst, side_sems.at[k])
        for k, (src, dst) in enumerate(((filt_any, filt_ref), (mode_any, mode_ref), (nat_any, nat_ref)))
    ]
    fetch(0).start()
    for side in sides:
        side.start()

    @pl.loop(1, tiles)
    def _(tile):
        fetch(tile).start()

    for side in sides:
        side.wait()

    @pl.loop(0, tiles)
    def _(tile):
        cols = lane_slice(tile)
        sub = lax.broadcasted_iota(jnp.int32, (SUBS, LANES), 0)
        decay = [jnp.broadcast_to(mode_ref[0, m : m + 1, cols], (SUBS, LANES)) for m in range(modes)]
        res = [jnp.broadcast_to(mode_ref[1, m : m + 1, cols], (SUBS, LANES)) for m in range(modes)]
        fall = [jnp.exp(-d) for d in decay]
        taps = [taps_of(filt_ref, i, cols) for i in range(3)]
        ids = nat_ref[0:1, lane_slice(tile % spread)]
        ids = jnp.where(tile < spread, ids // 256, jnp.where(tile < 2 * spread, ids % 256, 0)).astype(F32)
        fetch(tile).wait()
        for i in range(3):
            xs[i] = held[tile, i].astype(F32)

        def at(i, t):
            return xs[i, pl.ds(t, SUBS, stride=steps), :]

        def behind(value):
            return jnp.where(sub == 0, 0.0, pltpu.roll(value, 1, 0))

        back2 = [behind(at(i, steps - 2)) for i in range(3)]
        back1 = [behind(at(i, steps - 1)) for i in range(3)]
        state = [jnp.zeros((SUBS, LANES), F32) for _ in range(modes)]
        for t in range(steps):
            now = [at(i, t) for i in range(3)]
            mixed = [mix(taps[i], now[i], back1[i], back2[i]) for i in range(3)]
            back2, back1 = back1, now
            gs[pl.ds(t, SUBS, stride=steps), :] = mixed[0]
            prod = rounded(mixed[1] * mixed[2])
            if t < 2:
                prod = jnp.where(sub == 0, 0.0, prod)
            state = [f * s + prod for f, s in zip(fall, state)]
            y_ref[t * SUBS : (t + 1) * SUBS, cols] = functools.reduce(
                lambda p, q: p + q, [r * s for r, s in zip(res, state)]
            )
        gate_ref[:, cols] = gs[...].astype(BF16)
        ends = []
        for m in range(modes):
            total = state[m]
            for reach in (1, 2, 4):
                power = jnp.exp(-decay[m] * float(steps * reach))
                total = total + jnp.where(sub < reach, 0.0, power * pltpu.roll(total, reach, 0))
            start_ref[m * SUBS : (m + 1) * SUBS, cols] = behind(total)
            ends.append(total[SUBS - 1 : SUBS, :])
        end = jnp.concatenate(ends, axis=0)
        high = rounded(end)
        first = [xs[i, 0:2, :] for i in range(3)]
        last = [xs[i, rows - 2 : rows, :] for i in range(3)]
        edge = jnp.concatenate([first[1], first[2], last[1], last[2]], axis=0)
        other = jnp.concatenate([last[0], first[0], ids, jnp.zeros((3, LANES), F32)], axis=0)
        msg_ref[:, cols] = jnp.concatenate([high, end - high, edge, other], axis=0).astype(BF16)


SMALL = pltpu.CompilerParams(vmem_limit_bytes=16 * 2**20)


def in_vmem():
    return pl.BlockSpec(memory_space=pltpu.VMEM)


def local_part(streams, filt, modes_t, native):
    rows, width = streams.shape[1:]
    modes = modes_t.shape[1]
    steps = rows // SUBS
    tiles = width // LANES
    msg_rows = 2 * modes + 16
    return pl.pallas_call(
        functools.partial(local_kernel, steps, modes),
        in_specs=[pl.BlockSpec(memory_space=pltpu.HBM)] * 4,
        out_specs=[in_vmem()] * 6,
        out_shape=[
            pltpu.VMEM((rows, width), F32),
            pltpu.VMEM((rows, width), BF16),
            pltpu.VMEM((modes * SUBS, width), F32),
            pltpu.VMEM((msg_rows, width), BF16),
            pltpu.VMEM(filt.shape, F32),
            pltpu.VMEM(modes_t.shape, F32),
        ],
        scratch_shapes=[
            pltpu.VMEM((tiles, 3, rows, LANES), BF16),
            pltpu.VMEM((1, rows), jnp.int32),
            pltpu.VMEM((3, rows, LANES), F32),
            pltpu.VMEM((rows, LANES), F32),
            pltpu.SemaphoreType.DMA((tiles,)),
            pltpu.SemaphoreType.DMA((3,)),
        ],
        compiler_params=SMALL,
        cost_estimate=pl.CostEstimate(flops=rows * width * 64, bytes_accessed=rows * width * 12, transcendentals=0),
        name="local_part",
    )(*[pltpu.with_memory_space_constraint(v, pltpu.HBM) for v in (streams, filt, modes_t, native[None, :])])


def carry_kernel(steps, modes, stacked, count, where_ref, filt_ref, mode_ref, y_ref, gate_ref, start_ref, *rest):
    msg_refs, (out_ref, held, conv) = rest[:-3], rest[-3:]
    me = where_ref[0]
    rows = steps * SUBS
    base = 2 * modes

    @pl.loop(0, y_ref.shape[1] // LANES)
    def _(tile):
        cols = lane_slice(tile)
        sub = lax.broadcasted_iota(jnp.int32, (SUBS, LANES), 0)
        for k in range(count):
            if stacked:
                held[k] = msg_refs[0][k, :, cols].astype(F32)
            else:
                held[me ^ k] = msg_refs[k][:, cols].astype(F32)
        decay = mode_ref[0, :, cols]
        taps = [taps_of(filt_ref, i, cols) for i in range(3)]

        def firsts(own, prior, keep):
            pair = []
            for i, lane in ((1, 0), (2, 2)):
                f0 = own[base + lane : base + lane + 1, :]
                f1 = own[base + lane + 1 : base + lane + 2, :]
                l2 = jnp.where(keep, prior[base + lane + 4 : base + lane + 5, :], 0.0)
                l1 = jnp.where(keep, prior[base + lane + 5 : base + lane + 6, :], 0.0)
                pair.append((mix(taps[i], f0, l1, l2), mix(taps[i], f1, f0, l1)))
            return rounded(pair[0][0] * pair[1][0]), rounded(pair[0][1] * pair[1][1])

        full = jnp.exp(-decay * float(rows))
        near0 = jnp.exp(-decay * float(rows - 1))
        near1 = jnp.exp(-decay * float(rows - 2))

        def advance(b, entering):
            own = held[b]
            p0, p1 = firsts(own, held[jnp.maximum(b - 1, 0)], b > 0)
            end = own[0:modes, :] + own[modes : 2 * modes, :] + near0 * p0 + near1 * p1
            return jnp.where(b < me, full * entering + end, entering)

        entering = jnp.zeros((modes, LANES), F32)
        if count <= 8:
            for b in range(count - 1):
                entering = advance(b, entering)
        else:
            entering = lax.fori_loop(0, count - 1, advance, entering)
        own = held[me]
        prior = held[jnp.maximum(me - 1, 0)]
        p0, p1 = firsts(own, prior, me > 0)
        later = (
            jnp.exp(-decay * float(steps)) * entering
            + jnp.exp(-decay * float(steps - 1)) * p0
            + jnp.exp(-decay * float(steps - 2)) * p1
        )
        shift = float(steps) * jnp.maximum(sub - 1, 0).astype(F32)
        fall, res, flow = [], [], []
        for m in range(modes):
            d = jnp.broadcast_to(decay[m : m + 1, :], (SUBS, LANES))
            r = jnp.broadcast_to(mode_ref[1, m : m + 1, cols], (SUBS, LANES))
            fall.append(jnp.exp(-d))
            res.append(r)
            begin = jnp.where(sub == 0, entering[m : m + 1, :], jnp.exp(-d * shift) * later[m : m + 1, :])
            flow.append(r * (start_ref[m * SUBS : (m + 1) * SUBS, cols] + begin))
        inject = (p0, p1)
        for t in range(steps):
            flow = [f * v for f, v in zip(fall, flow)]
            if t < 2:
                extra = jnp.where(sub == 0, inject[t], 0.0)
                flow = [v + r * extra for v, r in zip(flow, res)]
            conv[pl.ds(t, SUBS, stride=steps), :] = functools.reduce(
                lambda p, q: p + q, flow, y_ref[t * SUBS : (t + 1) * SUBS, cols]
            )
        g0 = own[base + 10 : base + 11, :]
        g1 = own[base + 11 : base + 12, :]
        l2 = jnp.where(me > 0, prior[base + 8 : base + 9, :], 0.0)
        l1 = jnp.where(me > 0, prior[base + 9 : base + 10, :], 0.0)
        head0 = mix(taps[0], g0, l1, l2)
        head1 = mix(taps[0], g1, g0, l1)
        gate = gate_ref[:, cols].astype(F32)
        line = lax.broadcasted_iota(jnp.int32, (16, LANES), 0)
        head = jnp.where(line == 0, rounded(head0), jnp.where(line == 1, rounded(head1), gate[0:16, :]))
        out_ref[0:16, cols] = (head * rounded(conv[0:16, :])).astype(BF16)
        out_ref[16:rows, cols] = (gate[16:rows, :] * rounded(conv[16:rows, :])).astype(BF16)


def carry_part(me, filt, modes_t, y, gate, start, msgs, stacked):
    rows, width = y.shape
    modes = modes_t.shape[1]
    steps = rows // SUBS
    count = msgs[0].shape[0] if stacked else len(msgs)
    msg_rows = msgs[0].shape[-2]
    return pl.pallas_call(
        functools.partial(carry_kernel, steps, modes, stacked, count),
        in_specs=[pl.BlockSpec(memory_space=pltpu.SMEM)] + [in_vmem()] * (5 + len(msgs)),
        out_specs=in_vmem(),
        out_shape=jax.ShapeDtypeStruct((rows, width), BF16),
        scratch_shapes=[pltpu.VMEM((count, msg_rows, LANES), F32), pltpu.VMEM((rows, LANES), F32)],
        compiler_params=SMALL,
        cost_estimate=pl.CostEstimate(flops=rows * width * 32, bytes_accessed=rows * width * 8, transcendentals=0),
        name="carry_part",
    )(me, *[pltpu.with_memory_space_constraint(v, pltpu.VMEM) for v in (filt, modes_t, y, gate, start, *msgs)])


def bring_kernel(later_any, src_any, out_ref, sem):
    copy = pltpu.make_async_copy(src_any, out_ref, sem)
    copy.start()
    copy.wait()


def bring(later, weight):
    return pl.pallas_call(
        bring_kernel,
        in_specs=[pl.BlockSpec(memory_space=pl.ANY), pl.BlockSpec(memory_space=pltpu.HBM)],
        out_specs=in_vmem(),
        out_shape=pltpu.VMEM(weight.shape, weight.dtype),
        scratch_shapes=[pltpu.SemaphoreType.DMA],
        compiler_params=SMALL,
        name="bring",
    )(later, pltpu.with_memory_space_constraint(weight, pltpu.HBM))


def as_row(col, width):
    rows = col.shape[0]
    r = lax.broadcasted_iota(jnp.int32, (rows, width), 0)
    c = lax.broadcasted_iota(jnp.int32, (rows, width), 1)
    return jnp.sum(jnp.where(r == c, col, 0.0), axis=0, keepdims=True)


def exact_dot(onehot, values):
    high = values.astype(BF16)
    low = (values - high.astype(F32)).astype(BF16)
    return jnp.dot(onehot, high, preferred_element_type=F32) + jnp.dot(onehot, low, preferred_element_type=F32)


def two_rows(row, width):
    high = rounded(row)
    both = jnp.concatenate([high, row - high], axis=0)
    return jnp.concatenate([both, jnp.zeros((2, width - row.shape[1]), F32)], axis=1)


def logit_kernel(share, peers, where_ref, un_ref, gain_ref, row_ref, id_ref, nat_ref, *rest):
    slots = where_ref.shape[0] - 1
    slot_refs, rest = rest[:slots], rest[slots:]
    part_ref, square_ref, score_ref = rest[:3]
    msg_refs, acc = rest[3 : 3 + peers], rest[-1]
    for k in range(slots):
        acc[pl.ds(pl.multiple_of(where_ref[k] * share, share), share), :] = slot_refs[k][...]
    values = acc[...]
    total = values.shape[0]
    square = as_row(jnp.sum(values * values, axis=1, keepdims=True), total)
    square_ref[...] = square
    part = jnp.dot((values * gain_ref[...]).astype(BF16), un_ref[...], preferred_element_type=F32)
    part_ref[...] = part
    muts = row_ref.shape[0]
    vocab = part.shape[1]
    spots = lax.broadcasted_iota(jnp.int32, (muts, total), 1)
    picked = exact_dot((spots == row_ref[...]).astype(BF16), part)
    words = lax.broadcasted_iota(jnp.int32, (muts, vocab), 1)
    gain = jnp.where(words == id_ref[...], picked, 0.0) - jnp.where(words == nat_ref[...], picked, 0.0)
    score = as_row(jnp.sum(gain, axis=1, keepdims=True), muts)
    score_ref[...] = score
    if peers:
        me = where_ref[slots]
        extra = jnp.concatenate(
            [two_rows(square, vocab), two_rows(score, vocab), jnp.zeros((4, vocab), F32)], axis=0
        ).astype(BF16)
        for k in range(1, peers + 1):
            their = part_ref[pl.ds(pl.multiple_of((me ^ k) * share, share), share), :]
            msg_refs[k - 1][0:share, :] = their.astype(BF16)
            msg_refs[k - 1][share : share + 8, :] = extra


def logit_part(where, slots, un, gains, mut_row, mut_id, mut_nat, peers):
    share, wide = slots[0].shape
    total = share * len(slots)
    vocab = un.shape[1]
    muts = mut_row.shape[0]
    whole = pl.BlockSpec(memory_space=pltpu.VMEM)
    return pl.pallas_call(
        functools.partial(logit_kernel, share, peers),
        in_specs=[pl.BlockSpec(memory_space=pltpu.SMEM)] + [whole] * (5 + len(slots)),
        out_specs=[whole] * (3 + peers),
        out_shape=[
            jax.ShapeDtypeStruct((total, vocab), F32),
            jax.ShapeDtypeStruct((1, total), F32),
            jax.ShapeDtypeStruct((1, muts), F32),
        ]
        + [jax.ShapeDtypeStruct((share + 8, vocab), BF16)] * peers,
        scratch_shapes=[pltpu.VMEM((total, wide), F32)],
        compiler_params=SMALL,
        name="logit_part",
    )(where, un, gains, mut_row, mut_id, mut_nat, *slots)


def final_kernel(feats, where_ref, log_ref, square_ref, score_ref, nat_ref, row_ref, *rest):
    msg_refs, out_ref = rest[:-1], rest[-1]
    me, piece = where_ref[0], where_ref[1]
    share = nat_ref.shape[0]
    vocab = log_ref.shape[1]
    total = square_ref.shape[1]
    muts = score_ref.shape[1]
    width = out_ref.shape[1]
    if msg_refs:
        logits = log_ref[pl.ds(pl.multiple_of(me * share, share), share), :]
    else:
        logits = log_ref[...]
    square, score = square_ref[...], score_ref[...]
    for msg_ref in msg_refs:
        logits = logits + msg_ref[0:share, :].astype(F32)
        extra = msg_ref[share : share + 8, :].astype(F32)
        square = square + (extra[0:1, 0:total] + extra[1:2, 0:total])
        score = score + (extra[2:3, 0:muts] + extra[3:4, 0:muts])
    scale_row = lax.rsqrt(square / feats + EPS)
    r = lax.broadcasted_iota(jnp.int32, (share, total), 0)
    c = lax.broadcasted_iota(jnp.int32, (share, total), 1)
    scale = jnp.sum(jnp.where(c == r + me * share, scale_row, 0.0), axis=1, keepdims=True)
    logits = logits * scale
    top = jnp.max(logits, axis=1, keepdims=True)
    norm = top + jnp.log(jnp.sum(jnp.exp(logits - top), axis=1, keepdims=True))
    words = lax.broadcasted_iota(jnp.int32, (share, vocab), 1)
    like = jnp.sum(jnp.where(words == nat_ref[...], logits, 0.0), axis=1, keepdims=True) - norm
    r = lax.broadcasted_iota(jnp.int32, (share, width), 0)
    c = lax.broadcasted_iota(jnp.int32, (share, width), 1)
    out_ref[0:1, :] = jnp.sum(jnp.where(c == r + piece * share, like, 0.0), axis=0, keepdims=True)
    r = lax.broadcasted_iota(jnp.int32, (muts, total), 0)
    c = lax.broadcasted_iota(jnp.int32, (muts, total), 1)
    at_mut = jnp.sum(jnp.where(c == row_ref[...], scale_row, 0.0), axis=1, keepdims=True)
    out_ref[1:2, 0:muts] = score * as_row(at_mut, muts)


def final_part(feats, where, logits, squares, scores, nat, mut_row, msgs, width):
    whole = pl.BlockSpec(memory_space=pltpu.VMEM)
    return pl.pallas_call(
        functools.partial(final_kernel, float(feats)),
        in_specs=[pl.BlockSpec(memory_space=pltpu.SMEM)] + [whole] * (5 + len(msgs)),
        out_specs=whole,
        out_shape=jax.ShapeDtypeStruct((2, width), F32),
        compiler_params=SMALL,
        name="final_part",
    )(where, logits, squares, scores, nat, mut_row, *msgs)


def total_kernel(*refs):
    like_ref, score_ref = refs[-2:]
    total = functools.reduce(lambda p, q: p + q, [ref[...] for ref in refs[:-2]])
    like_ref[...] = total[0:1, 0 : like_ref.shape[1]]
    score_ref[...] = total[1:2, 0 : score_ref.shape[1]]


def total_part(pieces, rows, muts):
    whole = pl.BlockSpec(memory_space=pltpu.VMEM)
    return pl.pallas_call(
        total_kernel,
        in_specs=[whole] * len(pieces),
        out_specs=[whole] * 2,
        out_shape=[jax.ShapeDtypeStruct((1, rows), F32), jax.ShapeDtypeStruct((1, muts), F32)],
        compiler_params=SMALL,
        name="total_part",
    )(*pieces)


def owners(rows_held, rows_wanted):
    return [i * rows_wanted // rows_held for i in range(lax.axis_size("ctx"))]


def hand_on(value, owner, bit, holders):
    count, shards = lax.axis_size("ctx"), lax.axis_size("mp")
    pairs = [(i * shards + (owner[i] ^ h), i * shards + (owner[i] ^ h ^ bit)) for i in range(count) for h in holders]
    return lax.ppermute(value, ("ctx", "mp"), pairs)


def feature_rows(unembed, norm_gain, rows_wanted, z, m, first_move):
    shards = lax.axis_size("mp")
    held = unembed.shape[0]
    if held % rows_wanted != 0:
        unembed = lax.all_gather(unembed, "mp", axis=0, tiled=True)
        norm_gain = lax.all_gather(norm_gain, "mp", axis=0, tiled=True)
        return tuple(lax.dynamic_slice_in_dim(v, z * rows_wanted, rows_wanted, 0) for v in (unembed, norm_gain))
    owner = owners(held, rows_wanted)
    ratio = held // rows_wanted
    place = m ^ (z // ratio)
    result = []
    for value, moved in ((unembed, first_move), (norm_gain, None)):
        value = lax.dynamic_slice_in_dim(value, (z % ratio) * rows_wanted, rows_wanted, 0)
        bit, holders, known = shards // 2, [0], place == 0
        while bit:
            if moved is None:
                moved = hand_on(value, owner, bit, holders)
            value = jnp.where(known, value, moved)
            holders = holders + [h ^ bit for h in holders]
            known = sum((place == h).astype(jnp.int32) for h in holders) > 0
            bit, moved = bit // 2, None
        result.append(value)
    return tuple(result)


def split_half(value, upper):
    half = value.shape[0] // 2
    keep = lax.dynamic_slice_in_dim(value, upper * half, half, 0)
    send = lax.dynamic_slice_in_dim(value, (1 - upper) * half, half, 0)
    return keep, send


def project(gated, weight, m):
    shards = lax.axis_size("mp")
    bit = 1
    value = None
    while bit < shards:
        upper = (m // bit) % 2
        keep, send = split_half(gated if value is None else value, upper)
        if value is None:
            sent = jnp.dot(send, weight, preferred_element_type=F32).astype(BF16)
            keep = jnp.dot(keep, weight, preferred_element_type=F32)
        else:
            sent = send.astype(BF16)
        got = swap(sent, "mp", bit)
        value = keep + got.astype(F32)
        bit *= 2
    return jnp.dot(gated, weight, preferred_element_type=F32) if value is None else value


def row_piece(m):
    shards = lax.axis_size("mp")
    piece, bit = 0, 1
    while bit < shards:
        piece = piece * 2 + (m // bit) % 2
        bit *= 2
    return piece


def body(streams, short_filter, mode_params, out_weight, norm_gain, unembed, native, mut_pos, mut_ids):
    rows, _ = streams.shape[1:]
    count, shards = lax.axis_size("ctx"), lax.axis_size("mp")
    z = lax.axis_index("ctx")
    quick = count == 4
    modes_t = jnp.swapaxes(mode_params, 1, 2)
    me = z.astype(jnp.int32)[None]
    y, gate, start, msg, filt, modes_t = local_part(streams, short_filter, modes_t, native)
    nat_at = 2 * mode_params.shape[2] + 12
    if quick:
        msgs = [msg]
        for k in range(1, count):
            msgs.append(swap(msg, "ctx", k))
        width_out = out_weight.shape[1]
        moved = None
        if unembed.shape[0] == width_out and shards > 1:
            moved = hand_on(unembed, owners(width_out, width_out), shards // 2, [0])
        gated = carry_part(me, filt, modes_t, y, gate, start, msgs, False)
        nat_rows = msgs
    else:
        moved = None
        every = lax.all_gather(msg, "ctx")
        gated = carry_part(me, filt, modes_t, y, gate, start, [every], True)
        nat_rows = every
    gated, nat_rows, native, mut_pos, mut_ids, z, m, norm_gain = lax.optimization_barrier(
        (gated, nat_rows, native, mut_pos, mut_ids, z, lax.axis_index("mp"), norm_gain)
    )
    if quick:
        nat_rows = jnp.stack([nat_rows[k][nat_at, : 2 * rows] for k in range(count)])[z ^ jnp.arange(count)]
    else:
        nat_rows = nat_rows[:, nat_at, : 2 * rows]
    nat_rows = nat_rows.astype(jnp.int32)
    nat_all = (nat_rows[:, :rows] * 256 + nat_rows[:, rows:]).reshape(-1)

    un, gains = feature_rows(unembed, norm_gain, out_weight.shape[1], z, m, moved)
    piece = row_piece(m)
    share = rows // shards
    block, inner = mut_pos // rows, mut_pos % rows
    mut_row = jnp.where(inner // share == piece, block * share + inner % share, -1)[:, None]
    mut_nat = nat_all[mut_pos][:, None]

    if quick:
        middle = [(1, 2), (2, 1)]
        beside = swap(gated, "ctx", 1)
        mid_a = lax.ppermute(gated, "ctx", middle)
        mid_b = lax.ppermute(beside, "ctx", middle)
        far_a = swap(mid_a, "ctx", 1)
        far_b = swap(mid_b, "ctx", 1)
        third = mid_a + far_a
        fourth = mid_b + far_b
        blocks = [gated, beside, third, fourth]
        low = z < 2
        where = [z, z ^ 1, jnp.where(low, 2, 1), jnp.where(low, 3, 0)]
    else:
        every = lax.all_gather(gated, "ctx")
        blocks = [every[b] for b in range(count)]
        where = list(range(count))
    where = jnp.stack([jnp.asarray(w, jnp.int32) for w in where + [z]])
    if quick:
        out_weight = bring(gated, out_weight)
    slots = []
    for part in blocks:
        slots.append(project(part, out_weight, m))
    peers = count - 1 if quick else 0
    part, squares, scores, *msgs = logit_part(where, slots, un, gains[None, :], mut_row, mut_ids[:, None], mut_nat, peers)
    if quick:
        for k in range(1, count):
            msgs[k - 1] = swap(msgs[k - 1], "ctx", k)
    else:
        part = lax.psum_scatter(part, "ctx", scatter_dimension=0, tiled=True)
        squares = lax.psum(squares, "ctx")
        scores = lax.psum(scores, "ctx")

    own_nat = lax.dynamic_slice_in_dim(native, piece * share, share, 0)[:, None]
    spot = jnp.stack([z, piece]).astype(jnp.int32)
    feats = norm_gain.shape[0] * shards
    span = max(rows, mut_pos.shape[0])
    result = final_part(feats, spot, part, squares, scores, own_nat, mut_row, msgs, span)
    pieces = [result] + [swap(result, "mp", k) for k in range(1, shards)]
    like, score = total_part(pieces, rows, mut_pos.shape[0])
    return like[0], score[0]


def solution(mesh):
    in_specs = (
        P(None, ("groups", "ctx"), "mp"),
        P(None, None, "mp"),
        P(None, "mp", None),
        P("mp", "ctx"),
        P("mp"),
        P("mp", None),
        P(("groups", "ctx")),
        P("groups"),
        P("groups"),
    )
    out_specs = (P(("groups", "ctx")), P("groups"))
    return jax.shard_map(body, mesh=mesh, in_specs=in_specs, out_specs=out_specs, check_vma=False)
```

```python
import functools

import jax
import jax.numpy as jnp
from jax import lax
from jax.experimental import pallas as pl
from jax.experimental.pallas import tpu as pltpu
from jax.sharding import PartitionSpec as P


F32 = jnp.float32
BF16 = jnp.bfloat16
LANES = 128
SUBS = 8
EPS = 1e-05


def swap(value, axis, bit):
    count = lax.axis_size(axis)
    return lax.ppermute(value, axis, [(i, i ^ bit) for i in range(count)])


def mix(taps, now, back1, back2):
    return taps[0] * now + taps[1] * back1 + taps[2] * back2


def rounded(value):
    return value.astype(BF16).astype(F32)


def taps_of(filt_ref, stream, cols):
    return [filt_ref[stream, j : j + 1, cols] for j in range(3)]


def lane_slice(tile):
    return pl.ds(pl.multiple_of(tile * LANES, LANES), LANES)


def behind(value):
    sub = lax.broadcasted_iota(jnp.int32, value.shape, 0)
    return jnp.where(sub == 0, 0.0, pltpu.roll(value, 1, 0))


def spread_modes(mode_ref, cols, modes):
    decay = [jnp.broadcast_to(mode_ref[0, m : m + 1, cols], (SUBS, LANES)) for m in range(modes)]
    return decay, [jnp.exp(-d) for d in decay]


def running(state, decay, steps):
    sub = lax.broadcasted_iota(jnp.int32, state.shape, 0)
    for reach in (1, 2, 4):
        power = jnp.exp(-decay * float(steps * reach))
        state = state + jnp.where(sub < reach, 0.0, power * pltpu.roll(state, reach, 0))
    return state


def end_kernel(
    steps, modes, x_any, filt_any, mode_any, nat_any, prod_ref, gate_ref, msg_ref, filt_ref, mode_ref,
    held, nat_ref, xs, sems, side_sems
):
    rows = steps * SUBS
    tiles = held.shape[0]
    base = 2 * modes

    def fetch(tile):
        return pltpu.make_async_copy(x_any.at[1:3, :, lane_slice(tile)], held.at[tile], sems.at[tile])

    sides = [
        pltpu.make_async_copy(src, dst, side_sems.at[k])
        for k, (src, dst) in enumerate(
            ((filt_any, filt_ref), (mode_any, mode_ref), (nat_any, nat_ref), (x_any.at[0], gate_ref))
        )
    ]
    fetch(0).start()
    for side in sides[:3]:
        side.start()

    @pl.loop(1, tiles)
    def _(tile):
        fetch(tile).start()

    sides[3].start()
    for side in sides[:3]:
        side.wait()

    @pl.loop(0, tiles)
    def _(tile):
        cols = lane_slice(tile)
        sub = lax.broadcasted_iota(jnp.int32, (SUBS, LANES), 0)
        decay, fall = spread_modes(mode_ref, cols, modes)
        taps = [taps_of(filt_ref, i, cols) for i in (1, 2)]
        fetch(tile).wait()
        for i in range(2):
            xs[i] = held[tile, i].astype(F32)

        def at(i, t):
            return xs[i, pl.ds(t, SUBS, stride=steps), :]

        back2 = [behind(at(i, steps - 2)) for i in range(2)]
        back1 = [behind(at(i, steps - 1)) for i in range(2)]
        state = [jnp.zeros((SUBS, LANES), F32) for _ in range(modes)]
        for t in range(steps):
            now = [at(i, t) for i in range(2)]
            mixed = [mix(taps[i], now[i], back1[i], back2[i]) for i in range(2)]
            back2, back1 = back1, now
            prod = rounded(mixed[0] * mixed[1])
            if t < 2:
                prod = jnp.where(sub == 0, 0.0, prod)
            prod_ref[t * SUBS : (t + 1) * SUBS, cols] = prod
            state = [f * s + prod for f, s in zip(fall, state)]
        ends = [running(state[m], decay[m], steps)[SUBS - 1 : SUBS, :] for m in range(modes)]
        end = jnp.concatenate(ends, axis=0)
        high = rounded(end)
        edge = [xs[0, 0:2, :], xs[1, 0:2, :], xs[0, rows - 2 : rows, :], xs[1, rows - 2 : rows, :]]
        msg_ref[0 : base + 8, cols] = jnp.concatenate([high, end - high] + edge, axis=0).astype(BF16)

    sides[3].wait()
    width = gate_ref.shape[1]
    ids = nat_ref[...]
    empty = jnp.zeros((1, width - 2 * rows), jnp.int32)
    ids = jnp.concatenate([ids // 256, ids % 256, empty], axis=1).astype(F32)
    head = gate_ref[0:16, :].astype(F32)
    tail = gate_ref[rows - 16 : rows, :].astype(F32)
    other = jnp.concatenate([tail[14:16, :], head[0:2, :], ids, jnp.zeros((3, width), F32)], axis=0)
    msg_ref[base + 8 : base + 16, :] = other.astype(BF16)


def local_kernel(steps, modes, filt_ref, mode_ref, prod_ref, x_ref, y_ref, gate_ref, start_ref, xs, gs):
    @pl.loop(0, x_ref.shape[1] // LANES)
    def _(tile):
        cols = lane_slice(tile)
        decay, fall = spread_modes(mode_ref, cols, modes)
        res = [jnp.broadcast_to(mode_ref[1, m : m + 1, cols], (SUBS, LANES)) for m in range(modes)]
        taps = taps_of(filt_ref, 0, cols)
        xs[...] = x_ref[:, cols].astype(F32)
        back2 = behind(xs[pl.ds(steps - 2, SUBS, stride=steps), :])
        back1 = behind(xs[pl.ds(steps - 1, SUBS, stride=steps), :])
        state = [jnp.zeros((SUBS, LANES), F32) for _ in range(modes)]
        for t in range(steps):
            now = xs[pl.ds(t, SUBS, stride=steps), :]
            gs[pl.ds(t, SUBS, stride=steps), :] = mix(taps, now, back1, back2)
            back2, back1 = back1, now
            prod = prod_ref[t * SUBS : (t + 1) * SUBS, cols]
            state = [f * s + prod for f, s in zip(fall, state)]
            y_ref[t * SUBS : (t + 1) * SUBS, cols] = functools.reduce(
                lambda p, q: p + q, [r * s for r, s in zip(res, state)]
            )
        gate_ref[:, cols] = gs[...].astype(BF16)
        for m in range(modes):
            start_ref[m * SUBS : (m + 1) * SUBS, cols] = behind(running(state[m], decay[m], steps))


SMALL = pltpu.CompilerParams(vmem_limit_bytes=16 * 2**20)


def in_vmem():
    return pl.BlockSpec(memory_space=pltpu.VMEM)


def end_part(streams, filt, modes_t, native):
    rows, width = streams.shape[1:]
    modes = modes_t.shape[1]
    steps = rows // SUBS
    tiles = width // LANES
    msg_rows = 2 * modes + 16
    return pl.pallas_call(
        functools.partial(end_kernel, steps, modes),
        in_specs=[pl.BlockSpec(memory_space=pltpu.HBM)] * 4,
        out_specs=[in_vmem()] * 5,
        out_shape=[
            pltpu.VMEM((rows, width), F32),
            pltpu.VMEM((rows, width), BF16),
            pltpu.VMEM((msg_rows, width), BF16),
            pltpu.VMEM(filt.shape, F32),
            pltpu.VMEM(modes_t.shape, F32),
        ],
        scratch_shapes=[
            pltpu.VMEM((tiles, 2, rows, LANES), BF16),
            pltpu.VMEM((1, rows), jnp.int32),
            pltpu.VMEM((2, rows, LANES), F32),
            pltpu.SemaphoreType.DMA((tiles,)),
            pltpu.SemaphoreType.DMA((4,)),
        ],
        compiler_params=SMALL,
        name="end_part",
    )(*[pltpu.with_memory_space_constraint(v, pltpu.HBM) for v in (streams, filt, modes_t, native[None, :])])


def local_part(filt, modes_t, prod, gate_stream):
    rows, width = prod.shape
    modes = modes_t.shape[1]
    return pl.pallas_call(
        functools.partial(local_kernel, rows // SUBS, modes),
        in_specs=[in_vmem()] * 4,
        out_specs=[in_vmem()] * 3,
        out_shape=[
            pltpu.VMEM((rows, width), F32),
            pltpu.VMEM((rows, width), BF16),
            pltpu.VMEM((modes * SUBS, width), F32),
        ],
        input_output_aliases={2: 0, 3: 1},
        scratch_shapes=[pltpu.VMEM((rows, LANES), F32), pltpu.VMEM((rows, LANES), F32)],
        compiler_params=SMALL,
        name="local_part",
    )(*[pltpu.with_memory_space_constraint(v, pltpu.VMEM) for v in (filt, modes_t, prod, gate_stream)])


def carry_kernel(steps, modes, stacked, count, where_ref, filt_ref, mode_ref, y_ref, gate_ref, start_ref, *rest):
    msg_refs, (out_ref, held, conv) = rest[:-3], rest[-3:]
    me = where_ref[0]
    rows = steps * SUBS
    base = 2 * modes

    @pl.loop(0, y_ref.shape[1] // LANES)
    def _(tile):
        cols = lane_slice(tile)
        sub = lax.broadcasted_iota(jnp.int32, (SUBS, LANES), 0)
        for k in range(count):
            if stacked:
                held[k] = msg_refs[0][k, :, cols].astype(F32)
            else:
                held[me ^ k] = msg_refs[k][:, cols].astype(F32)
        decay = mode_ref[0, :, cols]
        taps = [taps_of(filt_ref, i, cols) for i in range(3)]

        def firsts(own, prior, keep):
            pair = []
            for i, lane in ((1, 0), (2, 2)):
                f0 = own[base + lane : base + lane + 1, :]
                f1 = own[base + lane + 1 : base + lane + 2, :]
                l2 = jnp.where(keep, prior[base + lane + 4 : base + lane + 5, :], 0.0)
                l1 = jnp.where(keep, prior[base + lane + 5 : base + lane + 6, :], 0.0)
                pair.append((mix(taps[i], f0, l1, l2), mix(taps[i], f1, f0, l1)))
            return rounded(pair[0][0] * pair[1][0]), rounded(pair[0][1] * pair[1][1])

        full = jnp.exp(-decay * float(rows))
        near0 = jnp.exp(-decay * float(rows - 1))
        near1 = jnp.exp(-decay * float(rows - 2))

        def advance(b, entering):
            own = held[b]
            p0, p1 = firsts(own, held[jnp.maximum(b - 1, 0)], b > 0)
            end = own[0:modes, :] + own[modes : 2 * modes, :] + near0 * p0 + near1 * p1
            return jnp.where(b < me, full * entering + end, entering)

        entering = jnp.zeros((modes, LANES), F32)
        if count <= 8:
            for b in range(count - 1):
                entering = advance(b, entering)
        else:
            entering = lax.fori_loop(0, count - 1, advance, entering)
        own = held[me]
        prior = held[jnp.maximum(me - 1, 0)]
        p0, p1 = firsts(own, prior, me > 0)
        later = (
            jnp.exp(-decay * float(steps)) * entering
            + jnp.exp(-decay * float(steps - 1)) * p0
            + jnp.exp(-decay * float(steps - 2)) * p1
        )
        shift = float(steps) * jnp.maximum(sub - 1, 0).astype(F32)
        fall, res, flow = [], [], []
        for m in range(modes):
            d = jnp.broadcast_to(decay[m : m + 1, :], (SUBS, LANES))
            r = jnp.broadcast_to(mode_ref[1, m : m + 1, cols], (SUBS, LANES))
            fall.append(jnp.exp(-d))
            res.append(r)
            begin = jnp.where(sub == 0, entering[m : m + 1, :], jnp.exp(-d * shift) * later[m : m + 1, :])
            flow.append(r * (start_ref[m * SUBS : (m + 1) * SUBS, cols] + begin))
        inject = (p0, p1)
        for t in range(steps):
            flow = [f * v for f, v in zip(fall, flow)]
            if t < 2:
                extra = jnp.where(sub == 0, inject[t], 0.0)
                flow = [v + r * extra for v, r in zip(flow, res)]
            conv[pl.ds(t, SUBS, stride=steps), :] = functools.reduce(
                lambda p, q: p + q, flow, y_ref[t * SUBS : (t + 1) * SUBS, cols]
            )
        g0 = own[base + 10 : base + 11, :]
        g1 = own[base + 11 : base + 12, :]
        l2 = jnp.where(me > 0, prior[base + 8 : base + 9, :], 0.0)
        l1 = jnp.where(me > 0, prior[base + 9 : base + 10, :], 0.0)
        head0 = mix(taps[0], g0, l1, l2)
        head1 = mix(taps[0], g1, g0, l1)
        gate = gate_ref[:, cols].astype(F32)
        line = lax.broadcasted_iota(jnp.int32, (16, LANES), 0)
        head = jnp.where(line == 0, rounded(head0), jnp.where(line == 1, rounded(head1), gate[0:16, :]))
        out_ref[0:16, cols] = (head * rounded(conv[0:16, :])).astype(BF16)
        out_ref[16:rows, cols] = (gate[16:rows, :] * rounded(conv[16:rows, :])).astype(BF16)


def carry_part(me, filt, modes_t, y, gate, start, msgs, stacked):
    rows, width = y.shape
    modes = modes_t.shape[1]
    steps = rows // SUBS
    count = msgs[0].shape[0] if stacked else len(msgs)
    msg_rows = msgs[0].shape[-2]
    return pl.pallas_call(
        functools.partial(carry_kernel, steps, modes, stacked, count),
        in_specs=[pl.BlockSpec(memory_space=pltpu.SMEM)] + [in_vmem()] * (5 + len(msgs)),
        out_specs=in_vmem(),
        out_shape=jax.ShapeDtypeStruct((rows, width), BF16),
        scratch_shapes=[pltpu.VMEM((count, msg_rows, LANES), F32), pltpu.VMEM((rows, LANES), F32)],
        compiler_params=SMALL,
        cost_estimate=pl.CostEstimate(flops=rows * width * 32, bytes_accessed=rows * width * 8, transcendentals=0),
        name="carry_part",
    )(me, *[pltpu.with_memory_space_constraint(v, pltpu.VMEM) for v in (filt, modes_t, y, gate, start, *msgs)])


def bring_kernel(later_any, src_any, out_ref, sem):
    copy = pltpu.make_async_copy(src_any, out_ref, sem)
    copy.start()
    copy.wait()


def bring(later, weight):
    return pl.pallas_call(
        bring_kernel,
        in_specs=[pl.BlockSpec(memory_space=pl.ANY), pl.BlockSpec(memory_space=pltpu.HBM)],
        out_specs=in_vmem(),
        out_shape=pltpu.VMEM(weight.shape, weight.dtype),
        scratch_shapes=[pltpu.SemaphoreType.DMA],
        compiler_params=SMALL,
        name="bring",
    )(later, pltpu.with_memory_space_constraint(weight, pltpu.HBM))


def as_row(col, width):
    rows = col.shape[0]
    r = lax.broadcasted_iota(jnp.int32, (rows, width), 0)
    c = lax.broadcasted_iota(jnp.int32, (rows, width), 1)
    return jnp.sum(jnp.where(r == c, col, 0.0), axis=0, keepdims=True)


def exact_dot(onehot, values):
    high = values.astype(BF16)
    low = (values - high.astype(F32)).astype(BF16)
    return jnp.dot(onehot, high, preferred_element_type=F32) + jnp.dot(onehot, low, preferred_element_type=F32)


def two_rows(row, width):
    high = rounded(row)
    both = jnp.concatenate([high, row - high], axis=0)
    return jnp.concatenate([both, jnp.zeros((2, width - row.shape[1]), F32)], axis=1)


def logit_kernel(share, peers, where_ref, un_ref, gain_ref, row_ref, id_ref, nat_ref, *rest):
    slots = where_ref.shape[0] - 1
    slot_refs, rest = rest[:slots], rest[slots:]
    part_ref, square_ref, score_ref = rest[:3]
    msg_refs, acc = rest[3 : 3 + peers], rest[-1]
    for k in range(slots):
        acc[pl.ds(pl.multiple_of(where_ref[k] * share, share), share), :] = slot_refs[k][...]
    values = acc[...]
    total = values.shape[0]
    square = as_row(jnp.sum(values * values, axis=1, keepdims=True), total)
    square_ref[...] = square
    part = jnp.dot((values * gain_ref[...]).astype(BF16), un_ref[...], preferred_element_type=F32)
    part_ref[...] = part
    muts = row_ref.shape[0]
    vocab = part.shape[1]
    spots = lax.broadcasted_iota(jnp.int32, (muts, total), 1)
    picked = exact_dot((spots == row_ref[...]).astype(BF16), part)
    words = lax.broadcasted_iota(jnp.int32, (muts, vocab), 1)
    gain = jnp.where(words == id_ref[...], picked, 0.0) - jnp.where(words == nat_ref[...], picked, 0.0)
    score = as_row(jnp.sum(gain, axis=1, keepdims=True), muts)
    score_ref[...] = score
    if peers:
        me = where_ref[slots]
        extra = jnp.concatenate(
            [two_rows(square, vocab), two_rows(score, vocab), jnp.zeros((4, vocab), F32)], axis=0
        ).astype(BF16)
        for k in range(1, peers + 1):
            their = part_ref[pl.ds(pl.multiple_of((me ^ k) * share, share), share), :]
            msg_refs[k - 1][0:share, :] = their.astype(BF16)
            msg_refs[k - 1][share : share + 8, :] = extra


def logit_part(where, slots, un, gains, mut_row, mut_id, mut_nat, peers):
    share, wide = slots[0].shape
    total = share * len(slots)
    vocab = un.shape[1]
    muts = mut_row.shape[0]
    whole = pl.BlockSpec(memory_space=pltpu.VMEM)
    return pl.pallas_call(
        functools.partial(logit_kernel, share, peers),
        in_specs=[pl.BlockSpec(memory_space=pltpu.SMEM)] + [whole] * (5 + len(slots)),
        out_specs=[whole] * (3 + peers),
        out_shape=[
            jax.ShapeDtypeStruct((total, vocab), F32),
            jax.ShapeDtypeStruct((1, total), F32),
            jax.ShapeDtypeStruct((1, muts), F32),
        ]
        + [jax.ShapeDtypeStruct((share + 8, vocab), BF16)] * peers,
        scratch_shapes=[pltpu.VMEM((total, wide), F32)],
        compiler_params=SMALL,
        name="logit_part",
    )(where, un, gains, mut_row, mut_id, mut_nat, *slots)


def final_kernel(feats, where_ref, log_ref, square_ref, score_ref, nat_ref, row_ref, *rest):
    msg_refs, out_ref = rest[:-1], rest[-1]
    me, piece = where_ref[0], where_ref[1]
    share = nat_ref.shape[0]
    vocab = log_ref.shape[1]
    total = square_ref.shape[1]
    muts = score_ref.shape[1]
    width = out_ref.shape[1]
    if msg_refs:
        logits = log_ref[pl.ds(pl.multiple_of(me * share, share), share), :]
    else:
        logits = log_ref[...]
    square, score = square_ref[...], score_ref[...]
    for msg_ref in msg_refs:
        logits = logits + msg_ref[0:share, :].astype(F32)
        extra = msg_ref[share : share + 8, :].astype(F32)
        square = square + (extra[0:1, 0:total] + extra[1:2, 0:total])
        score = score + (extra[2:3, 0:muts] + extra[3:4, 0:muts])
    scale_row = lax.rsqrt(square / feats + EPS)
    r = lax.broadcasted_iota(jnp.int32, (share, total), 0)
    c = lax.broadcasted_iota(jnp.int32, (share, total), 1)
    scale = jnp.sum(jnp.where(c == r + me * share, scale_row, 0.0), axis=1, keepdims=True)
    logits = logits * scale
    top = jnp.max(logits, axis=1, keepdims=True)
    norm = top + jnp.log(jnp.sum(jnp.exp(logits - top), axis=1, keepdims=True))
    words = lax.broadcasted_iota(jnp.int32, (share, vocab), 1)
    like = jnp.sum(jnp.where(words == nat_ref[...], logits, 0.0), axis=1, keepdims=True) - norm
    r = lax.broadcasted_iota(jnp.int32, (share, width), 0)
    c = lax.broadcasted_iota(jnp.int32, (share, width), 1)
    out_ref[0:1, :] = jnp.sum(jnp.where(c == r + piece * share, like, 0.0), axis=0, keepdims=True)
    r = lax.broadcasted_iota(jnp.int32, (muts, total), 0)
    c = lax.broadcasted_iota(jnp.int32, (muts, total), 1)
    at_mut = jnp.sum(jnp.where(c == row_ref[...], scale_row, 0.0), axis=1, keepdims=True)
    out_ref[1:2, 0:muts] = score * as_row(at_mut, muts)


def final_part(feats, where, logits, squares, scores, nat, mut_row, msgs, width):
    whole = pl.BlockSpec(memory_space=pltpu.VMEM)
    return pl.pallas_call(
        functools.partial(final_kernel, float(feats)),
        in_specs=[pl.BlockSpec(memory_space=pltpu.SMEM)] + [whole] * (5 + len(msgs)),
        out_specs=whole,
        out_shape=jax.ShapeDtypeStruct((2, width), F32),
        compiler_params=SMALL,
        name="final_part",
    )(where, logits, squares, scores, nat, mut_row, *msgs)


def total_kernel(*refs):
    like_ref, score_ref = refs[-2:]
    total = functools.reduce(lambda p, q: p + q, [ref[...] for ref in refs[:-2]])
    like_ref[...] = total[0:1, 0 : like_ref.shape[1]]
    score_ref[...] = total[1:2, 0 : score_ref.shape[1]]


def total_part(pieces, rows, muts):
    whole = pl.BlockSpec(memory_space=pltpu.VMEM)
    return pl.pallas_call(
        total_kernel,
        in_specs=[whole] * len(pieces),
        out_specs=[whole] * 2,
        out_shape=[jax.ShapeDtypeStruct((1, rows), F32), jax.ShapeDtypeStruct((1, muts), F32)],
        compiler_params=SMALL,
        name="total_part",
    )(*pieces)


def owners(rows_held, rows_wanted):
    return [i * rows_wanted // rows_held for i in range(lax.axis_size("ctx"))]


def hand_on(value, owner, bit, holders):
    count, shards = lax.axis_size("ctx"), lax.axis_size("mp")
    pairs = [(i * shards + (owner[i] ^ h), i * shards + (owner[i] ^ h ^ bit)) for i in range(count) for h in holders]
    return lax.ppermute(value, ("ctx", "mp"), pairs)


def feature_rows(unembed, norm_gain, rows_wanted, z, m):
    shards = lax.axis_size("mp")
    held = unembed.shape[0]
    if held % rows_wanted != 0:
        unembed = lax.all_gather(unembed, "mp", axis=0, tiled=True)
        norm_gain = lax.all_gather(norm_gain, "mp", axis=0, tiled=True)
        return tuple(lax.dynamic_slice_in_dim(v, z * rows_wanted, rows_wanted, 0) for v in (unembed, norm_gain))
    owner = owners(held, rows_wanted)
    ratio = held // rows_wanted
    place = m ^ (z // ratio)
    result = []
    for value in (unembed, norm_gain):
        value = lax.dynamic_slice_in_dim(value, (z % ratio) * rows_wanted, rows_wanted, 0)
        bit, holders, known = shards // 2, [0], place == 0
        while bit:
            moved = hand_on(value, owner, bit, holders)
            value = jnp.where(known, value, moved)
            holders = holders + [h ^ bit for h in holders]
            known = sum((place == h).astype(jnp.int32) for h in holders) > 0
            bit //= 2
        result.append(value)
    return tuple(result)


def split_half(value, upper):
    half = value.shape[0] // 2
    keep = lax.dynamic_slice_in_dim(value, upper * half, half, 0)
    send = lax.dynamic_slice_in_dim(value, (1 - upper) * half, half, 0)
    return keep, send


def project(gated, weight, m):
    shards = lax.axis_size("mp")
    bit = 1
    value = None
    while bit < shards:
        upper = (m // bit) % 2
        keep, send = split_half(gated if value is None else value, upper)
        if value is None:
            sent = jnp.dot(send, weight, preferred_element_type=F32).astype(BF16)
            keep = lax.optimization_barrier(jnp.dot(keep, weight, preferred_element_type=F32))
        else:
            sent = send.astype(BF16)
        got = swap(sent, "mp", bit)
        value = keep + got.astype(F32)
        bit *= 2
    return jnp.dot(gated, weight, preferred_element_type=F32) if value is None else value


def row_piece(m):
    shards = lax.axis_size("mp")
    piece, bit = 0, 1
    while bit < shards:
        piece = piece * 2 + (m // bit) % 2
        bit *= 2
    return piece


def body(streams, short_filter, mode_params, out_weight, norm_gain, unembed, native, mut_pos, mut_ids):
    rows, _ = streams.shape[1:]
    count, shards = lax.axis_size("ctx"), lax.axis_size("mp")
    z = lax.axis_index("ctx")
    quick = count == 4
    modes_t = jnp.swapaxes(mode_params, 1, 2)
    me = z.astype(jnp.int32)[None]
    prod, gate_stream, msg, filt, modes_t = end_part(streams, short_filter, modes_t, native)
    y, gate, start = local_part(filt, modes_t, prod, gate_stream)
    nat_at = 2 * mode_params.shape[2] + 12
    if quick:
        msgs = [msg]
        for k in range(1, count):
            msgs.append(swap(msg, "ctx", k))
        gated = carry_part(me, filt, modes_t, y, gate, start, msgs, False)
        nat_rows = msgs
    else:
        every = lax.all_gather(msg, "ctx")
        gated = carry_part(me, filt, modes_t, y, gate, start, [every], True)
        nat_rows = every
    gated, nat_rows, native, mut_pos, mut_ids, z, m, norm_gain = lax.optimization_barrier(
        (gated, nat_rows, native, mut_pos, mut_ids, z, lax.axis_index("mp"), norm_gain)
    )
    if quick:
        nat_rows = jnp.stack([nat_rows[k][nat_at, : 2 * rows] for k in range(count)])[z ^ jnp.arange(count)]
    else:
        nat_rows = nat_rows[:, nat_at, : 2 * rows]
    nat_rows = nat_rows.astype(jnp.int32)
    nat_all = (nat_rows[:, :rows] * 256 + nat_rows[:, rows:]).reshape(-1)

    un, gains = feature_rows(unembed, norm_gain, out_weight.shape[1], z, m)
    piece = row_piece(m)
    share = rows // shards
    block, inner = mut_pos // rows, mut_pos % rows
    mut_row = jnp.where(inner // share == piece, block * share + inner % share, -1)[:, None]
    mut_nat = nat_all[mut_pos][:, None]

    if quick:
        middle = [(1, 2), (2, 1)]
        beside = swap(gated, "ctx", 1)
        mid_a = lax.ppermute(gated, "ctx", middle)
        mid_b = lax.ppermute(beside, "ctx", middle)
        far_a = swap(mid_a, "ctx", 1)
        far_b = swap(mid_b, "ctx", 1)
        third = mid_a + far_a
        fourth = mid_b + far_b
        blocks = [gated, beside, third, fourth]
        low = z < 2
        where = [z, z ^ 1, jnp.where(low, 2, 1), jnp.where(low, 3, 0)]
    else:
        every = lax.all_gather(gated, "ctx")
        blocks = [every[b] for b in range(count)]
        where = list(range(count))
    where = jnp.stack([jnp.asarray(w, jnp.int32) for w in where + [z]])
    if quick:
        out_weight = bring(gated, out_weight)
    slots = []
    for part in blocks:
        slots.append(project(part, out_weight, m))
    peers = count - 1 if quick else 0
    part, squares, scores, *msgs = logit_part(where, slots, un, gains[None, :], mut_row, mut_ids[:, None], mut_nat, peers)
    if quick:
        for k in range(1, count):
            msgs[k - 1] = swap(msgs[k - 1], "ctx", k)
    else:
        part = lax.psum_scatter(part, "ctx", scatter_dimension=0, tiled=True)
        squares = lax.psum(squares, "ctx")
        scores = lax.psum(scores, "ctx")

    own_nat = lax.dynamic_slice_in_dim(native, piece * share, share, 0)[:, None]
    spot = jnp.stack([z, piece]).astype(jnp.int32)
    feats = norm_gain.shape[0] * shards
    span = max(rows, mut_pos.shape[0])
    result = final_part(feats, spot, part, squares, scores, own_nat, mut_row, msgs, span)
    pieces = [result] + [swap(result, "mp", k) for k in range(1, shards)]
    like, score = total_part(pieces, rows, mut_pos.shape[0])
    return like[0], score[0]


def solution(mesh):
    in_specs = (
        P(None, ("groups", "ctx"), "mp"),
        P(None, None, "mp"),
        P(None, "mp", None),
        P("mp", "ctx"),
        P("mp"),
        P("mp", None),
        P(("groups", "ctx")),
        P("groups"),
        P("groups"),
    )
    out_specs = (P(("groups", "ctx")), P("groups"))
    return jax.shard_map(body, mesh=mesh, in_specs=in_specs, out_specs=out_specs, check_vma=False)
```

```python
import functools

import jax
import jax.numpy as jnp
from jax import lax
from jax.experimental import pallas as pl
from jax.experimental.pallas import tpu as pltpu
from jax.sharding import PartitionSpec as P


F32 = jnp.float32
BF16 = jnp.bfloat16
LANES = 128
SUBS = 8
EPS = 1e-05


def swap(value, axis, bit):
    count = lax.axis_size(axis)
    return lax.ppermute(value, axis, [(i, i ^ bit) for i in range(count)])


def mix(taps, now, back1, back2):
    return taps[0] * now + taps[1] * back1 + taps[2] * back2


def rounded(value):
    return value.astype(BF16).astype(F32)


def taps_of(filt_ref, stream, cols):
    return [filt_ref[stream, j : j + 1, cols] for j in range(3)]


def lane_slice(tile):
    return pl.ds(pl.multiple_of(tile * LANES, LANES), LANES)


def behind(value):
    sub = lax.broadcasted_iota(jnp.int32, value.shape, 0)
    return jnp.where(sub == 0, 0.0, pltpu.roll(value, 1, 0))


def spread_modes(mode_ref, cols, modes):
    decay = [jnp.broadcast_to(mode_ref[0, m : m + 1, cols], (SUBS, LANES)) for m in range(modes)]
    return decay, [jnp.exp(-d) for d in decay]


def running(state, decay, steps):
    sub = lax.broadcasted_iota(jnp.int32, state.shape, 0)
    for reach in (1, 2, 4):
        power = jnp.exp(-decay * float(steps * reach))
        state = state + jnp.where(sub < reach, 0.0, power * pltpu.roll(state, reach, 0))
    return state


def end_kernel(
    steps, modes, x_any, filt_any, mode_any, nat_any, prod_ref, gate_ref, msg_ref, filt_ref, mode_ref,
    held, nat_ref, xs, sems, side_sems
):
    rows = steps * SUBS
    tiles = held.shape[0]
    base = 2 * modes

    def fetch(tile):
        return pltpu.make_async_copy(x_any.at[1:3, :, lane_slice(tile)], held.at[tile], sems.at[tile])

    sides = [
        pltpu.make_async_copy(src, dst, side_sems.at[k])
        for k, (src, dst) in enumerate(
            ((filt_any, filt_ref), (mode_any, mode_ref), (nat_any, nat_ref), (x_any.at[0], gate_ref))
        )
    ]
    fetch(0).start()
    for side in sides[:3]:
        side.start()

    @pl.loop(1, tiles)
    def _(tile):
        fetch(tile).start()

    sides[3].start()
    for side in sides[:3]:
        side.wait()

    @pl.loop(0, tiles)
    def _(tile):
        cols = lane_slice(tile)
        sub = lax.broadcasted_iota(jnp.int32, (SUBS, LANES), 0)
        decay, fall = spread_modes(mode_ref, cols, modes)
        taps = [taps_of(filt_ref, i, cols) for i in (1, 2)]
        fetch(tile).wait()
        for i in range(2):
            xs[i] = held[tile, i].astype(F32)

        def at(i, t):
            return xs[i, pl.ds(t, SUBS, stride=steps), :]

        back2 = [behind(at(i, steps - 2)) for i in range(2)]
        back1 = [behind(at(i, steps - 1)) for i in range(2)]
        state = [jnp.zeros((SUBS, LANES), F32) for _ in range(modes)]
        for t in range(steps):
            now = [at(i, t) for i in range(2)]
            mixed = [mix(taps[i], now[i], back1[i], back2[i]) for i in range(2)]
            back2, back1 = back1, now
            prod = rounded(mixed[0] * mixed[1])
            if t < 2:
                prod = jnp.where(sub == 0, 0.0, prod)
            prod_ref[t * SUBS : (t + 1) * SUBS, cols] = prod
            state = [f * s + prod for f, s in zip(fall, state)]
        ends = [running(state[m], decay[m], steps)[SUBS - 1 : SUBS, :] for m in range(modes)]
        end = jnp.concatenate(ends, axis=0)
        high = rounded(end)
        edge = [xs[0, 0:2, :], xs[1, 0:2, :], xs[0, rows - 2 : rows, :], xs[1, rows - 2 : rows, :]]
        msg_ref[0 : base + 8, cols] = jnp.concatenate([high, end - high] + edge, axis=0).astype(BF16)

    sides[3].wait()
    width = gate_ref.shape[1]
    ids = nat_ref[...]
    empty = jnp.zeros((1, width - 2 * rows), jnp.int32)
    ids = jnp.concatenate([ids // 256, ids % 256, empty], axis=1).astype(F32)
    head = gate_ref[0:16, :].astype(F32)
    tail = gate_ref[rows - 16 : rows, :].astype(F32)
    other = jnp.concatenate([tail[14:16, :], head[0:2, :], ids, jnp.zeros((3, width), F32)], axis=0)
    msg_ref[base + 8 : base + 16, :] = other.astype(BF16)


def local_kernel(steps, modes, filt_ref, mode_ref, prod_ref, x_ref, y_ref, gate_ref, start_ref, xs, gs):
    @pl.loop(0, x_ref.shape[1] // LANES)
    def _(tile):
        cols = lane_slice(tile)
        decay, fall = spread_modes(mode_ref, cols, modes)
        res = [jnp.broadcast_to(mode_ref[1, m : m + 1, cols], (SUBS, LANES)) for m in range(modes)]
        taps = taps_of(filt_ref, 0, cols)
        xs[...] = x_ref[:, cols].astype(F32)
        back2 = behind(xs[pl.ds(steps - 2, SUBS, stride=steps), :])
        back1 = behind(xs[pl.ds(steps - 1, SUBS, stride=steps), :])
        state = [jnp.zeros((SUBS, LANES), F32) for _ in range(modes)]
        for t in range(steps):
            now = xs[pl.ds(t, SUBS, stride=steps), :]
            gs[pl.ds(t, SUBS, stride=steps), :] = mix(taps, now, back1, back2)
            back2, back1 = back1, now
            prod = prod_ref[t * SUBS : (t + 1) * SUBS, cols]
            state = [f * s + prod for f, s in zip(fall, state)]
            y_ref[t * SUBS : (t + 1) * SUBS, cols] = functools.reduce(
                lambda p, q: p + q, [r * s for r, s in zip(res, state)]
            )
        gate_ref[:, cols] = gs[...].astype(BF16)
        for m in range(modes):
            start_ref[m * SUBS : (m + 1) * SUBS, cols] = behind(running(state[m], decay[m], steps))


SMALL = pltpu.CompilerParams(vmem_limit_bytes=16 * 2**20)


def in_vmem():
    return pl.BlockSpec(memory_space=pltpu.VMEM)


def end_part(streams, filt, modes_t, native):
    rows, width = streams.shape[1:]
    modes = modes_t.shape[1]
    steps = rows // SUBS
    tiles = width // LANES
    msg_rows = 2 * modes + 16
    return pl.pallas_call(
        functools.partial(end_kernel, steps, modes),
        in_specs=[pl.BlockSpec(memory_space=pltpu.HBM)] * 4,
        out_specs=[in_vmem()] * 5,
        out_shape=[
            pltpu.VMEM((rows, width), F32),
            pltpu.VMEM((rows, width), BF16),
            pltpu.VMEM((msg_rows, width), BF16),
            pltpu.VMEM(filt.shape, F32),
            pltpu.VMEM(modes_t.shape, F32),
        ],
        scratch_shapes=[
            pltpu.VMEM((tiles, 2, rows, LANES), BF16),
            pltpu.VMEM((1, rows), jnp.int32),
            pltpu.VMEM((2, rows, LANES), F32),
            pltpu.SemaphoreType.DMA((tiles,)),
            pltpu.SemaphoreType.DMA((4,)),
        ],
        compiler_params=SMALL,
        name="end_part",
    )(*[pltpu.with_memory_space_constraint(v, pltpu.HBM) for v in (streams, filt, modes_t, native[None, :])])


def local_part(filt, modes_t, prod, gate_stream):
    rows, width = prod.shape
    modes = modes_t.shape[1]
    return pl.pallas_call(
        functools.partial(local_kernel, rows // SUBS, modes),
        in_specs=[in_vmem()] * 4,
        out_specs=[in_vmem()] * 3,
        out_shape=[
            pltpu.VMEM((rows, width), F32),
            pltpu.VMEM((rows, width), BF16),
            pltpu.VMEM((modes * SUBS, width), F32),
        ],
        input_output_aliases={2: 0, 3: 1},
        scratch_shapes=[pltpu.VMEM((rows, LANES), F32), pltpu.VMEM((rows, LANES), F32)],
        compiler_params=SMALL,
        name="local_part",
    )(*[pltpu.with_memory_space_constraint(v, pltpu.VMEM) for v in (filt, modes_t, prod, gate_stream)])


def carry_kernel(steps, modes, stacked, count, where_ref, filt_ref, mode_ref, y_ref, gate_ref, start_ref, *rest):
    msg_refs, (out_ref, held, conv) = rest[:-3], rest[-3:]
    me = where_ref[0]
    rows = steps * SUBS
    base = 2 * modes

    @pl.loop(0, y_ref.shape[1] // LANES)
    def _(tile):
        cols = lane_slice(tile)
        sub = lax.broadcasted_iota(jnp.int32, (SUBS, LANES), 0)
        for k in range(count):
            if stacked:
                held[k] = msg_refs[0][k, :, cols].astype(F32)
            else:
                held[me ^ k] = msg_refs[k][:, cols].astype(F32)
        decay = mode_ref[0, :, cols]
        taps = [taps_of(filt_ref, i, cols) for i in range(3)]

        def firsts(own, prior, keep):
            pair = []
            for i, lane in ((1, 0), (2, 2)):
                f0 = own[base + lane : base + lane + 1, :]
                f1 = own[base + lane + 1 : base + lane + 2, :]
                l2 = jnp.where(keep, prior[base + lane + 4 : base + lane + 5, :], 0.0)
                l1 = jnp.where(keep, prior[base + lane + 5 : base + lane + 6, :], 0.0)
                pair.append((mix(taps[i], f0, l1, l2), mix(taps[i], f1, f0, l1)))
            return rounded(pair[0][0] * pair[1][0]), rounded(pair[0][1] * pair[1][1])

        full = jnp.exp(-decay * float(rows))
        near0 = jnp.exp(-decay * float(rows - 1))
        near1 = jnp.exp(-decay * float(rows - 2))

        def advance(b, entering):
            own = held[b]
            p0, p1 = firsts(own, held[jnp.maximum(b - 1, 0)], b > 0)
            end = own[0:modes, :] + own[modes : 2 * modes, :] + near0 * p0 + near1 * p1
            return jnp.where(b < me, full * entering + end, entering)

        entering = jnp.zeros((modes, LANES), F32)
        if count <= 8:
            for b in range(count - 1):
                entering = advance(b, entering)
        else:
            entering = lax.fori_loop(0, count - 1, advance, entering)
        own = held[me]
        prior = held[jnp.maximum(me - 1, 0)]
        p0, p1 = firsts(own, prior, me > 0)
        later = (
            jnp.exp(-decay * float(steps)) * entering
            + jnp.exp(-decay * float(steps - 1)) * p0
            + jnp.exp(-decay * float(steps - 2)) * p1
        )
        shift = float(steps) * jnp.maximum(sub - 1, 0).astype(F32)
        fall, res, flow = [], [], []
        for m in range(modes):
            d = jnp.broadcast_to(decay[m : m + 1, :], (SUBS, LANES))
            r = jnp.broadcast_to(mode_ref[1, m : m + 1, cols], (SUBS, LANES))
            fall.append(jnp.exp(-d))
            res.append(r)
            begin = jnp.where(sub == 0, entering[m : m + 1, :], jnp.exp(-d * shift) * later[m : m + 1, :])
            flow.append(r * (start_ref[m * SUBS : (m + 1) * SUBS, cols] + begin))
        inject = (p0, p1)
        for t in range(steps):
            flow = [f * v for f, v in zip(fall, flow)]
            if t < 2:
                extra = jnp.where(sub == 0, inject[t], 0.0)
                flow = [v + r * extra for v, r in zip(flow, res)]
            conv[pl.ds(t, SUBS, stride=steps), :] = functools.reduce(
                lambda p, q: p + q, flow, y_ref[t * SUBS : (t + 1) * SUBS, cols]
            )
        g0 = own[base + 10 : base + 11, :]
        g1 = own[base + 11 : base + 12, :]
        l2 = jnp.where(me > 0, prior[base + 8 : base + 9, :], 0.0)
        l1 = jnp.where(me > 0, prior[base + 9 : base + 10, :], 0.0)
        head0 = mix(taps[0], g0, l1, l2)
        head1 = mix(taps[0], g1, g0, l1)
        gate = gate_ref[:, cols].astype(F32)
        line = lax.broadcasted_iota(jnp.int32, (16, LANES), 0)
        head = jnp.where(line == 0, rounded(head0), jnp.where(line == 1, rounded(head1), gate[0:16, :]))
        out_ref[0:16, cols] = (head * rounded(conv[0:16, :])).astype(BF16)
        out_ref[16:rows, cols] = (gate[16:rows, :] * rounded(conv[16:rows, :])).astype(BF16)


def carry_part(me, filt, modes_t, y, gate, start, msgs, stacked):
    rows, width = y.shape
    modes = modes_t.shape[1]
    steps = rows // SUBS
    count = msgs[0].shape[0] if stacked else len(msgs)
    msg_rows = msgs[0].shape[-2]
    return pl.pallas_call(
        functools.partial(carry_kernel, steps, modes, stacked, count),
        in_specs=[pl.BlockSpec(memory_space=pltpu.SMEM)] + [in_vmem()] * (5 + len(msgs)),
        out_specs=in_vmem(),
        out_shape=jax.ShapeDtypeStruct((rows, width), BF16),
        scratch_shapes=[pltpu.VMEM((count, msg_rows, LANES), F32), pltpu.VMEM((rows, LANES), F32)],
        compiler_params=SMALL,
        cost_estimate=pl.CostEstimate(flops=rows * width * 32, bytes_accessed=rows * width * 8, transcendentals=0),
        name="carry_part",
    )(me, *[pltpu.with_memory_space_constraint(v, pltpu.VMEM) for v in (filt, modes_t, y, gate, start, *msgs)])


def bring_kernel(later_any, src_any, out_ref, sem):
    copy = pltpu.make_async_copy(src_any, out_ref, sem)
    copy.start()
    copy.wait()


def bring(later, weight):
    return pl.pallas_call(
        bring_kernel,
        in_specs=[pl.BlockSpec(memory_space=pl.ANY), pl.BlockSpec(memory_space=pltpu.HBM)],
        out_specs=in_vmem(),
        out_shape=pltpu.VMEM(weight.shape, weight.dtype),
        scratch_shapes=[pltpu.SemaphoreType.DMA],
        compiler_params=SMALL,
        name="bring",
    )(later, pltpu.with_memory_space_constraint(weight, pltpu.HBM))


def as_row(col, width):
    rows = col.shape[0]
    r = lax.broadcasted_iota(jnp.int32, (rows, width), 0)
    c = lax.broadcasted_iota(jnp.int32, (rows, width), 1)
    return jnp.sum(jnp.where(r == c, col, 0.0), axis=0, keepdims=True)


def exact_dot(onehot, values):
    high = values.astype(BF16)
    low = (values - high.astype(F32)).astype(BF16)
    return jnp.dot(onehot, high, preferred_element_type=F32) + jnp.dot(onehot, low, preferred_element_type=F32)


def two_rows(row, width):
    high = rounded(row)
    both = jnp.concatenate([high, row - high], axis=0)
    return jnp.concatenate([both, jnp.zeros((2, width - row.shape[1]), F32)], axis=1)


def logit_kernel(share, peers, where_ref, un_ref, row_ref, id_ref, nat_ref, *rest):
    slots = where_ref.shape[0] - 1
    slot_refs, rest = rest[:slots], rest[slots:]
    part_ref, square_ref, score_ref = rest[:3]
    msg_refs, acc = rest[3 : 3 + peers], rest[-1]
    for k in range(slots):
        acc[pl.ds(pl.multiple_of(where_ref[k] * share, share), share), :] = slot_refs[k][...]
    values = acc[...]
    total = values.shape[0]
    square = as_row(jnp.sum(values * values, axis=1, keepdims=True), total)
    square_ref[...] = square
    part = jnp.dot(values.astype(BF16), un_ref[...], preferred_element_type=F32)
    part_ref[...] = part
    muts = row_ref.shape[0]
    vocab = part.shape[1]
    spots = lax.broadcasted_iota(jnp.int32, (muts, total), 1)
    picked = exact_dot((spots == row_ref[...]).astype(BF16), part)
    words = lax.broadcasted_iota(jnp.int32, (muts, vocab), 1)
    gain = jnp.where(words == id_ref[...], picked, 0.0) - jnp.where(words == nat_ref[...], picked, 0.0)
    score = as_row(jnp.sum(gain, axis=1, keepdims=True), muts)
    score_ref[...] = score
    if peers:
        me = where_ref[slots]
        extra = jnp.concatenate(
            [two_rows(square, vocab), two_rows(score, vocab), jnp.zeros((4, vocab), F32)], axis=0
        ).astype(BF16)
        for k in range(1, peers + 1):
            their = part_ref[pl.ds(pl.multiple_of((me ^ k) * share, share), share), :]
            msg_refs[k - 1][0:share, :] = their.astype(BF16)
            msg_refs[k - 1][share : share + 8, :] = extra


def logit_part(where, slots, un, mut_row, mut_id, mut_nat, peers):
    share, wide = slots[0].shape
    total = share * len(slots)
    vocab = un.shape[1]
    muts = mut_row.shape[0]
    whole = pl.BlockSpec(memory_space=pltpu.VMEM)
    return pl.pallas_call(
        functools.partial(logit_kernel, share, peers),
        in_specs=[pl.BlockSpec(memory_space=pltpu.SMEM)] + [whole] * (4 + len(slots)),
        out_specs=[whole] * (3 + peers),
        out_shape=[
            jax.ShapeDtypeStruct((total, vocab), F32),
            jax.ShapeDtypeStruct((1, total), F32),
            jax.ShapeDtypeStruct((1, muts), F32),
        ]
        + [jax.ShapeDtypeStruct((share + 8, vocab), BF16)] * peers,
        scratch_shapes=[pltpu.VMEM((total, wide), F32)],
        compiler_params=SMALL,
        name="logit_part",
    )(where, un, mut_row, mut_id, mut_nat, *slots)


def final_kernel(feats, where_ref, log_ref, square_ref, score_ref, nat_ref, row_ref, *rest):
    msg_refs, out_ref = rest[:-1], rest[-1]
    me, piece = where_ref[0], where_ref[1]
    share = nat_ref.shape[0]
    vocab = log_ref.shape[1]
    total = square_ref.shape[1]
    muts = score_ref.shape[1]
    width = out_ref.shape[1]
    if msg_refs:
        logits = log_ref[pl.ds(pl.multiple_of(me * share, share), share), :]
    else:
        logits = log_ref[...]
    square, score = square_ref[...], score_ref[...]
    for msg_ref in msg_refs:
        logits = logits + msg_ref[0:share, :].astype(F32)
        extra = msg_ref[share : share + 8, :].astype(F32)
        square = square + (extra[0:1, 0:total] + extra[1:2, 0:total])
        score = score + (extra[2:3, 0:muts] + extra[3:4, 0:muts])
    scale_row = lax.rsqrt(square / feats + EPS)
    r = lax.broadcasted_iota(jnp.int32, (share, total), 0)
    c = lax.broadcasted_iota(jnp.int32, (share, total), 1)
    scale = jnp.sum(jnp.where(c == r + me * share, scale_row, 0.0), axis=1, keepdims=True)
    logits = logits * scale
    top = jnp.max(logits, axis=1, keepdims=True)
    norm = top + jnp.log(jnp.sum(jnp.exp(logits - top), axis=1, keepdims=True))
    words = lax.broadcasted_iota(jnp.int32, (share, vocab), 1)
    like = jnp.sum(jnp.where(words == nat_ref[...], logits, 0.0), axis=1, keepdims=True) - norm
    r = lax.broadcasted_iota(jnp.int32, (share, width), 0)
    c = lax.broadcasted_iota(jnp.int32, (share, width), 1)
    out_ref[0:1, :] = jnp.sum(jnp.where(c == r + piece * share, like, 0.0), axis=0, keepdims=True)
    r = lax.broadcasted_iota(jnp.int32, (muts, total), 0)
    c = lax.broadcasted_iota(jnp.int32, (muts, total), 1)
    at_mut = jnp.sum(jnp.where(c == row_ref[...], scale_row, 0.0), axis=1, keepdims=True)
    out_ref[1:2, 0:muts] = score * as_row(at_mut, muts)


def final_part(feats, where, logits, squares, scores, nat, mut_row, msgs, width):
    whole = pl.BlockSpec(memory_space=pltpu.VMEM)
    return pl.pallas_call(
        functools.partial(final_kernel, float(feats)),
        in_specs=[pl.BlockSpec(memory_space=pltpu.SMEM)] + [whole] * (5 + len(msgs)),
        out_specs=whole,
        out_shape=jax.ShapeDtypeStruct((2, width), F32),
        compiler_params=SMALL,
        name="final_part",
    )(where, logits, squares, scores, nat, mut_row, *msgs)


def total_kernel(*refs):
    like_ref, score_ref = refs[-2:]
    total = functools.reduce(lambda p, q: p + q, [ref[...] for ref in refs[:-2]])
    like_ref[...] = total[0:1, 0 : like_ref.shape[1]]
    score_ref[...] = total[1:2, 0 : score_ref.shape[1]]


def total_part(pieces, rows, muts):
    whole = pl.BlockSpec(memory_space=pltpu.VMEM)
    return pl.pallas_call(
        total_kernel,
        in_specs=[whole] * len(pieces),
        out_specs=[whole] * 2,
        out_shape=[jax.ShapeDtypeStruct((1, rows), F32), jax.ShapeDtypeStruct((1, muts), F32)],
        compiler_params=SMALL,
        name="total_part",
    )(*pieces)


def choose_kernel(place_ref, *refs):
    sources, (out_ref, sem) = refs[:-2], refs[-2:]
    for k, source in enumerate(sources):

        @pl.when(place_ref[0] == k)
        def _():
            copy = pltpu.make_async_copy(source, out_ref, sem)
            copy.start()
            copy.wait()


def choose(place, sources):
    return pl.pallas_call(
        choose_kernel,
        in_specs=[pl.BlockSpec(memory_space=pltpu.SMEM)] + [pl.BlockSpec(memory_space=pltpu.HBM)] * len(sources),
        out_specs=in_vmem(),
        out_shape=pltpu.VMEM(sources[0].shape, sources[0].dtype),
        scratch_shapes=[pltpu.SemaphoreType.DMA],
        compiler_params=SMALL,
        name="choose",
    )(place, *[pltpu.with_memory_space_constraint(v, pltpu.HBM) for v in sources])


def feature_rows(unembed, norm_gain, rows_wanted, z, m):
    count, shards = lax.axis_size("ctx"), lax.axis_size("mp")
    held = unembed.shape[0]
    scaled = (unembed.astype(F32) * norm_gain[:, None]).astype(BF16)
    if held % rows_wanted != 0:
        every = lax.all_gather(scaled, "mp", axis=0, tiled=True)
        return lax.dynamic_slice_in_dim(every, z * rows_wanted, rows_wanted, 0)
    ratio = held // rows_wanted
    piece = lax.dynamic_slice_in_dim(scaled, (z % ratio) * rows_wanted, rows_wanted, 0)
    copies = [piece]
    for k in range(1, shards):
        owner = [i // ratio for i in range(count)]
        pairs = [(i * shards + owner[i], i * shards + (owner[i] ^ k)) for i in range(count)]
        copies.append(lax.ppermute(piece, ("ctx", "mp"), pairs))
    return choose((m ^ (z // ratio)).astype(jnp.int32)[None], copies)


def split_half(value, upper):
    half = value.shape[0] // 2
    keep = lax.dynamic_slice_in_dim(value, upper * half, half, 0)
    send = lax.dynamic_slice_in_dim(value, (1 - upper) * half, half, 0)
    return keep, send


def project(gated, weight, m):
    shards = lax.axis_size("mp")
    bit = 1
    value = None
    while bit < shards:
        upper = (m // bit) % 2
        keep, send = split_half(gated if value is None else value, upper)
        if value is None:
            sent = jnp.dot(send, weight, preferred_element_type=F32).astype(BF16)
            keep = lax.optimization_barrier(jnp.dot(keep, weight, preferred_element_type=F32))
        else:
            sent = send.astype(BF16)
        got = swap(sent, "mp", bit)
        value = keep + got.astype(F32)
        bit *= 2
    return jnp.dot(gated, weight, preferred_element_type=F32) if value is None else value


def row_piece(m):
    shards = lax.axis_size("mp")
    piece, bit = 0, 1
    while bit < shards:
        piece = piece * 2 + (m // bit) % 2
        bit *= 2
    return piece


def body(streams, short_filter, mode_params, out_weight, norm_gain, unembed, native, mut_pos, mut_ids):
    rows, _ = streams.shape[1:]
    count, shards = lax.axis_size("ctx"), lax.axis_size("mp")
    z = lax.axis_index("ctx")
    quick = count == 4
    modes_t = jnp.swapaxes(mode_params, 1, 2)
    me = z.astype(jnp.int32)[None]
    prod, gate_stream, msg, filt, modes_t = end_part(streams, short_filter, modes_t, native)
    y, gate, start = local_part(filt, modes_t, prod, gate_stream)
    nat_at = 2 * mode_params.shape[2] + 12
    if quick:
        msgs = [msg]
        for k in range(1, count):
            msgs.append(swap(msg, "ctx", k))
        gated = carry_part(me, filt, modes_t, y, gate, start, msgs, False)
        nat_rows = msgs
    else:
        every = lax.all_gather(msg, "ctx")
        gated = carry_part(me, filt, modes_t, y, gate, start, [every], True)
        nat_rows = every
    gated, nat_rows, native, mut_pos, mut_ids, z, m, norm_gain = lax.optimization_barrier(
        (gated, nat_rows, native, mut_pos, mut_ids, z, lax.axis_index("mp"), norm_gain)
    )
    un = feature_rows(unembed, norm_gain, out_weight.shape[1], z, m)
    piece = row_piece(m)
    share = rows // shards
    if quick:
        nat_rows = jnp.stack([nat_rows[k][nat_at, : 2 * rows] for k in range(count)])[z ^ jnp.arange(count)]
    else:
        nat_rows = nat_rows[:, nat_at, : 2 * rows]
    nat_rows = nat_rows.astype(jnp.int32)
    nat_all = (nat_rows[:, :rows] * 256 + nat_rows[:, rows:]).reshape(-1)
    block, inner = mut_pos // rows, mut_pos % rows
    mut_row = jnp.where(inner // share == piece, block * share + inner % share, -1)[:, None]
    mut_nat = nat_all[mut_pos][:, None]
    mut_col = mut_ids[:, None]
    own_nat = lax.dynamic_slice_in_dim(native, piece * share, share, 0)[:, None]

    if quick:
        middle = [(1, 2), (2, 1)]
        beside = swap(gated, "ctx", 1)
        mid_a = lax.ppermute(gated, "ctx", middle)
        mid_b = lax.ppermute(beside, "ctx", middle)
        far_a = swap(mid_a, "ctx", 1)
        far_b = swap(mid_b, "ctx", 1)
        third = mid_a + far_a
        fourth = mid_b + far_b
        blocks = [gated, beside, third, fourth]
        low = z < 2
        where = [z, z ^ 1, jnp.where(low, 2, 1), jnp.where(low, 3, 0)]
    else:
        every = lax.all_gather(gated, "ctx")
        blocks = [every[b] for b in range(count)]
        where = list(range(count))
    where = jnp.stack([jnp.asarray(w, jnp.int32) for w in where + [z]])
    if quick:
        out_weight = bring(gated, out_weight)
    slots = []
    for part in blocks:
        slots.append(project(part, out_weight, m))
    peers = count - 1 if quick else 0
    part, squares, scores, *msgs = logit_part(where, slots, un, mut_row, mut_col, mut_nat, peers)
    if quick:
        for k in range(1, count):
            msgs[k - 1] = swap(msgs[k - 1], "ctx", k)
    else:
        part = lax.psum_scatter(part, "ctx", scatter_dimension=0, tiled=True)
        squares = lax.psum(squares, "ctx")
        scores = lax.psum(scores, "ctx")

    spot = jnp.stack([z, piece]).astype(jnp.int32)
    feats = norm_gain.shape[0] * shards
    span = max(rows, mut_pos.shape[0])
    result = final_part(feats, spot, part, squares, scores, own_nat, mut_row, msgs, span)
    pieces = [result] + [swap(result, "mp", k) for k in range(1, shards)]
    like, score = total_part(pieces, rows, mut_pos.shape[0])
    return like[0], score[0]


def solution(mesh):
    in_specs = (
        P(None, ("groups", "ctx"), "mp"),
        P(None, None, "mp"),
        P(None, "mp", None),
        P("mp", "ctx"),
        P("mp"),
        P("mp", None),
        P(("groups", "ctx")),
        P("groups"),
        P("groups"),
    )
    out_specs = (P(("groups", "ctx")), P("groups"))
    return jax.shard_map(body, mesh=mesh, in_specs=in_specs, out_specs=out_specs, check_vma=False)
```

```python
import functools

import jax
import jax.numpy as jnp
from jax import lax
from jax.experimental import pallas as pl
from jax.experimental.pallas import tpu as pltpu
from jax.sharding import PartitionSpec as P


F32 = jnp.float32
BF16 = jnp.bfloat16
LANES = 128
SUBS = 8
EPS = 1e-05


def swap(value, axis, bit):
    count = lax.axis_size(axis)
    return lax.ppermute(value, axis, [(i, i ^ bit) for i in range(count)])


def mix(taps, now, back1, back2):
    return taps[0] * now + taps[1] * back1 + taps[2] * back2


def rounded(value):
    return value.astype(BF16).astype(F32)


def taps_of(filt_ref, stream, cols):
    return [filt_ref[stream, j : j + 1, cols] for j in range(3)]


def lane_slice(tile):
    return pl.ds(pl.multiple_of(tile * LANES, LANES), LANES)


def behind(value):
    sub = lax.broadcasted_iota(jnp.int32, value.shape, 0)
    return jnp.where(sub == 0, 0.0, pltpu.roll(value, 1, 0))


def spread_modes(mode_ref, cols, modes):
    decay = [jnp.broadcast_to(mode_ref[0, m : m + 1, cols], (SUBS, LANES)) for m in range(modes)]
    return decay, [jnp.exp(-d) for d in decay]


def running(state, decay, steps):
    sub = lax.broadcasted_iota(jnp.int32, state.shape, 0)
    for reach in (1, 2, 4):
        power = jnp.exp(-decay * float(steps * reach))
        state = state + jnp.where(sub < reach, 0.0, power * pltpu.roll(state, reach, 0))
    return state


def end_kernel(
    steps, modes, x_any, filt_any, mode_any, nat_any, prod_ref, gate_ref, msg_ref, filt_ref, mode_ref,
    held, nat_ref, xs, sems, side_sems
):
    rows = steps * SUBS
    tiles = held.shape[0]
    base = 2 * modes

    def fetch(tile):
        return pltpu.make_async_copy(x_any.at[1:3, :, lane_slice(tile)], held.at[tile], sems.at[tile])

    sides = [
        pltpu.make_async_copy(src, dst, side_sems.at[k])
        for k, (src, dst) in enumerate(
            ((filt_any, filt_ref), (mode_any, mode_ref), (nat_any, nat_ref), (x_any.at[0], gate_ref))
        )
    ]
    fetch(0).start()
    for side in sides[:3]:
        side.start()

    @pl.loop(1, tiles)
    def _(tile):
        fetch(tile).start()

    sides[3].start()
    for side in sides[:3]:
        side.wait()

    @pl.loop(0, tiles)
    def _(tile):
        cols = lane_slice(tile)
        sub = lax.broadcasted_iota(jnp.int32, (SUBS, LANES), 0)
        decay, fall = spread_modes(mode_ref, cols, modes)
        taps = [taps_of(filt_ref, i, cols) for i in (1, 2)]
        fetch(tile).wait()
        for i in range(2):
            xs[i] = held[tile, i].astype(F32)

        def at(i, t):
            return xs[i, pl.ds(t, SUBS, stride=steps), :]

        back2 = [behind(at(i, steps - 2)) for i in range(2)]
        back1 = [behind(at(i, steps - 1)) for i in range(2)]
        state = [jnp.zeros((SUBS, LANES), F32) for _ in range(modes)]
        for t in range(steps):
            now = [at(i, t) for i in range(2)]
            mixed = [mix(taps[i], now[i], back1[i], back2[i]) for i in range(2)]
            back2, back1 = back1, now
            prod = rounded(mixed[0] * mixed[1])
            if t < 2:
                prod = jnp.where(sub == 0, 0.0, prod)
            prod_ref[t * SUBS : (t + 1) * SUBS, cols] = prod
            state = [f * s + prod for f, s in zip(fall, state)]
        ends = [running(state[m], decay[m], steps)[SUBS - 1 : SUBS, :] for m in range(modes)]
        end = jnp.concatenate(ends, axis=0)
        high = rounded(end)
        edge = [xs[0, 0:2, :], xs[1, 0:2, :], xs[0, rows - 2 : rows, :], xs[1, rows - 2 : rows, :]]
        msg_ref[0 : base + 8, cols] = jnp.concatenate([high, end - high] + edge, axis=0).astype(BF16)

    sides[3].wait()
    width = gate_ref.shape[1]
    ids = nat_ref[...]
    empty = jnp.zeros((1, width - 2 * rows), jnp.int32)
    ids = jnp.concatenate([ids // 256, ids % 256, empty], axis=1).astype(F32)
    head = gate_ref[0:16, :].astype(F32)
    tail = gate_ref[rows - 16 : rows, :].astype(F32)
    other = jnp.concatenate([tail[14:16, :], head[0:2, :], ids, jnp.zeros((3, width), F32)], axis=0)
    msg_ref[base + 8 : base + 16, :] = other.astype(BF16)


def local_kernel(steps, modes, filt_ref, mode_ref, prod_ref, x_ref, y_ref, gate_ref, start_ref, xs, gs):
    @pl.loop(0, x_ref.shape[1] // LANES)
    def _(tile):
        cols = lane_slice(tile)
        decay, fall = spread_modes(mode_ref, cols, modes)
        res = [jnp.broadcast_to(mode_ref[1, m : m + 1, cols], (SUBS, LANES)) for m in range(modes)]
        taps = taps_of(filt_ref, 0, cols)
        xs[...] = x_ref[:, cols].astype(F32)
        back2 = behind(xs[pl.ds(steps - 2, SUBS, stride=steps), :])
        back1 = behind(xs[pl.ds(steps - 1, SUBS, stride=steps), :])
        state = [jnp.zeros((SUBS, LANES), F32) for _ in range(modes)]
        for t in range(steps):
            now = xs[pl.ds(t, SUBS, stride=steps), :]
            gs[pl.ds(t, SUBS, stride=steps), :] = mix(taps, now, back1, back2)
            back2, back1 = back1, now
            prod = prod_ref[t * SUBS : (t + 1) * SUBS, cols]
            state = [f * s + prod for f, s in zip(fall, state)]
            y_ref[t * SUBS : (t + 1) * SUBS, cols] = functools.reduce(
                lambda p, q: p + q, [r * s for r, s in zip(res, state)]
            )
        gate_ref[:, cols] = gs[...].astype(BF16)
        for m in range(modes):
            start_ref[m * SUBS : (m + 1) * SUBS, cols] = behind(running(state[m], decay[m], steps))


SMALL = pltpu.CompilerParams(vmem_limit_bytes=16 * 2**20)


def in_vmem():
    return pl.BlockSpec(memory_space=pltpu.VMEM)


def end_part(streams, filt, modes_t, native):
    rows, width = streams.shape[1:]
    modes = modes_t.shape[1]
    steps = rows // SUBS
    tiles = width // LANES
    msg_rows = 2 * modes + 16
    return pl.pallas_call(
        functools.partial(end_kernel, steps, modes),
        in_specs=[pl.BlockSpec(memory_space=pltpu.HBM)] * 4,
        out_specs=[in_vmem()] * 5,
        out_shape=[
            pltpu.VMEM((rows, width), F32),
            pltpu.VMEM((rows, width), BF16),
            pltpu.VMEM((msg_rows, width), BF16),
            pltpu.VMEM(filt.shape, F32),
            pltpu.VMEM(modes_t.shape, F32),
        ],
        scratch_shapes=[
            pltpu.VMEM((tiles, 2, rows, LANES), BF16),
            pltpu.VMEM((1, rows), jnp.int32),
            pltpu.VMEM((2, rows, LANES), F32),
            pltpu.SemaphoreType.DMA((tiles,)),
            pltpu.SemaphoreType.DMA((4,)),
        ],
        compiler_params=SMALL,
        name="end_part",
    )(*[pltpu.with_memory_space_constraint(v, pltpu.HBM) for v in (streams, filt, modes_t, native[None, :])])


def local_part(filt, modes_t, prod, gate_stream):
    rows, width = prod.shape
    modes = modes_t.shape[1]
    return pl.pallas_call(
        functools.partial(local_kernel, rows // SUBS, modes),
        in_specs=[in_vmem()] * 4,
        out_specs=[in_vmem()] * 3,
        out_shape=[
            pltpu.VMEM((rows, width), F32),
            pltpu.VMEM((rows, width), BF16),
            pltpu.VMEM((modes * SUBS, width), F32),
        ],
        input_output_aliases={2: 0, 3: 1},
        scratch_shapes=[pltpu.VMEM((rows, LANES), F32), pltpu.VMEM((rows, LANES), F32)],
        compiler_params=SMALL,
        name="local_part",
    )(*[pltpu.with_memory_space_constraint(v, pltpu.VMEM) for v in (filt, modes_t, prod, gate_stream)])


def carry_kernel(steps, modes, stacked, count, where_ref, filt_ref, mode_ref, y_ref, gate_ref, start_ref, *rest):
    msg_refs, (out_ref, held, conv) = rest[:-3], rest[-3:]
    me = where_ref[0]
    rows = steps * SUBS
    base = 2 * modes

    @pl.loop(0, y_ref.shape[1] // LANES)
    def _(tile):
        cols = lane_slice(tile)
        sub = lax.broadcasted_iota(jnp.int32, (SUBS, LANES), 0)
        for k in range(count):
            if stacked:
                held[k] = msg_refs[0][k, :, cols].astype(F32)
            else:
                held[me ^ k] = msg_refs[k][:, cols].astype(F32)
        decay = mode_ref[0, :, cols]
        taps = [taps_of(filt_ref, i, cols) for i in range(3)]

        def firsts(own, prior, keep):
            pair = []
            for i, lane in ((1, 0), (2, 2)):
                f0 = own[base + lane : base + lane + 1, :]
                f1 = own[base + lane + 1 : base + lane + 2, :]
                l2 = jnp.where(keep, prior[base + lane + 4 : base + lane + 5, :], 0.0)
                l1 = jnp.where(keep, prior[base + lane + 5 : base + lane + 6, :], 0.0)
                pair.append((mix(taps[i], f0, l1, l2), mix(taps[i], f1, f0, l1)))
            return rounded(pair[0][0] * pair[1][0]), rounded(pair[0][1] * pair[1][1])

        full = jnp.exp(-decay * float(rows))
        near0 = jnp.exp(-decay * float(rows - 1))
        near1 = jnp.exp(-decay * float(rows - 2))

        def advance(b, entering):
            own = held[b]
            p0, p1 = firsts(own, held[jnp.maximum(b - 1, 0)], b > 0)
            end = own[0:modes, :] + own[modes : 2 * modes, :] + near0 * p0 + near1 * p1
            return jnp.where(b < me, full * entering + end, entering)

        entering = jnp.zeros((modes, LANES), F32)
        if count <= 8:
            for b in range(count - 1):
                entering = advance(b, entering)
        else:
            entering = lax.fori_loop(0, count - 1, advance, entering)
        own = held[me]
        prior = held[jnp.maximum(me - 1, 0)]
        p0, p1 = firsts(own, prior, me > 0)
        later = (
            jnp.exp(-decay * float(steps)) * entering
            + jnp.exp(-decay * float(steps - 1)) * p0
            + jnp.exp(-decay * float(steps - 2)) * p1
        )
        shift = float(steps) * jnp.maximum(sub - 1, 0).astype(F32)
        fall, res, flow = [], [], []
        for m in range(modes):
            d = jnp.broadcast_to(decay[m : m + 1, :], (SUBS, LANES))
            r = jnp.broadcast_to(mode_ref[1, m : m + 1, cols], (SUBS, LANES))
            fall.append(jnp.exp(-d))
            res.append(r)
            begin = jnp.where(sub == 0, entering[m : m + 1, :], jnp.exp(-d * shift) * later[m : m + 1, :])
            flow.append(r * (start_ref[m * SUBS : (m + 1) * SUBS, cols] + begin))
        inject = (p0, p1)
        for t in range(steps):
            flow = [f * v for f, v in zip(fall, flow)]
            if t < 2:
                extra = jnp.where(sub == 0, inject[t], 0.0)
                flow = [v + r * extra for v, r in zip(flow, res)]
            conv[pl.ds(t, SUBS, stride=steps), :] = functools.reduce(
                lambda p, q: p + q, flow, y_ref[t * SUBS : (t + 1) * SUBS, cols]
            )
        g0 = own[base + 10 : base + 11, :]
        g1 = own[base + 11 : base + 12, :]
        l2 = jnp.where(me > 0, prior[base + 8 : base + 9, :], 0.0)
        l1 = jnp.where(me > 0, prior[base + 9 : base + 10, :], 0.0)
        head0 = mix(taps[0], g0, l1, l2)
        head1 = mix(taps[0], g1, g0, l1)
        gate = gate_ref[:, cols].astype(F32)
        line = lax.broadcasted_iota(jnp.int32, (16, LANES), 0)
        head = jnp.where(line == 0, rounded(head0), jnp.where(line == 1, rounded(head1), gate[0:16, :]))
        out_ref[0:16, cols] = (head * rounded(conv[0:16, :])).astype(BF16)
        out_ref[16:rows, cols] = (gate[16:rows, :] * rounded(conv[16:rows, :])).astype(BF16)


def carry_part(me, filt, modes_t, y, gate, start, msgs, stacked):
    rows, width = y.shape
    modes = modes_t.shape[1]
    steps = rows // SUBS
    count = msgs[0].shape[0] if stacked else len(msgs)
    msg_rows = msgs[0].shape[-2]
    return pl.pallas_call(
        functools.partial(carry_kernel, steps, modes, stacked, count),
        in_specs=[pl.BlockSpec(memory_space=pltpu.SMEM)] + [in_vmem()] * (5 + len(msgs)),
        out_specs=in_vmem(),
        out_shape=jax.ShapeDtypeStruct((rows, width), BF16),
        scratch_shapes=[pltpu.VMEM((count, msg_rows, LANES), F32), pltpu.VMEM((rows, LANES), F32)],
        compiler_params=SMALL,
        cost_estimate=pl.CostEstimate(flops=rows * width * 32, bytes_accessed=rows * width * 8, transcendentals=0),
        name="carry_part",
    )(me, *[pltpu.with_memory_space_constraint(v, pltpu.VMEM) for v in (filt, modes_t, y, gate, start, *msgs)])


def bring_kernel(later_any, src_any, out_ref, sem):
    copy = pltpu.make_async_copy(src_any, out_ref, sem)
    copy.start()
    copy.wait()


def bring(later, weight):
    return pl.pallas_call(
        bring_kernel,
        in_specs=[pl.BlockSpec(memory_space=pl.ANY), pl.BlockSpec(memory_space=pltpu.HBM)],
        out_specs=in_vmem(),
        out_shape=pltpu.VMEM(weight.shape, weight.dtype),
        scratch_shapes=[pltpu.SemaphoreType.DMA],
        compiler_params=SMALL,
        name="bring",
    )(later, pltpu.with_memory_space_constraint(weight, pltpu.HBM))


def as_row(col, width):
    rows = col.shape[0]
    r = lax.broadcasted_iota(jnp.int32, (rows, width), 0)
    c = lax.broadcasted_iota(jnp.int32, (rows, width), 1)
    return jnp.sum(jnp.where(r == c, col, 0.0), axis=0, keepdims=True)


def exact_dot(onehot, values):
    high = values.astype(BF16)
    low = (values - high.astype(F32)).astype(BF16)
    return jnp.dot(onehot, high, preferred_element_type=F32) + jnp.dot(onehot, low, preferred_element_type=F32)


def two_rows(row, width):
    high = rounded(row)
    both = jnp.concatenate([high, row - high], axis=0)
    return jnp.concatenate([both, jnp.zeros((2, width - row.shape[1]), F32)], axis=1)


def logit_kernel(share, given, peers, where_ref, un_ref, row_ref, id_ref, nat_ref, *rest):
    slots = where_ref.shape[0] - 1
    slot_refs, rest = rest[:given], rest[given:]
    part_ref, square_ref, score_ref = rest[:3]
    msg_refs, acc = rest[3 : 3 + peers], rest[-1]
    at = 0
    for slot_ref in slot_refs:
        for k in range(slot_ref.shape[0] // share):
            acc[pl.ds(pl.multiple_of(where_ref[at] * share, share), share), :] = slot_ref[k * share : (k + 1) * share, :]
            at += 1
    values = acc[...]
    total = values.shape[0]
    square = as_row(jnp.sum(values * values, axis=1, keepdims=True), total)
    square_ref[...] = square
    part = jnp.dot(values.astype(BF16), un_ref[...], preferred_element_type=F32)
    part_ref[...] = part
    muts = row_ref.shape[0]
    vocab = part.shape[1]
    spots = lax.broadcasted_iota(jnp.int32, (muts, total), 1)
    picked = exact_dot((spots == row_ref[...]).astype(BF16), part)
    words = lax.broadcasted_iota(jnp.int32, (muts, vocab), 1)
    gain = jnp.where(words == id_ref[...], picked, 0.0) - jnp.where(words == nat_ref[...], picked, 0.0)
    score = as_row(jnp.sum(gain, axis=1, keepdims=True), muts)
    score_ref[...] = score
    if peers:
        me = where_ref[slots]
        extra = jnp.concatenate(
            [two_rows(square, vocab), two_rows(score, vocab), jnp.zeros((4, vocab), F32)], axis=0
        ).astype(BF16)
        for k in range(1, peers + 1):
            their = part_ref[pl.ds(pl.multiple_of((me ^ k) * share, share), share), :]
            msg_refs[k - 1][0:share, :] = their.astype(BF16)
            msg_refs[k - 1][share : share + 8, :] = extra


def logit_part(share, where, slots, un, mut_row, mut_id, mut_nat, peers):
    wide = slots[0].shape[1]
    total = share * (where.shape[0] - 1)
    vocab = un.shape[1]
    muts = mut_row.shape[0]
    whole = pl.BlockSpec(memory_space=pltpu.VMEM)
    return pl.pallas_call(
        functools.partial(logit_kernel, share, len(slots), peers),
        in_specs=[pl.BlockSpec(memory_space=pltpu.SMEM)] + [whole] * (4 + len(slots)),
        out_specs=[whole] * (3 + peers),
        out_shape=[
            jax.ShapeDtypeStruct((total, vocab), F32),
            jax.ShapeDtypeStruct((1, total), F32),
            jax.ShapeDtypeStruct((1, muts), F32),
        ]
        + [jax.ShapeDtypeStruct((share + 8, vocab), BF16)] * peers,
        scratch_shapes=[pltpu.VMEM((total, wide), F32)],
        compiler_params=SMALL,
        name="logit_part",
    )(where, un, mut_row, mut_id, mut_nat, *slots)


def final_kernel(feats, where_ref, log_ref, square_ref, score_ref, nat_ref, row_ref, *rest):
    msg_refs, out_ref = rest[:-1], rest[-1]
    me, piece = where_ref[0], where_ref[1]
    share = nat_ref.shape[0]
    vocab = log_ref.shape[1]
    total = square_ref.shape[1]
    muts = score_ref.shape[1]
    width = out_ref.shape[1]
    if msg_refs:
        logits = log_ref[pl.ds(pl.multiple_of(me * share, share), share), :]
    else:
        logits = log_ref[...]
    square, score = square_ref[...], score_ref[...]
    for msg_ref in msg_refs:
        logits = logits + msg_ref[0:share, :].astype(F32)
        extra = msg_ref[share : share + 8, :].astype(F32)
        square = square + (extra[0:1, 0:total] + extra[1:2, 0:total])
        score = score + (extra[2:3, 0:muts] + extra[3:4, 0:muts])
    scale_row = lax.rsqrt(square / feats + EPS)
    r = lax.broadcasted_iota(jnp.int32, (share, total), 0)
    c = lax.broadcasted_iota(jnp.int32, (share, total), 1)
    scale = jnp.sum(jnp.where(c == r + me * share, scale_row, 0.0), axis=1, keepdims=True)
    logits = logits * scale
    top = jnp.max(logits, axis=1, keepdims=True)
    norm = top + jnp.log(jnp.sum(jnp.exp(logits - top), axis=1, keepdims=True))
    words = lax.broadcasted_iota(jnp.int32, (share, vocab), 1)
    like = jnp.sum(jnp.where(words == nat_ref[...], logits, 0.0), axis=1, keepdims=True) - norm
    r = lax.broadcasted_iota(jnp.int32, (share, width), 0)
    c = lax.broadcasted_iota(jnp.int32, (share, width), 1)
    out_ref[0:1, :] = jnp.sum(jnp.where(c == r + piece * share, like, 0.0), axis=0, keepdims=True)
    r = lax.broadcasted_iota(jnp.int32, (muts, total), 0)
    c = lax.broadcasted_iota(jnp.int32, (muts, total), 1)
    at_mut = jnp.sum(jnp.where(c == row_ref[...], scale_row, 0.0), axis=1, keepdims=True)
    out_ref[1:2, 0:muts] = score * as_row(at_mut, muts)


def final_part(feats, where, logits, squares, scores, nat, mut_row, msgs, width):
    whole = pl.BlockSpec(memory_space=pltpu.VMEM)
    return pl.pallas_call(
        functools.partial(final_kernel, float(feats)),
        in_specs=[pl.BlockSpec(memory_space=pltpu.SMEM)] + [whole] * (5 + len(msgs)),
        out_specs=whole,
        out_shape=jax.ShapeDtypeStruct((2, width), F32),
        compiler_params=SMALL,
        name="final_part",
    )(where, logits, squares, scores, nat, mut_row, *msgs)


def total_kernel(*refs):
    like_ref, score_ref = refs[-2:]
    total = functools.reduce(lambda p, q: p + q, [ref[...] for ref in refs[:-2]])
    like_ref[...] = total[0:1, 0 : like_ref.shape[1]]
    score_ref[...] = total[1:2, 0 : score_ref.shape[1]]


def total_part(pieces, rows, muts):
    whole = pl.BlockSpec(memory_space=pltpu.VMEM)
    return pl.pallas_call(
        total_kernel,
        in_specs=[whole] * len(pieces),
        out_specs=[whole] * 2,
        out_shape=[jax.ShapeDtypeStruct((1, rows), F32), jax.ShapeDtypeStruct((1, muts), F32)],
        compiler_params=SMALL,
        name="total_part",
    )(*pieces)


def choose_kernel(place_ref, *refs):
    sources, (out_ref, sem) = refs[:-2], refs[-2:]
    for k, source in enumerate(sources):

        @pl.when(place_ref[0] == k)
        def _():
            copy = pltpu.make_async_copy(source, out_ref, sem)
            copy.start()
            copy.wait()


def choose(place, sources):
    return pl.pallas_call(
        choose_kernel,
        in_specs=[pl.BlockSpec(memory_space=pltpu.SMEM)] + [pl.BlockSpec(memory_space=pltpu.HBM)] * len(sources),
        out_specs=in_vmem(),
        out_shape=pltpu.VMEM(sources[0].shape, sources[0].dtype),
        scratch_shapes=[pltpu.SemaphoreType.DMA],
        compiler_params=SMALL,
        name="choose",
    )(place, *[pltpu.with_memory_space_constraint(v, pltpu.HBM) for v in sources])


def feature_rows(unembed, norm_gain, rows_wanted, z, m):
    count, shards = lax.axis_size("ctx"), lax.axis_size("mp")
    held = unembed.shape[0]
    scaled = (unembed.astype(F32) * norm_gain[:, None]).astype(BF16)
    if held % rows_wanted != 0:
        every = lax.all_gather(scaled, "mp", axis=0, tiled=True)
        return lax.dynamic_slice_in_dim(every, z * rows_wanted, rows_wanted, 0)
    ratio = held // rows_wanted
    piece = lax.dynamic_slice_in_dim(scaled, (z % ratio) * rows_wanted, rows_wanted, 0)
    copies = [piece]
    for k in range(1, shards):
        owner = [i // ratio for i in range(count)]
        pairs = [(i * shards + owner[i], i * shards + (owner[i] ^ k)) for i in range(count)]
        copies.append(lax.ppermute(piece, ("ctx", "mp"), pairs))
    return choose((m ^ (z // ratio)).astype(jnp.int32)[None], copies)


def half_kernel(groups, which_ref, weight_ref, *refs):
    out_ref = refs[-1]
    half = refs[0].shape[0] // 2
    rows = pl.ds(pl.multiple_of(which_ref[0] * half, half), half)
    parts, at = [], 0
    for size in groups:
        parts.append(functools.reduce(lambda p, q: p + q, [ref[rows, :] for ref in refs[at : at + size]]))
        at += size
    block = parts[0] if len(parts) == 1 else jnp.concatenate(parts, axis=0)
    out_ref[...] = jnp.dot(block, weight_ref[...], preferred_element_type=F32).astype(out_ref.dtype)


def half_part(which, weight, blocks, dtype):
    rows = len(blocks) * (blocks[0][0].shape[0] // 2)
    flat = [part for block in blocks for part in block]
    return pl.pallas_call(
        functools.partial(half_kernel, tuple(len(block) for block in blocks)),
        in_specs=[pl.BlockSpec(memory_space=pltpu.SMEM)] + [in_vmem()] * (1 + len(flat)),
        out_specs=in_vmem(),
        out_shape=jax.ShapeDtypeStruct((rows, weight.shape[1]), dtype),
        compiler_params=SMALL,
        name="half_part",
    )(which.astype(jnp.int32)[None], weight, *flat)


def project(blocks, weight, m):
    shards, count = lax.axis_size("mp"), len(blocks)
    if shards == 1:
        whole = [functools.reduce(lambda p, q: p + q, block) for block in blocks]
        return jnp.dot(jnp.concatenate(whole, axis=0), weight, preferred_element_type=F32)
    bit, value = 1, None
    while bit < shards:
        upper = (m // bit) % 2
        if value is None:
            send = half_part(1 - upper, weight, blocks, BF16)
            keep = half_part(upper, weight, blocks, F32)
        else:
            half = value.shape[0] // count // 2
            pieces = value.reshape(count, 2, half, value.shape[1])
            keep = lax.dynamic_index_in_dim(pieces, upper, 1, False).reshape(count * half, value.shape[1])
            send = lax.dynamic_index_in_dim(pieces, 1 - upper, 1, False).reshape(count * half, value.shape[1])
            send = send.astype(BF16)
        got = swap(send, "mp", bit)
        value = keep + got.astype(F32)
        bit *= 2
    return value


def row_piece(m):
    shards = lax.axis_size("mp")
    piece, bit = 0, 1
    while bit < shards:
        piece = piece * 2 + (m // bit) % 2
        bit *= 2
    return piece


def body(streams, short_filter, mode_params, out_weight, norm_gain, unembed, native, mut_pos, mut_ids):
    rows, _ = streams.shape[1:]
    count, shards = lax.axis_size("ctx"), lax.axis_size("mp")
    z = lax.axis_index("ctx")
    quick = count == 4
    modes_t = jnp.swapaxes(mode_params, 1, 2)
    me = z.astype(jnp.int32)[None]
    prod, gate_stream, msg, filt, modes_t = end_part(streams, short_filter, modes_t, native)
    y, gate, start = local_part(filt, modes_t, prod, gate_stream)
    nat_at = 2 * mode_params.shape[2] + 12
    if quick:
        msgs = [msg]
        for k in range(1, count):
            msgs.append(swap(msg, "ctx", k))
        gated = carry_part(me, filt, modes_t, y, gate, start, msgs, False)
        nat_rows = msgs
    else:
        every = lax.all_gather(msg, "ctx")
        gated = carry_part(me, filt, modes_t, y, gate, start, [every], True)
        nat_rows = every
    gated, nat_rows, native, mut_pos, mut_ids, z, m, norm_gain = lax.optimization_barrier(
        (gated, nat_rows, native, mut_pos, mut_ids, z, lax.axis_index("mp"), norm_gain)
    )
    un = feature_rows(unembed, norm_gain, out_weight.shape[1], z, m)
    piece = row_piece(m)
    share = rows // shards
    if quick:
        nat_rows = jnp.stack([nat_rows[k][nat_at, : 2 * rows] for k in range(count)])[z ^ jnp.arange(count)]
    else:
        nat_rows = nat_rows[:, nat_at, : 2 * rows]
    nat_rows = nat_rows.astype(jnp.int32)
    nat_all = (nat_rows[:, :rows] * 256 + nat_rows[:, rows:]).reshape(-1)
    block, inner = mut_pos // rows, mut_pos % rows
    mut_row = jnp.where(inner // share == piece, block * share + inner % share, -1)[:, None]
    mut_nat = nat_all[mut_pos][:, None]
    mut_col = mut_ids[:, None]
    own_nat = lax.dynamic_slice_in_dim(native, piece * share, share, 0)[:, None]

    if quick:
        middle = [(1, 2), (2, 1)]
        beside = swap(gated, "ctx", 1)
        mid_a = lax.ppermute(gated, "ctx", middle)
        mid_b = lax.ppermute(beside, "ctx", middle)
        far_a = swap(mid_a, "ctx", 1)
        far_b = swap(mid_b, "ctx", 1)
        groups = [[[gated], [beside]], [[mid_a, far_a]], [[mid_b, far_b]]]
        low = z < 2
        where = [z, z ^ 1, jnp.where(low, 2, 1), jnp.where(low, 3, 0)]
    else:
        every = lax.all_gather(gated, "ctx")
        groups = [[[every[b]]] for b in range(count)]
        where = list(range(count))
    where = jnp.stack([jnp.asarray(w, jnp.int32) for w in where + [z]])
    if quick:
        out_weight = bring(gated, out_weight)
    slots = []
    for blocks in groups:
        slots.append(project(blocks, out_weight, m))
    peers = count - 1 if quick else 0
    part, squares, scores, *msgs = logit_part(share, where, slots, un, mut_row, mut_col, mut_nat, peers)
    if quick:
        for k in range(1, count):
            msgs[k - 1] = swap(msgs[k - 1], "ctx", k)
    else:
        part = lax.psum_scatter(part, "ctx", scatter_dimension=0, tiled=True)
        squares = lax.psum(squares, "ctx")
        scores = lax.psum(scores, "ctx")

    spot = jnp.stack([z, piece]).astype(jnp.int32)
    feats = norm_gain.shape[0] * shards
    span = max(rows, mut_pos.shape[0])
    result = final_part(feats, spot, part, squares, scores, own_nat, mut_row, msgs, span)
    pieces = [result] + [swap(result, "mp", k) for k in range(1, shards)]
    like, score = total_part(pieces, rows, mut_pos.shape[0])
    return like[0], score[0]


def solution(mesh):
    in_specs = (
        P(None, ("groups", "ctx"), "mp"),
        P(None, None, "mp"),
        P(None, "mp", None),
        P("mp", "ctx"),
        P("mp"),
        P("mp", None),
        P(("groups", "ctx")),
        P("groups"),
        P("groups"),
    )
    out_specs = (P(("groups", "ctx")), P("groups"))
    return jax.shard_map(body, mesh=mesh, in_specs=in_specs, out_specs=out_specs, check_vma=False)
```

```python
import functools

import jax
import jax.numpy as jnp
from jax import lax
from jax.experimental import pallas as pl
from jax.experimental.pallas import tpu as pltpu
from jax.sharding import PartitionSpec as P


F32 = jnp.float32
BF16 = jnp.bfloat16
LANES = 128
SUBS = 8
EPS = 1e-05


def swap(value, axis, bit):
    count = lax.axis_size(axis)
    return lax.ppermute(value, axis, [(i, i ^ bit) for i in range(count)])


def mix(taps, now, back1, back2):
    return taps[0] * now + taps[1] * back1 + taps[2] * back2


def rounded(value):
    return value.astype(BF16).astype(F32)


def taps_of(filt_ref, stream, cols):
    return [filt_ref[stream, j : j + 1, cols] for j in range(3)]


def lane_slice(tile):
    return pl.ds(pl.multiple_of(tile * LANES, LANES), LANES)


def behind(value):
    sub = lax.broadcasted_iota(jnp.int32, value.shape, 0)
    return jnp.where(sub == 0, 0.0, pltpu.roll(value, 1, 0))


def spread_modes(mode_ref, cols, modes):
    decay = [jnp.broadcast_to(mode_ref[0, m : m + 1, cols], (SUBS, LANES)) for m in range(modes)]
    return decay, [jnp.exp(-d) for d in decay]


def running(state, decay, steps):
    sub = lax.broadcasted_iota(jnp.int32, state.shape, 0)
    for reach in (1, 2, 4):
        power = jnp.exp(-decay * float(steps * reach))
        state = state + jnp.where(sub < reach, 0.0, power * pltpu.roll(state, reach, 0))
    return state


def end_kernel(
    steps, modes, x_any, filt_any, mode_any, nat_any, prod_ref, gate_ref, msg_ref, filt_ref, mode_ref,
    held, nat_ref, xs, sems, side_sems
):
    rows = steps * SUBS
    tiles = held.shape[0]
    base = 2 * modes

    def fetch(tile):
        return pltpu.make_async_copy(x_any.at[1:3, :, lane_slice(tile)], held.at[tile], sems.at[tile])

    sides = [
        pltpu.make_async_copy(src, dst, side_sems.at[k])
        for k, (src, dst) in enumerate(
            ((filt_any, filt_ref), (mode_any, mode_ref), (nat_any, nat_ref), (x_any.at[0], gate_ref))
        )
    ]
    fetch(0).start()
    for side in sides[:3]:
        side.start()

    @pl.loop(1, tiles)
    def _(tile):
        fetch(tile).start()

    sides[3].start()
    for side in sides[:3]:
        side.wait()

    @pl.loop(0, tiles)
    def _(tile):
        cols = lane_slice(tile)
        sub = lax.broadcasted_iota(jnp.int32, (SUBS, LANES), 0)
        decay, fall = spread_modes(mode_ref, cols, modes)
        taps = [taps_of(filt_ref, i, cols) for i in (1, 2)]
        fetch(tile).wait()
        for i in range(2):
            xs[i] = held[tile, i].astype(F32)

        def at(i, t):
            return xs[i, pl.ds(t, SUBS, stride=steps), :]

        back2 = [behind(at(i, steps - 2)) for i in range(2)]
        back1 = [behind(at(i, steps - 1)) for i in range(2)]
        state = [jnp.zeros((SUBS, LANES), F32) for _ in range(modes)]
        for t in range(steps):
            now = [at(i, t) for i in range(2)]
            mixed = [mix(taps[i], now[i], back1[i], back2[i]) for i in range(2)]
            back2, back1 = back1, now
            prod = rounded(mixed[0] * mixed[1])
            if t < 2:
                prod = jnp.where(sub == 0, 0.0, prod)
            prod_ref[t * SUBS : (t + 1) * SUBS, cols] = prod
            state = [f * s + prod for f, s in zip(fall, state)]
        ends = [running(state[m], decay[m], steps)[SUBS - 1 : SUBS, :] for m in range(modes)]
        end = jnp.concatenate(ends, axis=0)
        high = rounded(end)
        edge = [xs[0, 0:2, :], xs[1, 0:2, :], xs[0, rows - 2 : rows, :], xs[1, rows - 2 : rows, :]]
        msg_ref[0 : base + 8, cols] = jnp.concatenate([high, end - high] + edge, axis=0).astype(BF16)

    sides[3].wait()
    width = gate_ref.shape[1]
    ids = nat_ref[...]
    empty = jnp.zeros((1, width - 2 * rows), jnp.int32)
    ids = jnp.concatenate([ids // 256, ids % 256, empty], axis=1).astype(F32)
    head = gate_ref[0:16, :].astype(F32)
    tail = gate_ref[rows - 16 : rows, :].astype(F32)
    other = jnp.concatenate([tail[14:16, :], head[0:2, :], ids, jnp.zeros((3, width), F32)], axis=0)
    msg_ref[base + 8 : base + 16, :] = other.astype(BF16)


def local_kernel(steps, modes, filt_ref, mode_ref, prod_ref, x_ref, y_ref, gate_ref, start_ref, xs, gs):
    @pl.loop(0, x_ref.shape[1] // LANES)
    def _(tile):
        cols = lane_slice(tile)
        decay, fall = spread_modes(mode_ref, cols, modes)
        res = [jnp.broadcast_to(mode_ref[1, m : m + 1, cols], (SUBS, LANES)) for m in range(modes)]
        taps = taps_of(filt_ref, 0, cols)
        xs[...] = x_ref[:, cols].astype(F32)
        back2 = behind(xs[pl.ds(steps - 2, SUBS, stride=steps), :])
        back1 = behind(xs[pl.ds(steps - 1, SUBS, stride=steps), :])
        state = [jnp.zeros((SUBS, LANES), F32) for _ in range(modes)]
        for t in range(steps):
            now = xs[pl.ds(t, SUBS, stride=steps), :]
            gs[pl.ds(t, SUBS, stride=steps), :] = mix(taps, now, back1, back2)
            back2, back1 = back1, now
            prod = prod_ref[t * SUBS : (t + 1) * SUBS, cols]
            state = [f * s + prod for f, s in zip(fall, state)]
            y_ref[t * SUBS : (t + 1) * SUBS, cols] = functools.reduce(
                lambda p, q: p + q, [r * s for r, s in zip(res, state)]
            )
        gate_ref[:, cols] = gs[...].astype(BF16)
        for m in range(modes):
            start_ref[m * SUBS : (m + 1) * SUBS, cols] = behind(running(state[m], decay[m], steps))


SMALL = pltpu.CompilerParams(vmem_limit_bytes=16 * 2**20)


def in_vmem():
    return pl.BlockSpec(memory_space=pltpu.VMEM)


def end_part(streams, filt, modes_t, native):
    rows, width = streams.shape[1:]
    modes = modes_t.shape[1]
    steps = rows // SUBS
    tiles = width // LANES
    msg_rows = 2 * modes + 16
    return pl.pallas_call(
        functools.partial(end_kernel, steps, modes),
        in_specs=[pl.BlockSpec(memory_space=pltpu.HBM)] * 4,
        out_specs=[in_vmem()] * 5,
        out_shape=[
            pltpu.VMEM((rows, width), F32),
            pltpu.VMEM((rows, width), BF16),
            pltpu.VMEM((msg_rows, width), BF16),
            pltpu.VMEM(filt.shape, F32),
            pltpu.VMEM(modes_t.shape, F32),
        ],
        scratch_shapes=[
            pltpu.VMEM((tiles, 2, rows, LANES), BF16),
            pltpu.VMEM((1, rows), jnp.int32),
            pltpu.VMEM((2, rows, LANES), F32),
            pltpu.SemaphoreType.DMA((tiles,)),
            pltpu.SemaphoreType.DMA((4,)),
        ],
        compiler_params=SMALL,
        name="end_part",
    )(*[pltpu.with_memory_space_constraint(v, pltpu.HBM) for v in (streams, filt, modes_t, native[None, :])])


def local_part(filt, modes_t, prod, gate_stream):
    rows, width = prod.shape
    modes = modes_t.shape[1]
    return pl.pallas_call(
        functools.partial(local_kernel, rows // SUBS, modes),
        in_specs=[in_vmem()] * 4,
        out_specs=[in_vmem()] * 3,
        out_shape=[
            pltpu.VMEM((rows, width), F32),
            pltpu.VMEM((rows, width), BF16),
            pltpu.VMEM((modes * SUBS, width), F32),
        ],
        input_output_aliases={2: 0, 3: 1},
        scratch_shapes=[pltpu.VMEM((rows, LANES), F32), pltpu.VMEM((rows, LANES), F32)],
        compiler_params=SMALL,
        name="local_part",
    )(*[pltpu.with_memory_space_constraint(v, pltpu.VMEM) for v in (filt, modes_t, prod, gate_stream)])


def carry_kernel(steps, modes, stacked, count, where_ref, filt_ref, mode_ref, y_ref, gate_ref, start_ref, *rest):
    msg_refs, (out_ref, nat_ref, held, conv) = rest[:-4], rest[-4:]
    me = where_ref[0]
    rows = steps * SUBS
    base = 2 * modes

    @pl.loop(0, y_ref.shape[1] // LANES)
    def _(tile):
        cols = lane_slice(tile)
        sub = lax.broadcasted_iota(jnp.int32, (SUBS, LANES), 0)
        for k in range(count):
            if stacked:
                held[k] = msg_refs[0][k, :, cols].astype(F32)
            else:
                held[me ^ k] = msg_refs[k][:, cols].astype(F32)
        for b in range(count):
            nat_ref[b : b + 1, cols] = held[b, base + 12 : base + 13, :]
        decay = mode_ref[0, :, cols]
        taps = [taps_of(filt_ref, i, cols) for i in range(3)]

        def firsts(own, prior, keep):
            pair = []
            for i, lane in ((1, 0), (2, 2)):
                f0 = own[base + lane : base + lane + 1, :]
                f1 = own[base + lane + 1 : base + lane + 2, :]
                l2 = jnp.where(keep, prior[base + lane + 4 : base + lane + 5, :], 0.0)
                l1 = jnp.where(keep, prior[base + lane + 5 : base + lane + 6, :], 0.0)
                pair.append((mix(taps[i], f0, l1, l2), mix(taps[i], f1, f0, l1)))
            return rounded(pair[0][0] * pair[1][0]), rounded(pair[0][1] * pair[1][1])

        full = jnp.exp(-decay * float(rows))
        near0 = jnp.exp(-decay * float(rows - 1))
        near1 = jnp.exp(-decay * float(rows - 2))

        def advance(b, entering):
            own = held[b]
            p0, p1 = firsts(own, held[jnp.maximum(b - 1, 0)], b > 0)
            end = own[0:modes, :] + own[modes : 2 * modes, :] + near0 * p0 + near1 * p1
            return jnp.where(b < me, full * entering + end, entering)

        entering = jnp.zeros((modes, LANES), F32)
        if count <= 8:
            for b in range(count - 1):
                entering = advance(b, entering)
        else:
            entering = lax.fori_loop(0, count - 1, advance, entering)
        own = held[me]
        prior = held[jnp.maximum(me - 1, 0)]
        p0, p1 = firsts(own, prior, me > 0)
        later = (
            jnp.exp(-decay * float(steps)) * entering
            + jnp.exp(-decay * float(steps - 1)) * p0
            + jnp.exp(-decay * float(steps - 2)) * p1
        )
        shift = float(steps) * jnp.maximum(sub - 1, 0).astype(F32)
        fall, res, flow = [], [], []
        for m in range(modes):
            d = jnp.broadcast_to(decay[m : m + 1, :], (SUBS, LANES))
            r = jnp.broadcast_to(mode_ref[1, m : m + 1, cols], (SUBS, LANES))
            fall.append(jnp.exp(-d))
            res.append(r)
            begin = jnp.where(sub == 0, entering[m : m + 1, :], jnp.exp(-d * shift) * later[m : m + 1, :])
            flow.append(r * (start_ref[m * SUBS : (m + 1) * SUBS, cols] + begin))
        inject = (p0, p1)
        for t in range(steps):
            flow = [f * v for f, v in zip(fall, flow)]
            if t < 2:
                extra = jnp.where(sub == 0, inject[t], 0.0)
                flow = [v + r * extra for v, r in zip(flow, res)]
            conv[pl.ds(t, SUBS, stride=steps), :] = functools.reduce(
                lambda p, q: p + q, flow, y_ref[t * SUBS : (t + 1) * SUBS, cols]
            )
        g0 = own[base + 10 : base + 11, :]
        g1 = own[base + 11 : base + 12, :]
        l2 = jnp.where(me > 0, prior[base + 8 : base + 9, :], 0.0)
        l1 = jnp.where(me > 0, prior[base + 9 : base + 10, :], 0.0)
        head0 = mix(taps[0], g0, l1, l2)
        head1 = mix(taps[0], g1, g0, l1)
        gate = gate_ref[:, cols].astype(F32)
        line = lax.broadcasted_iota(jnp.int32, (16, LANES), 0)
        head = jnp.where(line == 0, rounded(head0), jnp.where(line == 1, rounded(head1), gate[0:16, :]))
        out_ref[0:16, cols] = (head * rounded(conv[0:16, :])).astype(BF16)
        out_ref[16:rows, cols] = (gate[16:rows, :] * rounded(conv[16:rows, :])).astype(BF16)


def carry_part(me, filt, modes_t, y, gate, start, msgs, stacked):
    rows, width = y.shape
    modes = modes_t.shape[1]
    steps = rows // SUBS
    count = msgs[0].shape[0] if stacked else len(msgs)
    msg_rows = msgs[0].shape[-2]
    return pl.pallas_call(
        functools.partial(carry_kernel, steps, modes, stacked, count),
        in_specs=[pl.BlockSpec(memory_space=pltpu.SMEM)] + [in_vmem()] * (5 + len(msgs)),
        out_specs=[in_vmem()] * 2,
        out_shape=[jax.ShapeDtypeStruct((rows, width), BF16), jax.ShapeDtypeStruct((count, width), F32)],
        scratch_shapes=[pltpu.VMEM((count, msg_rows, LANES), F32), pltpu.VMEM((rows, LANES), F32)],
        compiler_params=SMALL,
        cost_estimate=pl.CostEstimate(flops=rows * width * 32, bytes_accessed=rows * width * 8, transcendentals=0),
        name="carry_part",
    )(me, *[pltpu.with_memory_space_constraint(v, pltpu.VMEM) for v in (filt, modes_t, y, gate, start, *msgs)])


def bring_kernel(later_any, src_any, out_ref, sem):
    copy = pltpu.make_async_copy(src_any, out_ref, sem)
    copy.start()
    copy.wait()


def bring(later, weight):
    return pl.pallas_call(
        bring_kernel,
        in_specs=[pl.BlockSpec(memory_space=pl.ANY), pl.BlockSpec(memory_space=pltpu.HBM)],
        out_specs=in_vmem(),
        out_shape=pltpu.VMEM(weight.shape, weight.dtype),
        scratch_shapes=[pltpu.SemaphoreType.DMA],
        compiler_params=SMALL,
        name="bring",
    )(later, pltpu.with_memory_space_constraint(weight, pltpu.HBM))


def as_row(col, width):
    rows = col.shape[0]
    r = lax.broadcasted_iota(jnp.int32, (rows, width), 0)
    c = lax.broadcasted_iota(jnp.int32, (rows, width), 1)
    return jnp.sum(jnp.where(r == c, col, 0.0), axis=0, keepdims=True)


def two_rows(row, width):
    high = rounded(row)
    both = jnp.concatenate([high, row - high], axis=0)
    return jnp.concatenate([both, jnp.zeros((2, width - row.shape[1]), F32)], axis=1)


def logit_kernel(share, given, peers, where_ref, un_ref, row_ref, id_ref, nat_ref, *rest):
    slots = where_ref.shape[0] - 1
    slot_refs, rest = rest[:given], rest[given:]
    part_ref, square_ref, score_ref = rest[:3]
    msg_refs, acc = rest[3 : 3 + peers], rest[-1]
    at = 0
    for slot_ref in slot_refs:
        for k in range(slot_ref.shape[0] // share):
            acc[pl.ds(pl.multiple_of(where_ref[at] * share, share), share), :] = slot_ref[k * share : (k + 1) * share, :]
            at += 1
    values = acc[...]
    total = values.shape[0]
    square = as_row(jnp.sum(values * values, axis=1, keepdims=True), total)
    square_ref[...] = square
    part = jnp.dot(values.astype(BF16), un_ref[...], preferred_element_type=F32)
    part_ref[...] = part
    muts = row_ref.shape[0]
    vocab = part.shape[1]
    high = part.astype(BF16)
    low = (part - high.astype(F32)).astype(BF16)
    words = lax.broadcasted_iota(jnp.int32, (total, vocab), 1)
    both = high.astype(F32) + low.astype(F32)
    native = as_row(jnp.sum(jnp.where(words == nat_ref[...], both, 0.0), axis=1, keepdims=True), total)
    spots = lax.broadcasted_iota(jnp.int32, (muts, total), 1)
    hit = spots == row_ref[...]
    onehot = hit.astype(BF16)
    picked = jnp.dot(onehot, high, preferred_element_type=F32) + jnp.dot(onehot, low, preferred_element_type=F32)
    words = lax.broadcasted_iota(jnp.int32, (muts, vocab), 1)
    chosen = jnp.sum(jnp.where(words == id_ref[...], picked, 0.0), axis=1, keepdims=True)
    base = jnp.sum(jnp.where(hit, native, 0.0), axis=1, keepdims=True)
    score = as_row(chosen - base, muts)
    score_ref[...] = score
    if peers:
        me = where_ref[slots]
        extra = jnp.concatenate(
            [two_rows(square, vocab), two_rows(score, vocab), jnp.zeros((4, vocab), F32)], axis=0
        ).astype(BF16)
        for k in range(1, peers + 1):
            their = part_ref[pl.ds(pl.multiple_of((me ^ k) * share, share), share), :]
            msg_refs[k - 1][0:share, :] = their.astype(BF16)
            msg_refs[k - 1][share : share + 8, :] = extra


def logit_part(share, where, slots, un, mut_row, mut_id, mut_nat, peers):
    wide = slots[0].shape[1]
    total = share * (where.shape[0] - 1)
    vocab = un.shape[1]
    muts = mut_row.shape[0]
    whole = pl.BlockSpec(memory_space=pltpu.VMEM)
    return pl.pallas_call(
        functools.partial(logit_kernel, share, len(slots), peers),
        in_specs=[pl.BlockSpec(memory_space=pltpu.SMEM)] + [whole] * (4 + len(slots)),
        out_specs=[whole] * (3 + peers),
        out_shape=[
            jax.ShapeDtypeStruct((total, vocab), F32),
            jax.ShapeDtypeStruct((1, total), F32),
            jax.ShapeDtypeStruct((1, muts), F32),
        ]
        + [jax.ShapeDtypeStruct((share + 8, vocab), BF16)] * peers,
        scratch_shapes=[pltpu.VMEM((total, wide), F32)],
        compiler_params=SMALL,
        name="logit_part",
    )(where, un, mut_row, mut_id, mut_nat, *slots)


def final_kernel(feats, share, where_ref, log_ref, square_ref, score_ref, nat_ref, row_ref, *rest):
    msg_refs, out_ref = rest[:-1], rest[-1]
    me, piece = where_ref[0], where_ref[1]
    vocab = log_ref.shape[1]
    total = square_ref.shape[1]
    muts = score_ref.shape[1]
    width = out_ref.shape[1]
    if msg_refs:
        logits = log_ref[pl.ds(pl.multiple_of(me * share, share), share), :]
    else:
        logits = log_ref[...]
    square, score = square_ref[...], score_ref[...]
    for msg_ref in msg_refs:
        logits = logits + msg_ref[0:share, :].astype(F32)
        extra = msg_ref[share : share + 8, :].astype(F32)
        square = square + (extra[0:1, 0:total] + extra[1:2, 0:total])
        score = score + (extra[2:3, 0:muts] + extra[3:4, 0:muts])
    scale_row = lax.rsqrt(square / feats + EPS)
    r = lax.broadcasted_iota(jnp.int32, (share, total), 0)
    c = lax.broadcasted_iota(jnp.int32, (share, total), 1)
    scale = jnp.sum(jnp.where(c == r + me * share, scale_row, 0.0), axis=1, keepdims=True)
    logits = logits * scale
    top = jnp.max(logits, axis=1, keepdims=True)
    norm = top + jnp.log(jnp.sum(jnp.exp(logits - top), axis=1, keepdims=True))
    words = lax.broadcasted_iota(jnp.int32, (share, vocab), 1)
    native = nat_ref[pl.ds(pl.multiple_of(me * share, share), share), :]
    like = jnp.sum(jnp.where(words == native, logits, 0.0), axis=1, keepdims=True) - norm
    r = lax.broadcasted_iota(jnp.int32, (share, width), 0)
    c = lax.broadcasted_iota(jnp.int32, (share, width), 1)
    out_ref[0:1, :] = jnp.sum(jnp.where(c == r + piece * share, like, 0.0), axis=0, keepdims=True)
    r = lax.broadcasted_iota(jnp.int32, (muts, total), 0)
    c = lax.broadcasted_iota(jnp.int32, (muts, total), 1)
    at_mut = jnp.sum(jnp.where(c == row_ref[...], scale_row, 0.0), axis=1, keepdims=True)
    out_ref[1:2, 0:muts] = score * as_row(at_mut, muts)


def final_part(feats, share, where, logits, squares, scores, nat, mut_row, msgs, width):
    whole = pl.BlockSpec(memory_space=pltpu.VMEM)
    return pl.pallas_call(
        functools.partial(final_kernel, float(feats), share),
        in_specs=[pl.BlockSpec(memory_space=pltpu.SMEM)] + [whole] * (5 + len(msgs)),
        out_specs=whole,
        out_shape=jax.ShapeDtypeStruct((2, width), F32),
        compiler_params=SMALL,
        name="final_part",
    )(where, logits, squares, scores, nat, mut_row, *msgs)


def total_kernel(*refs):
    like_ref, score_ref = refs[-2:]
    total = functools.reduce(lambda p, q: p + q, [ref[...] for ref in refs[:-2]])
    like_ref[...] = total[0:1, 0 : like_ref.shape[1]]
    score_ref[...] = total[1:2, 0 : score_ref.shape[1]]


def total_part(pieces, rows, muts):
    whole = pl.BlockSpec(memory_space=pltpu.VMEM)
    return pl.pallas_call(
        total_kernel,
        in_specs=[whole] * len(pieces),
        out_specs=[whole] * 2,
        out_shape=[jax.ShapeDtypeStruct((1, rows), F32), jax.ShapeDtypeStruct((1, muts), F32)],
        compiler_params=SMALL,
        name="total_part",
    )(*pieces)


def choose_kernel(place_ref, *refs):
    sources, (out_ref, sem) = refs[:-2], refs[-2:]
    for k, source in enumerate(sources):

        @pl.when(place_ref[0] == k)
        def _():
            copy = pltpu.make_async_copy(source, out_ref, sem)
            copy.start()
            copy.wait()


def choose(place, sources):
    return pl.pallas_call(
        choose_kernel,
        in_specs=[pl.BlockSpec(memory_space=pltpu.SMEM)] + [pl.BlockSpec(memory_space=pltpu.HBM)] * len(sources),
        out_specs=in_vmem(),
        out_shape=pltpu.VMEM(sources[0].shape, sources[0].dtype),
        scratch_shapes=[pltpu.SemaphoreType.DMA],
        compiler_params=SMALL,
        name="choose",
    )(place, *[pltpu.with_memory_space_constraint(v, pltpu.HBM) for v in sources])


def feature_rows(unembed, norm_gain, rows_wanted, z, m):
    count, shards = lax.axis_size("ctx"), lax.axis_size("mp")
    held = unembed.shape[0]
    scaled = (unembed.astype(F32) * norm_gain[:, None]).astype(BF16)
    if held % rows_wanted != 0:
        every = lax.all_gather(scaled, "mp", axis=0, tiled=True)
        return lax.dynamic_slice_in_dim(every, z * rows_wanted, rows_wanted, 0)
    ratio = held // rows_wanted
    piece = lax.dynamic_slice_in_dim(scaled, (z % ratio) * rows_wanted, rows_wanted, 0)
    owner = [i // ratio for i in range(count)]
    place = m ^ (z // ratio)
    value, bit, holders = piece, shards // 2, [0]
    while bit:
        pairs = [(i * shards + (owner[i] ^ h), i * shards + (owner[i] ^ h ^ bit)) for i in range(count) for h in holders]
        moved = lax.ppermute(value, ("ctx", "mp"), pairs)
        known = sum((place == h).astype(jnp.int32) for h in holders) > 0
        if bit == 1:
            return choose(jnp.where(known, 0, 1).astype(jnp.int32)[None], [value, moved])
        value = jnp.where(known, value, moved)
        holders, bit = holders + [h ^ bit for h in holders], bit // 2
    return value


def half_kernel(groups, which_ref, weight_ref, *refs):
    out_ref = refs[-1]
    half = refs[0].shape[0] // 2
    rows = pl.ds(pl.multiple_of(which_ref[0] * half, half), half)
    parts, at = [], 0
    for size in groups:
        parts.append(functools.reduce(lambda p, q: p + q, [ref[rows, :] for ref in refs[at : at + size]]))
        at += size
    block = parts[0] if len(parts) == 1 else jnp.concatenate(parts, axis=0)
    out_ref[...] = jnp.dot(block, weight_ref[...], preferred_element_type=F32).astype(out_ref.dtype)


def both_kernel(groups, which_ref, weight_ref, *refs):
    parts, (send_ref, keep_ref) = refs[:-2], refs[-2:]
    half = parts[0].shape[0] // 2
    for out_ref, which in ((send_ref, 1 - which_ref[0]), (keep_ref, which_ref[0])):
        rows = pl.ds(pl.multiple_of(which * half, half), half)
        at = 0
        for k, size in enumerate(groups):
            block = functools.reduce(lambda p, q: p + q, [ref[rows, :] for ref in parts[at : at + size]])
            at += size
            value = jnp.dot(block, weight_ref[...], preferred_element_type=F32)
            out_ref[k * half : (k + 1) * half, :] = value.astype(out_ref.dtype)


def both_parts(which, weight, blocks):
    rows = len(blocks) * (blocks[0][0].shape[0] // 2)
    flat = [part for block in blocks for part in block]
    return pl.pallas_call(
        functools.partial(both_kernel, tuple(len(block) for block in blocks)),
        in_specs=[pl.BlockSpec(memory_space=pltpu.SMEM)] + [in_vmem()] * (1 + len(flat)),
        out_specs=[in_vmem()] * 2,
        out_shape=[jax.ShapeDtypeStruct((rows, weight.shape[1]), dtype) for dtype in (BF16, F32)],
        compiler_params=SMALL,
        name="both_parts",
    )(which.astype(jnp.int32)[None], weight, *flat)


def half_part(which, weight, blocks, dtype):
    rows = len(blocks) * (blocks[0][0].shape[0] // 2)
    flat = [part for block in blocks for part in block]
    return pl.pallas_call(
        functools.partial(half_kernel, tuple(len(block) for block in blocks)),
        in_specs=[pl.BlockSpec(memory_space=pltpu.SMEM)] + [in_vmem()] * (1 + len(flat)),
        out_specs=in_vmem(),
        out_shape=jax.ShapeDtypeStruct((rows, weight.shape[1]), dtype),
        compiler_params=SMALL,
        name="half_part",
    )(which.astype(jnp.int32)[None], weight, *flat)


def project(blocks, weight, m, hurry):
    shards, count = lax.axis_size("mp"), len(blocks)
    if shards == 1:
        whole = [functools.reduce(lambda p, q: p + q, block) for block in blocks]
        return jnp.dot(jnp.concatenate(whole, axis=0), weight, preferred_element_type=F32)
    bit, value = 1, None
    while bit < shards:
        upper = (m // bit) % 2
        if value is None and not hurry:
            send, keep = both_parts(upper, weight, blocks)
        elif value is None:
            send = half_part(1 - upper, weight, blocks, BF16)
            keep = half_part(upper, weight, blocks, F32)
        else:
            half = value.shape[0] // count // 2
            pieces = value.reshape(count, 2, half, value.shape[1])
            keep = lax.dynamic_index_in_dim(pieces, upper, 1, False).reshape(count * half, value.shape[1])
            send = lax.dynamic_index_in_dim(pieces, 1 - upper, 1, False).reshape(count * half, value.shape[1])
            send = send.astype(BF16)
        got = swap(send, "mp", bit)
        value = keep + got.astype(F32)
        bit *= 2
    return value


def row_piece(m):
    shards = lax.axis_size("mp")
    piece, bit = 0, 1
    while bit < shards:
        piece = piece * 2 + (m // bit) % 2
        bit *= 2
    return piece


def body(streams, short_filter, mode_params, out_weight, norm_gain, unembed, native, mut_pos, mut_ids):
    rows, _ = streams.shape[1:]
    count, shards = lax.axis_size("ctx"), lax.axis_size("mp")
    z = lax.axis_index("ctx")
    quick = count == 4
    modes_t = jnp.swapaxes(mode_params, 1, 2)
    me = z.astype(jnp.int32)[None]
    prod, gate_stream, msg, filt, modes_t = end_part(streams, short_filter, modes_t, native)
    y, gate, start = local_part(filt, modes_t, prod, gate_stream)
    if quick:
        msgs = [msg]
        for k in range(1, count):
            msgs.append(swap(msg, "ctx", k))
        gated, nat_rows = carry_part(me, filt, modes_t, y, gate, start, msgs, False)
    else:
        every = lax.all_gather(msg, "ctx")
        gated, nat_rows = carry_part(me, filt, modes_t, y, gate, start, [every], True)
    gated, nat_rows, native, mut_pos, mut_ids, z, m, norm_gain = lax.optimization_barrier(
        (gated, nat_rows, native, mut_pos, mut_ids, z, lax.axis_index("mp"), norm_gain)
    )
    un = feature_rows(unembed, norm_gain, out_weight.shape[1], z, m)
    piece = row_piece(m)
    share = rows // shards
    nat = (nat_rows[:, :rows] * 256.0 + nat_rows[:, rows : 2 * rows]).astype(jnp.int32)
    nat_col = lax.dynamic_slice_in_dim(nat, piece * share, share, 1).reshape(count * share, 1)
    block, inner = mut_pos // rows, mut_pos % rows
    mut_row = jnp.where(inner // share == piece, block * share + inner % share, -1)[:, None]
    mut_col = mut_ids[:, None]

    if quick:
        middle = [(1, 2), (2, 1)]
        beside = swap(gated, "ctx", 1)
        mid_a = lax.ppermute(gated, "ctx", middle)
        mid_b = lax.ppermute(beside, "ctx", middle)
        far_a = swap(mid_a, "ctx", 1)
        far_b = swap(mid_b, "ctx", 1)
        mid_here = bring(gated, mid_b)
        groups = [[[gated], [beside]], [[mid_a, far_a]], [[mid_here, far_b]]]
        low = z < 2
        where = [z, z ^ 1, jnp.where(low, 2, 1), jnp.where(low, 3, 0)]
    else:
        every = lax.all_gather(gated, "ctx")
        groups = [[[every[b]]] for b in range(count)]
        where = list(range(count))
    where = jnp.stack([jnp.asarray(w, jnp.int32) for w in where + [z]])
    if quick:
        out_weight = bring(gated, out_weight)
    slots = []
    for k, blocks in enumerate(groups):
        slots.append(project(blocks, out_weight, m, k != 1))
    peers = count - 1 if quick else 0
    part, squares, scores, *msgs = logit_part(share, where, slots, un, mut_row, mut_col, nat_col, peers)
    if quick:
        for k in range(1, count):
            msgs[k - 1] = swap(msgs[k - 1], "ctx", k)
    else:
        part = lax.psum_scatter(part, "ctx", scatter_dimension=0, tiled=True)
        squares = lax.psum(squares, "ctx")
        scores = lax.psum(scores, "ctx")

    spot = jnp.stack([z, piece]).astype(jnp.int32)
    feats = norm_gain.shape[0] * shards
    span = max(rows, mut_pos.shape[0])
    result = final_part(feats, share, spot, part, squares, scores, nat_col, mut_row, msgs, span)
    pieces = [result] + [swap(result, "mp", k) for k in range(1, shards)]
    like, score = total_part(pieces, rows, mut_pos.shape[0])
    return like[0], score[0]


def solution(mesh):
    in_specs = (
        P(None, ("groups", "ctx"), "mp"),
        P(None, None, "mp"),
        P(None, "mp", None),
        P("mp", "ctx"),
        P("mp"),
        P("mp", None),
        P(("groups", "ctx")),
        P("groups"),
        P("groups"),
    )
    out_specs = (P(("groups", "ctx")), P("groups"))
    return jax.shard_map(body, mesh=mesh, in_specs=in_specs, out_specs=out_specs, check_vma=False)
```

```python
import functools

import jax
import jax.numpy as jnp
from jax import lax
from jax.experimental import pallas as pl
from jax.experimental.pallas import tpu as pltpu
from jax.sharding import PartitionSpec as P


F32 = jnp.float32
BF16 = jnp.bfloat16
LANES = 128
SUBS = 8
EPS = 1e-05


def swap(value, axis, bit):
    count = lax.axis_size(axis)
    return lax.ppermute(value, axis, [(i, i ^ bit) for i in range(count)])


def mix(taps, now, back1, back2):
    return taps[0] * now + taps[1] * back1 + taps[2] * back2


def rounded(value):
    return value.astype(BF16).astype(F32)


def taps_of(filt_ref, stream, cols):
    return [filt_ref[stream, j : j + 1, cols] for j in range(3)]


def lane_slice(tile):
    return pl.ds(pl.multiple_of(tile * LANES, LANES), LANES)


def behind(value):
    sub = lax.broadcasted_iota(jnp.int32, value.shape, 0)
    return jnp.where(sub == 0, 0.0, pltpu.roll(value, 1, 0))


def spread_modes(mode_ref, cols, modes):
    decay = [jnp.broadcast_to(mode_ref[0, m : m + 1, cols], (SUBS, LANES)) for m in range(modes)]
    return decay, [jnp.exp(-d) for d in decay]


def running(state, decay, steps):
    sub = lax.broadcasted_iota(jnp.int32, state.shape, 0)
    for reach in (1, 2, 4):
        power = jnp.exp(-decay * float(steps * reach))
        state = state + jnp.where(sub < reach, 0.0, power * pltpu.roll(state, reach, 0))
    return state


def end_kernel(
    steps, modes, x_any, filt_any, mode_any, nat_any, prod_ref, gate_ref, msg_ref, filt_ref, mode_ref,
    held, nat_ref, xs, sems, side_sems
):
    rows = steps * SUBS
    tiles = held.shape[0]
    base = 2 * modes

    def fetch(tile):
        return pltpu.make_async_copy(x_any.at[1:3, :, lane_slice(tile)], held.at[tile], sems.at[tile])

    sides = [
        pltpu.make_async_copy(src, dst, side_sems.at[k])
        for k, (src, dst) in enumerate(
            ((filt_any, filt_ref), (mode_any, mode_ref), (nat_any, nat_ref), (x_any.at[0], gate_ref))
        )
    ]
    fetch(0).start()
    for side in sides[:3]:
        side.start()

    @pl.loop(1, tiles)
    def _(tile):
        fetch(tile).start()

    sides[3].start()
    for side in sides[:3]:
        side.wait()

    @pl.loop(0, tiles)
    def _(tile):
        cols = lane_slice(tile)
        sub = lax.broadcasted_iota(jnp.int32, (SUBS, LANES), 0)
        decay, fall = spread_modes(mode_ref, cols, modes)
        taps = [taps_of(filt_ref, i, cols) for i in (1, 2)]
        fetch(tile).wait()
        for i in range(2):
            xs[i] = held[tile, i].astype(F32)

        def at(i, t):
            return xs[i, pl.ds(t, SUBS, stride=steps), :]

        back2 = [behind(at(i, steps - 2)) for i in range(2)]
        back1 = [behind(at(i, steps - 1)) for i in range(2)]
        state = [jnp.zeros((SUBS, LANES), F32) for _ in range(modes)]
        for t in range(steps):
            now = [at(i, t) for i in range(2)]
            mixed = [mix(taps[i], now[i], back1[i], back2[i]) for i in range(2)]
            back2, back1 = back1, now
            prod = rounded(mixed[0] * mixed[1])
            if t < 2:
                prod = jnp.where(sub == 0, 0.0, prod)
            prod_ref[t * SUBS : (t + 1) * SUBS, cols] = prod
            state = [f * s + prod for f, s in zip(fall, state)]
        ends = [running(state[m], decay[m], steps)[SUBS - 1 : SUBS, :] for m in range(modes)]
        end = jnp.concatenate(ends, axis=0)
        high = rounded(end)
        edge = [xs[0, 0:2, :], xs[1, 0:2, :], xs[0, rows - 2 : rows, :], xs[1, rows - 2 : rows, :]]
        msg_ref[0 : base + 8, cols] = jnp.concatenate([high, end - high] + edge, axis=0).astype(BF16)

    sides[3].wait()
    width = gate_ref.shape[1]
    ids = nat_ref[...]
    empty = jnp.zeros((1, width - 2 * rows), jnp.int32)
    ids = jnp.concatenate([ids // 256, ids % 256, empty], axis=1).astype(F32)
    head = gate_ref[0:16, :].astype(F32)
    tail = gate_ref[rows - 16 : rows, :].astype(F32)
    other = jnp.concatenate([tail[14:16, :], head[0:2, :], ids, jnp.zeros((3, width), F32)], axis=0)
    msg_ref[base + 8 : base + 16, :] = other.astype(BF16)


def local_kernel(steps, modes, filt_ref, mode_ref, prod_ref, x_ref, y_ref, gate_ref, start_ref, xs, gs):
    @pl.loop(0, x_ref.shape[1] // LANES)
    def _(tile):
        cols = lane_slice(tile)
        decay, fall = spread_modes(mode_ref, cols, modes)
        res = [jnp.broadcast_to(mode_ref[1, m : m + 1, cols], (SUBS, LANES)) for m in range(modes)]
        taps = taps_of(filt_ref, 0, cols)
        xs[...] = x_ref[:, cols].astype(F32)
        back2 = behind(xs[pl.ds(steps - 2, SUBS, stride=steps), :])
        back1 = behind(xs[pl.ds(steps - 1, SUBS, stride=steps), :])
        state = [jnp.zeros((SUBS, LANES), F32) for _ in range(modes)]
        for t in range(steps):
            now = xs[pl.ds(t, SUBS, stride=steps), :]
            gs[pl.ds(t, SUBS, stride=steps), :] = mix(taps, now, back1, back2)
            back2, back1 = back1, now
            prod = prod_ref[t * SUBS : (t + 1) * SUBS, cols]
            state = [f * s + prod for f, s in zip(fall, state)]
            y_ref[t * SUBS : (t + 1) * SUBS, cols] = functools.reduce(
                lambda p, q: p + q, [r * s for r, s in zip(res, state)]
            )
        gate_ref[:, cols] = gs[...].astype(BF16)
        for m in range(modes):
            start_ref[m * SUBS : (m + 1) * SUBS, cols] = behind(running(state[m], decay[m], steps))


SMALL = pltpu.CompilerParams(vmem_limit_bytes=16 * 2**20)


def in_vmem():
    return pl.BlockSpec(memory_space=pltpu.VMEM)


def end_part(streams, filt, modes_t, native):
    rows, width = streams.shape[1:]
    modes = modes_t.shape[1]
    steps = rows // SUBS
    tiles = width // LANES
    msg_rows = 2 * modes + 16
    return pl.pallas_call(
        functools.partial(end_kernel, steps, modes),
        in_specs=[pl.BlockSpec(memory_space=pltpu.HBM)] * 4,
        out_specs=[in_vmem()] * 5,
        out_shape=[
            pltpu.VMEM((rows, width), F32),
            pltpu.VMEM((rows, width), BF16),
            pltpu.VMEM((msg_rows, width), BF16),
            pltpu.VMEM(filt.shape, F32),
            pltpu.VMEM(modes_t.shape, F32),
        ],
        scratch_shapes=[
            pltpu.VMEM((tiles, 2, rows, LANES), BF16),
            pltpu.VMEM((1, rows), jnp.int32),
            pltpu.VMEM((2, rows, LANES), F32),
            pltpu.SemaphoreType.DMA((tiles,)),
            pltpu.SemaphoreType.DMA((4,)),
        ],
        compiler_params=SMALL,
        name="end_part",
    )(*[pltpu.with_memory_space_constraint(v, pltpu.HBM) for v in (streams, filt, modes_t, native[None, :])])


def local_part(filt, modes_t, prod, gate_stream):
    rows, width = prod.shape
    modes = modes_t.shape[1]
    return pl.pallas_call(
        functools.partial(local_kernel, rows // SUBS, modes),
        in_specs=[in_vmem()] * 4,
        out_specs=[in_vmem()] * 3,
        out_shape=[
            pltpu.VMEM((rows, width), F32),
            pltpu.VMEM((rows, width), BF16),
            pltpu.VMEM((modes * SUBS, width), F32),
        ],
        input_output_aliases={2: 0, 3: 1},
        scratch_shapes=[pltpu.VMEM((rows, LANES), F32), pltpu.VMEM((rows, LANES), F32)],
        compiler_params=SMALL,
        name="local_part",
    )(*[pltpu.with_memory_space_constraint(v, pltpu.VMEM) for v in (filt, modes_t, prod, gate_stream)])


def carry_kernel(steps, modes, stacked, count, where_ref, filt_ref, mode_ref, y_ref, gate_ref, start_ref, *rest):
    msg_refs, (out_ref, nat_ref, held, conv) = rest[:-4], rest[-4:]
    me = where_ref[0]
    rows = steps * SUBS
    base = 2 * modes

    @pl.loop(0, y_ref.shape[1] // LANES)
    def _(tile):
        cols = lane_slice(tile)
        sub = lax.broadcasted_iota(jnp.int32, (SUBS, LANES), 0)
        for k in range(count):
            if stacked:
                held[k] = msg_refs[0][k, :, cols].astype(F32)
            else:
                held[me ^ k] = msg_refs[k][:, cols].astype(F32)
        for b in range(count):
            nat_ref[b : b + 1, cols] = held[b, base + 12 : base + 13, :]
        decay = mode_ref[0, :, cols]
        taps = [taps_of(filt_ref, i, cols) for i in range(3)]

        def firsts(own, prior, keep):
            pair = []
            for i, lane in ((1, 0), (2, 2)):
                f0 = own[base + lane : base + lane + 1, :]
                f1 = own[base + lane + 1 : base + lane + 2, :]
                l2 = jnp.where(keep, prior[base + lane + 4 : base + lane + 5, :], 0.0)
                l1 = jnp.where(keep, prior[base + lane + 5 : base + lane + 6, :], 0.0)
                pair.append((mix(taps[i], f0, l1, l2), mix(taps[i], f1, f0, l1)))
            return rounded(pair[0][0] * pair[1][0]), rounded(pair[0][1] * pair[1][1])

        full = jnp.exp(-decay * float(rows))
        near0 = jnp.exp(-decay * float(rows - 1))
        near1 = jnp.exp(-decay * float(rows - 2))

        def advance(b, entering):
            own = held[b]
            p0, p1 = firsts(own, held[jnp.maximum(b - 1, 0)], b > 0)
            end = own[0:modes, :] + own[modes : 2 * modes, :] + near0 * p0 + near1 * p1
            return jnp.where(b < me, full * entering + end, entering)

        entering = jnp.zeros((modes, LANES), F32)
        if count <= 8:
            for b in range(count - 1):
                entering = advance(b, entering)
        else:
            entering = lax.fori_loop(0, count - 1, advance, entering)
        own = held[me]
        prior = held[jnp.maximum(me - 1, 0)]
        p0, p1 = firsts(own, prior, me > 0)
        later = (
            jnp.exp(-decay * float(steps)) * entering
            + jnp.exp(-decay * float(steps - 1)) * p0
            + jnp.exp(-decay * float(steps - 2)) * p1
        )
        shift = float(steps) * jnp.maximum(sub - 1, 0).astype(F32)
        fall, res, flow = [], [], []
        for m in range(modes):
            d = jnp.broadcast_to(decay[m : m + 1, :], (SUBS, LANES))
            r = jnp.broadcast_to(mode_ref[1, m : m + 1, cols], (SUBS, LANES))
            fall.append(jnp.exp(-d))
            res.append(r)
            begin = jnp.where(sub == 0, entering[m : m + 1, :], jnp.exp(-d * shift) * later[m : m + 1, :])
            flow.append(r * (start_ref[m * SUBS : (m + 1) * SUBS, cols] + begin))
        inject = (p0, p1)
        for t in range(steps):
            flow = [f * v for f, v in zip(fall, flow)]
            if t < 2:
                extra = jnp.where(sub == 0, inject[t], 0.0)
                flow = [v + r * extra for v, r in zip(flow, res)]
            conv[pl.ds(t, SUBS, stride=steps), :] = functools.reduce(
                lambda p, q: p + q, flow, y_ref[t * SUBS : (t + 1) * SUBS, cols]
            )
        g0 = own[base + 10 : base + 11, :]
        g1 = own[base + 11 : base + 12, :]
        l2 = jnp.where(me > 0, prior[base + 8 : base + 9, :], 0.0)
        l1 = jnp.where(me > 0, prior[base + 9 : base + 10, :], 0.0)
        head0 = mix(taps[0], g0, l1, l2)
        head1 = mix(taps[0], g1, g0, l1)
        gate = gate_ref[:, cols].astype(F32)
        line = lax.broadcasted_iota(jnp.int32, (16, LANES), 0)
        head = jnp.where(line == 0, rounded(head0), jnp.where(line == 1, rounded(head1), gate[0:16, :]))
        out_ref[0:16, cols] = (head * rounded(conv[0:16, :])).astype(BF16)
        out_ref[16:rows, cols] = (gate[16:rows, :] * rounded(conv[16:rows, :])).astype(BF16)


def carry_part(me, filt, modes_t, y, gate, start, msgs, stacked):
    rows, width = y.shape
    modes = modes_t.shape[1]
    steps = rows // SUBS
    count = msgs[0].shape[0] if stacked else len(msgs)
    msg_rows = msgs[0].shape[-2]
    return pl.pallas_call(
        functools.partial(carry_kernel, steps, modes, stacked, count),
        in_specs=[pl.BlockSpec(memory_space=pltpu.SMEM)] + [in_vmem()] * (5 + len(msgs)),
        out_specs=[in_vmem()] * 2,
        out_shape=[jax.ShapeDtypeStruct((rows, width), BF16), jax.ShapeDtypeStruct((count, width), F32)],
        scratch_shapes=[pltpu.VMEM((count, msg_rows, LANES), F32), pltpu.VMEM((rows, LANES), F32)],
        compiler_params=SMALL,
        cost_estimate=pl.CostEstimate(flops=rows * width * 32, bytes_accessed=rows * width * 8, transcendentals=0),
        name="carry_part",
    )(me, *[pltpu.with_memory_space_constraint(v, pltpu.VMEM) for v in (filt, modes_t, y, gate, start, *msgs)])


def bring_kernel(later_any, src_any, out_ref, sem):
    copy = pltpu.make_async_copy(src_any, out_ref, sem)
    copy.start()
    copy.wait()


def bring(later, weight):
    return pl.pallas_call(
        bring_kernel,
        in_specs=[pl.BlockSpec(memory_space=pl.ANY), pl.BlockSpec(memory_space=pltpu.HBM)],
        out_specs=in_vmem(),
        out_shape=pltpu.VMEM(weight.shape, weight.dtype),
        scratch_shapes=[pltpu.SemaphoreType.DMA],
        compiler_params=SMALL,
        name="bring",
    )(later, pltpu.with_memory_space_constraint(weight, pltpu.HBM))


def as_row(col, width):
    rows = col.shape[0]
    r = lax.broadcasted_iota(jnp.int32, (rows, width), 0)
    c = lax.broadcasted_iota(jnp.int32, (rows, width), 1)
    return jnp.sum(jnp.where(r == c, col, 0.0), axis=0, keepdims=True)


def two_rows(row, width):
    high = rounded(row)
    both = jnp.concatenate([high, row - high], axis=0)
    return jnp.concatenate([both, jnp.zeros((2, width - row.shape[1]), F32)], axis=1)


def partial_logits(values, un_ref, rows, id_ref, native_ids):
    total, muts = values.shape[0], rows.shape[0]
    square = jnp.sum(values * values, axis=1, keepdims=True)
    part = jnp.dot(values.astype(BF16), un_ref[...], preferred_element_type=F32)
    high = part.astype(BF16)
    low = (part - high.astype(F32)).astype(BF16)
    words = lax.broadcasted_iota(jnp.int32, part.shape, 1)
    both = high.astype(F32) + low.astype(F32)
    native = as_row(jnp.sum(jnp.where(words == native_ids, both, 0.0), axis=1, keepdims=True), total)
    hit = lax.broadcasted_iota(jnp.int32, (muts, total), 1) == rows
    onehot = hit.astype(BF16)
    picked = jnp.dot(onehot, high, preferred_element_type=F32) + jnp.dot(onehot, low, preferred_element_type=F32)
    words = lax.broadcasted_iota(jnp.int32, (muts, part.shape[1]), 1)
    chosen = jnp.sum(jnp.where(words == id_ref[...], picked, 0.0), axis=1, keepdims=True)
    base = jnp.sum(jnp.where(hit, native, 0.0), axis=1, keepdims=True)
    return part, square, as_row(chosen - base, muts)


def logit_kernel(share, count, where_ref, row_ref, id_ref, nat_ref, *rest):
    sources, slot_refs = rest[:count], rest[count:-6]
    part_ref, square_ref, score_ref, un_ref, acc, sem = rest[-6:]
    for k, source in enumerate(sources):

        @pl.when(where_ref[where_ref.shape[0] - 1] == k)
        def _():
            pltpu.make_async_copy(source, un_ref, sem).start()

    if sum(ref.shape[0] for ref in slot_refs) < acc.shape[0]:
        acc[...] = jnp.zeros_like(acc)
    at = 0
    for slot_ref in slot_refs:
        for k in range(slot_ref.shape[0] // share):
            acc[pl.ds(pl.multiple_of(where_ref[at] * share, share), share), :] = slot_ref[k * share : (k + 1) * share, :]
            at += 1
    for k, source in enumerate(sources):

        @pl.when(where_ref[where_ref.shape[0] - 1] == k)
        def _():
            pltpu.make_async_copy(source, un_ref, sem).wait()

    part, square, score = partial_logits(acc[...], un_ref, row_ref[...], id_ref, nat_ref[...])
    part_ref[...] = part
    square_ref[...] = as_row(square, square.shape[0])
    score_ref[...] = score


def logit_part(share, where, slots, sources, mut_row, mut_id, nat_col):
    wide, (_, vocab) = slots[0].shape[1], sources[0].shape
    total, muts = nat_col.shape[0], mut_row.shape[0]
    return pl.pallas_call(
        functools.partial(logit_kernel, share, len(sources)),
        in_specs=[pl.BlockSpec(memory_space=pltpu.SMEM)]
        + [in_vmem()] * 3
        + [pl.BlockSpec(memory_space=pl.ANY)] * len(sources)
        + [in_vmem()] * len(slots),
        out_specs=[in_vmem()] * 4,
        out_shape=[
            jax.ShapeDtypeStruct((total, vocab), F32),
            jax.ShapeDtypeStruct((1, total), F32),
            jax.ShapeDtypeStruct((1, muts), F32),
            pltpu.VMEM(sources[0].shape, BF16),
        ],
        scratch_shapes=[pltpu.VMEM((total, wide), F32), pltpu.SemaphoreType.DMA],
        compiler_params=SMALL,
        name="logit_part",
    )(where, mut_row, mut_id, nat_col, *sources, *slots)


def message_kernel(share, peers, where_ref, un_ref, row_ref, id_ref, nat_ref, last_ref, part_ref, square_in, score_in, *rest):
    square_ref, score_ref, msg_refs = rest[0], rest[1], rest[2:]
    slots = where_ref.shape[0] - 2
    spot, me = where_ref[slots - 1], where_ref[slots]
    first = pl.multiple_of(spot * share, share)
    native_ids = nat_ref[pl.ds(first, share), :]
    part, square, score = partial_logits(last_ref[...], un_ref, row_ref[...] - first, id_ref, native_ids)
    total, vocab = square_in.shape[1], part.shape[1]
    r = lax.broadcasted_iota(jnp.int32, (share, total), 0)
    c = lax.broadcasted_iota(jnp.int32, (share, total), 1)
    square = square_in[...] + jnp.sum(jnp.where(c == r + first, square, 0.0), axis=0, keepdims=True)
    score = score_in[...] + score
    square_ref[...] = square
    score_ref[...] = score
    extra = jnp.concatenate(
        [two_rows(square, vocab), two_rows(score, vocab), jnp.zeros((4, vocab), F32)], axis=0
    ).astype(BF16)
    for k in range(1, peers + 1):
        their = part_ref[pl.ds(pl.multiple_of((me ^ k) * share, share), share), :]
        msg_refs[k - 1][0:share, :] = jnp.where((me ^ k) == spot, part, their).astype(BF16)
        msg_refs[k - 1][share : share + 8, :] = extra


def message_part(share, where, last, un, mut_row, mut_id, nat_col, part, squares, scores, peers):
    vocab = un.shape[1]
    return pl.pallas_call(
        functools.partial(message_kernel, share, peers),
        in_specs=[pl.BlockSpec(memory_space=pltpu.SMEM)] + [in_vmem()] * 8,
        out_specs=[in_vmem()] * (2 + peers),
        out_shape=[jax.ShapeDtypeStruct(squares.shape, F32), jax.ShapeDtypeStruct(scores.shape, F32)]
        + [jax.ShapeDtypeStruct((share + 8, vocab), BF16)] * peers,
        compiler_params=SMALL,
        name="message_part",
    )(where, un, mut_row, mut_id, nat_col, last, part, squares, scores)


def final_kernel(feats, share, where_ref, log_ref, square_ref, score_ref, nat_ref, row_ref, *rest):
    msg_refs, out_ref = rest[:-1], rest[-1]
    me, piece = where_ref[0], where_ref[1]
    vocab = log_ref.shape[1]
    total = square_ref.shape[1]
    muts = score_ref.shape[1]
    width = out_ref.shape[1]
    if msg_refs:
        logits = log_ref[pl.ds(pl.multiple_of(me * share, share), share), :]
    else:
        logits = log_ref[...]
    square, score = square_ref[...], score_ref[...]
    for msg_ref in msg_refs:
        logits = logits + msg_ref[0:share, :].astype(F32)
        extra = msg_ref[share : share + 8, :].astype(F32)
        square = square + (extra[0:1, 0:total] + extra[1:2, 0:total])
        score = score + (extra[2:3, 0:muts] + extra[3:4, 0:muts])
    scale_row = lax.rsqrt(square / feats + EPS)
    r = lax.broadcasted_iota(jnp.int32, (share, total), 0)
    c = lax.broadcasted_iota(jnp.int32, (share, total), 1)
    scale = jnp.sum(jnp.where(c == r + me * share, scale_row, 0.0), axis=1, keepdims=True)
    logits = logits * scale
    top = jnp.max(logits, axis=1, keepdims=True)
    norm = top + jnp.log(jnp.sum(jnp.exp(logits - top), axis=1, keepdims=True))
    words = lax.broadcasted_iota(jnp.int32, (share, vocab), 1)
    native = nat_ref[pl.ds(pl.multiple_of(me * share, share), share), :]
    like = jnp.sum(jnp.where(words == native, logits, 0.0), axis=1, keepdims=True) - norm
    r = lax.broadcasted_iota(jnp.int32, (share, width), 0)
    c = lax.broadcasted_iota(jnp.int32, (share, width), 1)
    out_ref[0:1, :] = jnp.sum(jnp.where(c == r + piece * share, like, 0.0), axis=0, keepdims=True)
    r = lax.broadcasted_iota(jnp.int32, (muts, total), 0)
    c = lax.broadcasted_iota(jnp.int32, (muts, total), 1)
    at_mut = jnp.sum(jnp.where(c == row_ref[...], scale_row, 0.0), axis=1, keepdims=True)
    out_ref[1:2, 0:muts] = score * as_row(at_mut, muts)


def final_part(feats, share, where, logits, squares, scores, nat, mut_row, msgs, width):
    whole = pl.BlockSpec(memory_space=pltpu.VMEM)
    return pl.pallas_call(
        functools.partial(final_kernel, float(feats), share),
        in_specs=[pl.BlockSpec(memory_space=pltpu.SMEM)] + [whole] * (5 + len(msgs)),
        out_specs=whole,
        out_shape=jax.ShapeDtypeStruct((2, width), F32),
        compiler_params=SMALL,
        name="final_part",
    )(where, logits, squares, scores, nat, mut_row, *msgs)


def total_kernel(*refs):
    like_ref, score_ref = refs[-2:]
    total = functools.reduce(lambda p, q: p + q, [ref[...] for ref in refs[:-2]])
    like_ref[...] = total[0:1, 0 : like_ref.shape[1]]
    score_ref[...] = total[1:2, 0 : score_ref.shape[1]]


def total_part(pieces, rows, muts):
    whole = pl.BlockSpec(memory_space=pltpu.VMEM)
    return pl.pallas_call(
        total_kernel,
        in_specs=[whole] * len(pieces),
        out_specs=[whole] * 2,
        out_shape=[jax.ShapeDtypeStruct((1, rows), F32), jax.ShapeDtypeStruct((1, muts), F32)],
        compiler_params=SMALL,
        name="total_part",
    )(*pieces)


def feature_rows(unembed, norm_gain, rows_wanted, z, m):
    count, shards = lax.axis_size("ctx"), lax.axis_size("mp")
    held = unembed.shape[0]
    scaled = (unembed.astype(F32) * norm_gain[:, None]).astype(BF16)
    if held % rows_wanted != 0:
        every = lax.all_gather(scaled, "mp", axis=0, tiled=True)
        return [lax.dynamic_slice_in_dim(every, z * rows_wanted, rows_wanted, 0)], 0
    ratio = held // rows_wanted
    piece = lax.dynamic_slice_in_dim(scaled, (z % ratio) * rows_wanted, rows_wanted, 0)
    owner = [i // ratio for i in range(count)]
    place = m ^ (z // ratio)
    value, bit, holders = piece, shards // 2, [0]
    while bit:
        pairs = [(i * shards + (owner[i] ^ h), i * shards + (owner[i] ^ h ^ bit)) for i in range(count) for h in holders]
        moved = lax.ppermute(value, ("ctx", "mp"), pairs)
        known = sum((place == h).astype(jnp.int32) for h in holders) > 0
        if bit == 1:
            return [value, moved], jnp.where(known, 0, 1)
        value = jnp.where(known, value, moved)
        holders, bit = holders + [h ^ bit for h in holders], bit // 2
    return [value], 0


def half_kernel(groups, which_ref, weight_ref, *refs):
    out_ref = refs[-1]
    half = refs[0].shape[0] // 2
    rows = pl.ds(pl.multiple_of(which_ref[0] * half, half), half)
    parts, at = [], 0
    for size in groups:
        parts.append(functools.reduce(lambda p, q: p + q, [ref[rows, :] for ref in refs[at : at + size]]))
        at += size
    block = parts[0] if len(parts) == 1 else jnp.concatenate(parts, axis=0)
    out_ref[...] = jnp.dot(block, weight_ref[...], preferred_element_type=F32).astype(out_ref.dtype)


def both_kernel(groups, which_ref, weight_ref, *refs):
    parts, (send_ref, keep_ref) = refs[:-2], refs[-2:]
    half = parts[0].shape[0] // 2
    for out_ref, which in ((send_ref, 1 - which_ref[0]), (keep_ref, which_ref[0])):
        rows = pl.ds(pl.multiple_of(which * half, half), half)
        at = 0
        for k, size in enumerate(groups):
            block = functools.reduce(lambda p, q: p + q, [ref[rows, :] for ref in parts[at : at + size]])
            at += size
            value = jnp.dot(block, weight_ref[...], preferred_element_type=F32)
            out_ref[k * half : (k + 1) * half, :] = value.astype(out_ref.dtype)


def both_parts(which, weight, blocks):
    rows = len(blocks) * (blocks[0][0].shape[0] // 2)
    flat = [part for block in blocks for part in block]
    return pl.pallas_call(
        functools.partial(both_kernel, tuple(len(block) for block in blocks)),
        in_specs=[pl.BlockSpec(memory_space=pltpu.SMEM)] + [in_vmem()] * (1 + len(flat)),
        out_specs=[in_vmem()] * 2,
        out_shape=[jax.ShapeDtypeStruct((rows, weight.shape[1]), dtype) for dtype in (BF16, F32)],
        compiler_params=SMALL,
        name="both_parts",
    )(which.astype(jnp.int32)[None], weight, *flat)


def half_part(which, weight, blocks, dtype):
    rows = len(blocks) * (blocks[0][0].shape[0] // 2)
    flat = [part for block in blocks for part in block]
    return pl.pallas_call(
        functools.partial(half_kernel, tuple(len(block) for block in blocks)),
        in_specs=[pl.BlockSpec(memory_space=pltpu.SMEM)] + [in_vmem()] * (1 + len(flat)),
        out_specs=in_vmem(),
        out_shape=jax.ShapeDtypeStruct((rows, weight.shape[1]), dtype),
        compiler_params=SMALL,
        name="half_part",
    )(which.astype(jnp.int32)[None], weight, *flat)


def project(blocks, weight, m, hurry):
    shards, count = lax.axis_size("mp"), len(blocks)
    if shards == 1:
        whole = [functools.reduce(lambda p, q: p + q, block) for block in blocks]
        return jnp.dot(jnp.concatenate(whole, axis=0), weight, preferred_element_type=F32)
    bit, value = 1, None
    while bit < shards:
        upper = (m // bit) % 2
        if value is None and not hurry:
            send, keep = both_parts(upper, weight, blocks)
        elif value is None:
            send = half_part(1 - upper, weight, blocks, BF16)
            keep = half_part(upper, weight, blocks, F32)
        else:
            half = value.shape[0] // count // 2
            pieces = value.reshape(count, 2, half, value.shape[1])
            keep = lax.dynamic_index_in_dim(pieces, upper, 1, False).reshape(count * half, value.shape[1])
            send = lax.dynamic_index_in_dim(pieces, 1 - upper, 1, False).reshape(count * half, value.shape[1])
            send = send.astype(BF16)
        got = swap(send, "mp", bit)
        value = keep + got.astype(F32)
        bit *= 2
    return value


def row_piece(m):
    shards = lax.axis_size("mp")
    piece, bit = 0, 1
    while bit < shards:
        piece = piece * 2 + (m // bit) % 2
        bit *= 2
    return piece


def body(streams, short_filter, mode_params, out_weight, norm_gain, unembed, native, mut_pos, mut_ids):
    rows, _ = streams.shape[1:]
    count, shards = lax.axis_size("ctx"), lax.axis_size("mp")
    z = lax.axis_index("ctx")
    quick = count == 4
    modes_t = jnp.swapaxes(mode_params, 1, 2)
    me = z.astype(jnp.int32)[None]
    prod, gate_stream, msg, filt, modes_t = end_part(streams, short_filter, modes_t, native)
    y, gate, start = local_part(filt, modes_t, prod, gate_stream)
    if quick:
        msgs = [msg]
        for k in range(1, count):
            msgs.append(swap(msg, "ctx", k))
        gated, nat_rows = carry_part(me, filt, modes_t, y, gate, start, msgs, False)
    else:
        every = lax.all_gather(msg, "ctx")
        gated, nat_rows = carry_part(me, filt, modes_t, y, gate, start, [every], True)
    gated, nat_rows, native, mut_pos, mut_ids, z, m, norm_gain = lax.optimization_barrier(
        (gated, nat_rows, native, mut_pos, mut_ids, z, lax.axis_index("mp"), norm_gain)
    )
    sources, chosen = feature_rows(unembed, norm_gain, out_weight.shape[1], z, m)
    piece = row_piece(m)
    share = rows // shards
    nat = (nat_rows[:, :rows] * 256.0 + nat_rows[:, rows : 2 * rows]).astype(jnp.int32)
    nat_col = lax.dynamic_slice_in_dim(nat, piece * share, share, 1).reshape(count * share, 1)
    block, inner = mut_pos // rows, mut_pos % rows
    mut_row = jnp.where(inner // share == piece, block * share + inner % share, -1)[:, None]
    mut_col = mut_ids[:, None]

    if quick:
        middle = [(1, 2), (2, 1)]
        beside = swap(gated, "ctx", 1)
        mid_a = lax.ppermute(gated, "ctx", middle)
        mid_b = lax.ppermute(beside, "ctx", middle)
        far_a = swap(mid_a, "ctx", 1)
        far_b = swap(mid_b, "ctx", 1)
        mid_here = bring(gated, mid_b)
        groups = [[[gated], [beside]], [[mid_a, far_a]], [[mid_here, far_b]]]
        low = z < 2
        where = [z, z ^ 1, jnp.where(low, 2, 1), jnp.where(low, 3, 0)]
    else:
        every = lax.all_gather(gated, "ctx")
        groups = [[[every[b]]] for b in range(count)]
        where = list(range(count))
    where = jnp.stack([jnp.asarray(w, jnp.int32) for w in where + [z, chosen]])
    if quick:
        out_weight = bring(gated, out_weight)
    slots = []
    for k, blocks in enumerate(groups):
        slots.append(project(blocks, out_weight, m, k != 1))
    early = slots[:-1] if quick else slots
    part, squares, scores, un = logit_part(share, where, early, sources, mut_row, mut_col, nat_col)
    msgs = []
    if quick:
        squares, scores, *msgs = message_part(
            share, where, slots[-1], un, mut_row, mut_col, nat_col, part, squares, scores, count - 1
        )
    if quick:
        for k in range(1, count):
            msgs[k - 1] = swap(msgs[k - 1], "ctx", k)
    else:
        part = lax.psum_scatter(part, "ctx", scatter_dimension=0, tiled=True)
        squares = lax.psum(squares, "ctx")
        scores = lax.psum(scores, "ctx")

    spot = jnp.stack([z, piece]).astype(jnp.int32)
    feats = norm_gain.shape[0] * shards
    span = max(rows, mut_pos.shape[0])
    result = final_part(feats, share, spot, part, squares, scores, nat_col, mut_row, msgs, span)
    pieces = [result] + [swap(result, "mp", k) for k in range(1, shards)]
    like, score = total_part(pieces, rows, mut_pos.shape[0])
    return like[0], score[0]


def solution(mesh):
    in_specs = (
        P(None, ("groups", "ctx"), "mp"),
        P(None, None, "mp"),
        P(None, "mp", None),
        P("mp", "ctx"),
        P("mp"),
        P("mp", None),
        P(("groups", "ctx")),
        P("groups"),
        P("groups"),
    )
    out_specs = (P(("groups", "ctx")), P("groups"))
    return jax.shard_map(body, mesh=mesh, in_specs=in_specs, out_specs=out_specs, check_vma=False)
```

```python
import functools

import jax
import jax.numpy as jnp
from jax import lax
from jax.experimental import pallas as pl
from jax.experimental.pallas import tpu as pltpu
from jax.sharding import PartitionSpec as P


F32 = jnp.float32
BF16 = jnp.bfloat16
LANES = 128
SUBS = 8
EPS = 1e-05


def swap(value, axis, bit):
    count = lax.axis_size(axis)
    return lax.ppermute(value, axis, [(i, i ^ bit) for i in range(count)])


def mix(taps, now, back1, back2):
    return taps[0] * now + taps[1] * back1 + taps[2] * back2


def rounded(value):
    return value.astype(BF16).astype(F32)


def taps_of(filt_ref, stream, cols):
    return [filt_ref[stream, j : j + 1, cols] for j in range(3)]


def lane_slice(tile):
    return pl.ds(pl.multiple_of(tile * LANES, LANES), LANES)


def behind(value):
    sub = lax.broadcasted_iota(jnp.int32, value.shape, 0)
    return jnp.where(sub == 0, 0.0, pltpu.roll(value, 1, 0))


def spread_modes(mode_ref, cols, modes):
    decay = [jnp.broadcast_to(mode_ref[0, m : m + 1, cols], (SUBS, LANES)) for m in range(modes)]
    return decay, [jnp.exp(-d) for d in decay]


def running(state, decay, steps):
    sub = lax.broadcasted_iota(jnp.int32, state.shape, 0)
    for reach in (1, 2, 4):
        power = jnp.exp(-decay * float(steps * reach))
        state = state + jnp.where(sub < reach, 0.0, power * pltpu.roll(state, reach, 0))
    return state


def end_kernel(
    steps, modes, x_any, filt_any, mode_any, nat_any, prod_ref, gate_ref, msg_ref, filt_ref, mode_ref,
    held, nat_ref, xs, sems, side_sems
):
    rows = steps * SUBS
    tiles = held.shape[0]
    base = 2 * modes

    def fetch(tile):
        return pltpu.make_async_copy(x_any.at[1:3, :, lane_slice(tile)], held.at[tile], sems.at[tile])

    sides = [
        pltpu.make_async_copy(src, dst, side_sems.at[k])
        for k, (src, dst) in enumerate(
            ((filt_any, filt_ref), (mode_any, mode_ref), (nat_any, nat_ref), (x_any.at[0], gate_ref))
        )
    ]
    fetch(0).start()
    for side in sides[:3]:
        side.start()

    @pl.loop(1, tiles)
    def _(tile):
        fetch(tile).start()

    sides[3].start()
    for side in sides[:3]:
        side.wait()

    @pl.loop(0, tiles)
    def _(tile):
        cols = lane_slice(tile)
        sub = lax.broadcasted_iota(jnp.int32, (SUBS, LANES), 0)
        decay, fall = spread_modes(mode_ref, cols, modes)
        taps = [taps_of(filt_ref, i, cols) for i in (1, 2)]
        fetch(tile).wait()
        for i in range(2):
            xs[i] = held[tile, i].astype(F32)

        def at(i, t):
            return xs[i, pl.ds(t, SUBS, stride=steps), :]

        back2 = [behind(at(i, steps - 2)) for i in range(2)]
        back1 = [behind(at(i, steps - 1)) for i in range(2)]
        state = [jnp.zeros((SUBS, LANES), F32) for _ in range(modes)]
        for t in range(steps):
            now = [at(i, t) for i in range(2)]
            mixed = [mix(taps[i], now[i], back1[i], back2[i]) for i in range(2)]
            back2, back1 = back1, now
            prod = rounded(mixed[0] * mixed[1])
            if t < 2:
                prod = jnp.where(sub == 0, 0.0, prod)
            prod_ref[t * SUBS : (t + 1) * SUBS, cols] = prod
            state = [f * s + prod for f, s in zip(fall, state)]
        ends = [running(state[m], decay[m], steps)[SUBS - 1 : SUBS, :] for m in range(modes)]
        end = jnp.concatenate(ends, axis=0)
        high = rounded(end)
        edge = [xs[0, 0:2, :], xs[1, 0:2, :], xs[0, rows - 2 : rows, :], xs[1, rows - 2 : rows, :]]
        msg_ref[0 : base + 8, cols] = jnp.concatenate([high, end - high] + edge, axis=0).astype(BF16)

    sides[3].wait()
    width = gate_ref.shape[1]
    ids = nat_ref[...]
    empty = jnp.zeros((1, width - 2 * rows), jnp.int32)
    ids = jnp.concatenate([ids // 256, ids % 256, empty], axis=1).astype(F32)
    head = gate_ref[0:16, :].astype(F32)
    tail = gate_ref[rows - 16 : rows, :].astype(F32)
    other = jnp.concatenate([tail[14:16, :], head[0:2, :], ids, jnp.zeros((3, width), F32)], axis=0)
    msg_ref[base + 8 : base + 16, :] = other.astype(BF16)


def local_kernel(steps, modes, filt_ref, mode_ref, prod_ref, x_ref, y_ref, gate_ref, start_ref, xs, gs):
    @pl.loop(0, x_ref.shape[1] // LANES)
    def _(tile):
        cols = lane_slice(tile)
        decay, fall = spread_modes(mode_ref, cols, modes)
        res = [jnp.broadcast_to(mode_ref[1, m : m + 1, cols], (SUBS, LANES)) for m in range(modes)]
        taps = taps_of(filt_ref, 0, cols)
        xs[...] = x_ref[:, cols].astype(F32)
        back2 = behind(xs[pl.ds(steps - 2, SUBS, stride=steps), :])
        back1 = behind(xs[pl.ds(steps - 1, SUBS, stride=steps), :])
        state = [jnp.zeros((SUBS, LANES), F32) for _ in range(modes)]
        for t in range(steps):
            now = xs[pl.ds(t, SUBS, stride=steps), :]
            gs[pl.ds(t, SUBS, stride=steps), :] = mix(taps, now, back1, back2)
            back2, back1 = back1, now
            prod = prod_ref[t * SUBS : (t + 1) * SUBS, cols]
            state = [f * s + prod for f, s in zip(fall, state)]
            y_ref[t * SUBS : (t + 1) * SUBS, cols] = functools.reduce(
                lambda p, q: p + q, [r * s for r, s in zip(res, state)]
            )
        gate_ref[:, cols] = gs[...].astype(BF16)
        for m in range(modes):
            start_ref[m * SUBS : (m + 1) * SUBS, cols] = behind(running(state[m], decay[m], steps))


SMALL = pltpu.CompilerParams(vmem_limit_bytes=16 * 2**20)


def in_vmem():
    return pl.BlockSpec(memory_space=pltpu.VMEM)


def end_part(streams, filt, modes_t, native):
    rows, width = streams.shape[1:]
    modes = modes_t.shape[1]
    steps = rows // SUBS
    tiles = width // LANES
    msg_rows = 2 * modes + 16
    return pl.pallas_call(
        functools.partial(end_kernel, steps, modes),
        in_specs=[pl.BlockSpec(memory_space=pltpu.HBM)] * 4,
        out_specs=[in_vmem()] * 5,
        out_shape=[
            pltpu.VMEM((rows, width), F32),
            pltpu.VMEM((rows, width), BF16),
            pltpu.VMEM((msg_rows, width), BF16),
            pltpu.VMEM(filt.shape, F32),
            pltpu.VMEM(modes_t.shape, F32),
        ],
        scratch_shapes=[
            pltpu.VMEM((tiles, 2, rows, LANES), BF16),
            pltpu.VMEM((1, rows), jnp.int32),
            pltpu.VMEM((2, rows, LANES), F32),
            pltpu.SemaphoreType.DMA((tiles,)),
            pltpu.SemaphoreType.DMA((4,)),
        ],
        compiler_params=SMALL,
        name="end_part",
    )(*[pltpu.with_memory_space_constraint(v, pltpu.HBM) for v in (streams, filt, modes_t, native[None, :])])


def local_part(filt, modes_t, prod, gate_stream):
    rows, width = prod.shape
    modes = modes_t.shape[1]
    return pl.pallas_call(
        functools.partial(local_kernel, rows // SUBS, modes),
        in_specs=[in_vmem()] * 4,
        out_specs=[in_vmem()] * 3,
        out_shape=[
            pltpu.VMEM((rows, width), F32),
            pltpu.VMEM((rows, width), BF16),
            pltpu.VMEM((modes * SUBS, width), F32),
        ],
        input_output_aliases={2: 0, 3: 1},
        scratch_shapes=[pltpu.VMEM((rows, LANES), F32), pltpu.VMEM((rows, LANES), F32)],
        compiler_params=SMALL,
        name="local_part",
    )(*[pltpu.with_memory_space_constraint(v, pltpu.VMEM) for v in (filt, modes_t, prod, gate_stream)])


def carry_kernel(steps, modes, stacked, count, where_ref, filt_ref, mode_ref, y_ref, gate_ref, start_ref, *rest):
    msg_refs, (out_ref, nat_ref, held, conv) = rest[:-4], rest[-4:]
    me = where_ref[0]
    rows = steps * SUBS
    base = 2 * modes

    @pl.loop(0, y_ref.shape[1] // LANES)
    def _(tile):
        cols = lane_slice(tile)
        sub = lax.broadcasted_iota(jnp.int32, (SUBS, LANES), 0)
        for k in range(count):
            if stacked:
                held[k] = msg_refs[0][k, :, cols].astype(F32)
            else:
                held[me ^ k] = msg_refs[k][:, cols].astype(F32)
        for b in range(count):
            nat_ref[b : b + 1, cols] = held[b, base + 12 : base + 13, :]
        decay = mode_ref[0, :, cols]
        taps = [taps_of(filt_ref, i, cols) for i in range(3)]

        def firsts(own, prior, keep):
            pair = []
            for i, lane in ((1, 0), (2, 2)):
                f0 = own[base + lane : base + lane + 1, :]
                f1 = own[base + lane + 1 : base + lane + 2, :]
                l2 = jnp.where(keep, prior[base + lane + 4 : base + lane + 5, :], 0.0)
                l1 = jnp.where(keep, prior[base + lane + 5 : base + lane + 6, :], 0.0)
                pair.append((mix(taps[i], f0, l1, l2), mix(taps[i], f1, f0, l1)))
            return rounded(pair[0][0] * pair[1][0]), rounded(pair[0][1] * pair[1][1])

        full = jnp.exp(-decay * float(rows))
        near0 = jnp.exp(-decay * float(rows - 1))
        near1 = jnp.exp(-decay * float(rows - 2))

        def advance(b, entering):
            own = held[b]
            p0, p1 = firsts(own, held[jnp.maximum(b - 1, 0)], b > 0)
            end = own[0:modes, :] + own[modes : 2 * modes, :] + near0 * p0 + near1 * p1
            return jnp.where(b < me, full * entering + end, entering)

        entering = jnp.zeros((modes, LANES), F32)
        if count <= 8:
            for b in range(count - 1):
                entering = advance(b, entering)
        else:
            entering = lax.fori_loop(0, count - 1, advance, entering)
        own = held[me]
        prior = held[jnp.maximum(me - 1, 0)]
        p0, p1 = firsts(own, prior, me > 0)
        later = (
            jnp.exp(-decay * float(steps)) * entering
            + jnp.exp(-decay * float(steps - 1)) * p0
            + jnp.exp(-decay * float(steps - 2)) * p1
        )
        shift = float(steps) * jnp.maximum(sub - 1, 0).astype(F32)
        fall, res, flow = [], [], []
        for m in range(modes):
            d = jnp.broadcast_to(decay[m : m + 1, :], (SUBS, LANES))
            r = jnp.broadcast_to(mode_ref[1, m : m + 1, cols], (SUBS, LANES))
            fall.append(jnp.exp(-d))
            res.append(r)
            begin = jnp.where(sub == 0, entering[m : m + 1, :], jnp.exp(-d * shift) * later[m : m + 1, :])
            flow.append(r * (start_ref[m * SUBS : (m + 1) * SUBS, cols] + begin))
        inject = (p0, p1)
        for t in range(steps):
            flow = [f * v for f, v in zip(fall, flow)]
            if t < 2:
                extra = jnp.where(sub == 0, inject[t], 0.0)
                flow = [v + r * extra for v, r in zip(flow, res)]
            conv[pl.ds(t, SUBS, stride=steps), :] = functools.reduce(
                lambda p, q: p + q, flow, y_ref[t * SUBS : (t + 1) * SUBS, cols]
            )
        g0 = own[base + 10 : base + 11, :]
        g1 = own[base + 11 : base + 12, :]
        l2 = jnp.where(me > 0, prior[base + 8 : base + 9, :], 0.0)
        l1 = jnp.where(me > 0, prior[base + 9 : base + 10, :], 0.0)
        head0 = mix(taps[0], g0, l1, l2)
        head1 = mix(taps[0], g1, g0, l1)
        gate = gate_ref[:, cols].astype(F32)
        line = lax.broadcasted_iota(jnp.int32, (16, LANES), 0)
        head = jnp.where(line == 0, rounded(head0), jnp.where(line == 1, rounded(head1), gate[0:16, :]))
        out_ref[0:16, cols] = (head * rounded(conv[0:16, :])).astype(BF16)
        out_ref[16:rows, cols] = (gate[16:rows, :] * rounded(conv[16:rows, :])).astype(BF16)


def carry_part(me, filt, modes_t, y, gate, start, msgs, stacked):
    rows, width = y.shape
    modes = modes_t.shape[1]
    steps = rows // SUBS
    count = msgs[0].shape[0] if stacked else len(msgs)
    msg_rows = msgs[0].shape[-2]
    return pl.pallas_call(
        functools.partial(carry_kernel, steps, modes, stacked, count),
        in_specs=[pl.BlockSpec(memory_space=pltpu.SMEM)] + [in_vmem()] * (5 + len(msgs)),
        out_specs=[in_vmem()] * 2,
        out_shape=[jax.ShapeDtypeStruct((rows, width), BF16), jax.ShapeDtypeStruct((count, width), F32)],
        scratch_shapes=[pltpu.VMEM((count, msg_rows, LANES), F32), pltpu.VMEM((rows, LANES), F32)],
        compiler_params=SMALL,
        cost_estimate=pl.CostEstimate(flops=rows * width * 32, bytes_accessed=rows * width * 8, transcendentals=0),
        name="carry_part",
    )(me, *[pltpu.with_memory_space_constraint(v, pltpu.VMEM) for v in (filt, modes_t, y, gate, start, *msgs)])


def bring_kernel(later_any, src_any, out_ref, sem):
    copy = pltpu.make_async_copy(src_any, out_ref, sem)
    copy.start()
    copy.wait()


def bring(later, weight):
    return pl.pallas_call(
        bring_kernel,
        in_specs=[pl.BlockSpec(memory_space=pl.ANY), pl.BlockSpec(memory_space=pltpu.HBM)],
        out_specs=in_vmem(),
        out_shape=pltpu.VMEM(weight.shape, weight.dtype),
        scratch_shapes=[pltpu.SemaphoreType.DMA],
        compiler_params=SMALL,
        name="bring",
    )(later, pltpu.with_memory_space_constraint(weight, pltpu.HBM))


def as_row(col, width):
    rows = col.shape[0]
    r = lax.broadcasted_iota(jnp.int32, (rows, width), 0)
    c = lax.broadcasted_iota(jnp.int32, (rows, width), 1)
    return jnp.sum(jnp.where(r == c, col, 0.0), axis=0, keepdims=True)


def two_rows(row, width):
    high = rounded(row)
    both = jnp.concatenate([high, row - high], axis=0)
    return jnp.concatenate([both, jnp.zeros((2, width - row.shape[1]), F32)], axis=1)


def partial_logits(values, un_ref, rows, id_ref, native_ids):
    total, muts = values.shape[0], rows.shape[0]
    square = jnp.sum(values * values, axis=1, keepdims=True)
    part = jnp.dot(values.astype(BF16), un_ref[...], preferred_element_type=F32)
    high = part.astype(BF16)
    low = (part - high.astype(F32)).astype(BF16)
    words = lax.broadcasted_iota(jnp.int32, part.shape, 1)
    both = high.astype(F32) + low.astype(F32)
    native = as_row(jnp.sum(jnp.where(words == native_ids, both, 0.0), axis=1, keepdims=True), total)
    hit = lax.broadcasted_iota(jnp.int32, (muts, total), 1) == rows
    onehot = hit.astype(BF16)
    picked = jnp.dot(onehot, high, preferred_element_type=F32) + jnp.dot(onehot, low, preferred_element_type=F32)
    words = lax.broadcasted_iota(jnp.int32, (muts, part.shape[1]), 1)
    chosen = jnp.sum(jnp.where(words == id_ref[...], picked, 0.0), axis=1, keepdims=True)
    base = jnp.sum(jnp.where(hit, native, 0.0), axis=1, keepdims=True)
    return part, square, as_row(chosen - base, muts)


def logit_kernel(share, count, where_ref, row_ref, id_ref, nat_ref, *rest):
    sources, slot_refs = rest[:count], rest[count:-6]
    part_ref, square_ref, score_ref, un_ref, acc, sem = rest[-6:]
    for k, source in enumerate(sources):

        @pl.when(where_ref[where_ref.shape[0] - 1] == k)
        def _():
            pltpu.make_async_copy(source, un_ref, sem).start()

    if sum(ref.shape[0] for ref in slot_refs) < acc.shape[0]:
        acc[...] = jnp.zeros_like(acc)
    at = 0
    for slot_ref in slot_refs:
        for k in range(slot_ref.shape[0] // share):
            acc[pl.ds(pl.multiple_of(where_ref[at] * share, share), share), :] = slot_ref[k * share : (k + 1) * share, :]
            at += 1
    for k, source in enumerate(sources):

        @pl.when(where_ref[where_ref.shape[0] - 1] == k)
        def _():
            pltpu.make_async_copy(source, un_ref, sem).wait()

    part, square, score = partial_logits(acc[...], un_ref, row_ref[...], id_ref, nat_ref[...])
    part_ref[...] = part
    square_ref[...] = as_row(square, square.shape[0])
    score_ref[...] = score


def logit_part(share, where, slots, sources, mut_row, mut_id, nat_col):
    wide, (_, vocab) = slots[0].shape[1], sources[0].shape
    total, muts = nat_col.shape[0], mut_row.shape[0]
    return pl.pallas_call(
        functools.partial(logit_kernel, share, len(sources)),
        in_specs=[pl.BlockSpec(memory_space=pltpu.SMEM)]
        + [in_vmem()] * 3
        + [pl.BlockSpec(memory_space=pl.ANY)] * len(sources)
        + [in_vmem()] * len(slots),
        out_specs=[in_vmem()] * 4,
        out_shape=[
            jax.ShapeDtypeStruct((total, vocab), F32),
            jax.ShapeDtypeStruct((1, total), F32),
            jax.ShapeDtypeStruct((1, muts), F32),
            pltpu.VMEM(sources[0].shape, BF16),
        ],
        scratch_shapes=[pltpu.VMEM((total, wide), F32), pltpu.SemaphoreType.DMA],
        compiler_params=SMALL,
        name="logit_part",
    )(where, mut_row, mut_id, nat_col, *sources, *slots)


def message_kernel(share, peers, where_ref, un_ref, row_ref, id_ref, nat_ref, last_ref, part_ref, square_in, score_in, *rest):
    square_ref, score_ref, msg_refs = rest[0], rest[1], rest[2:]
    slots = where_ref.shape[0] - 2
    spot, me = where_ref[slots - 1], where_ref[slots]
    first = pl.multiple_of(spot * share, share)
    native_ids = nat_ref[pl.ds(first, share), :]
    part, square, score = partial_logits(last_ref[...], un_ref, row_ref[...] - first, id_ref, native_ids)
    total, vocab = square_in.shape[1], part.shape[1]
    r = lax.broadcasted_iota(jnp.int32, (share, total), 0)
    c = lax.broadcasted_iota(jnp.int32, (share, total), 1)
    square = square_in[...] + jnp.sum(jnp.where(c == r + first, square, 0.0), axis=0, keepdims=True)
    score = score_in[...] + score
    square_ref[...] = square
    score_ref[...] = score
    extra = jnp.concatenate(
        [two_rows(square, vocab), two_rows(score, vocab), jnp.zeros((4, vocab), F32)], axis=0
    ).astype(BF16)
    for k in range(1, peers + 1):
        their = part_ref[pl.ds(pl.multiple_of((me ^ k) * share, share), share), :]
        msg_refs[k - 1][0:share, :] = jnp.where((me ^ k) == spot, part, their).astype(BF16)
        msg_refs[k - 1][share : share + 8, :] = extra


def message_part(share, where, last, un, mut_row, mut_id, nat_col, part, squares, scores, peers):
    vocab = un.shape[1]
    return pl.pallas_call(
        functools.partial(message_kernel, share, peers),
        in_specs=[pl.BlockSpec(memory_space=pltpu.SMEM)] + [in_vmem()] * 8,
        out_specs=[in_vmem()] * (2 + peers),
        out_shape=[jax.ShapeDtypeStruct(squares.shape, F32), jax.ShapeDtypeStruct(scores.shape, F32)]
        + [jax.ShapeDtypeStruct((share + 8, vocab), BF16)] * peers,
        compiler_params=SMALL,
        name="message_part",
    )(where, un, mut_row, mut_id, nat_col, last, part, squares, scores)


def final_kernel(feats, share, where_ref, log_ref, square_ref, score_ref, nat_ref, row_ref, *rest):
    msg_refs, out_ref = rest[:-1], rest[-1]
    me, piece = where_ref[0], where_ref[1]
    vocab = log_ref.shape[1]
    total = square_ref.shape[1]
    muts = score_ref.shape[1]
    width = out_ref.shape[1]
    if msg_refs:
        logits = log_ref[pl.ds(pl.multiple_of(me * share, share), share), :]
    else:
        logits = log_ref[...]
    square, score = square_ref[...], score_ref[...]
    for msg_ref in msg_refs:
        logits = logits + msg_ref[0:share, :].astype(F32)
        extra = msg_ref[share : share + 8, :].astype(F32)
        square = square + (extra[0:1, 0:total] + extra[1:2, 0:total])
        score = score + (extra[2:3, 0:muts] + extra[3:4, 0:muts])
    scale_row = lax.rsqrt(square / feats + EPS)
    r = lax.broadcasted_iota(jnp.int32, (share, total), 0)
    c = lax.broadcasted_iota(jnp.int32, (share, total), 1)
    scale = jnp.sum(jnp.where(c == r + me * share, scale_row, 0.0), axis=1, keepdims=True)
    logits = logits * scale
    top = jnp.max(logits, axis=1, keepdims=True)
    norm = top + jnp.log(jnp.sum(jnp.exp(logits - top), axis=1, keepdims=True))
    words = lax.broadcasted_iota(jnp.int32, (share, vocab), 1)
    native = nat_ref[pl.ds(pl.multiple_of(me * share, share), share), :]
    like = jnp.sum(jnp.where(words == native, logits, 0.0), axis=1, keepdims=True) - norm
    r = lax.broadcasted_iota(jnp.int32, (share, width), 0)
    c = lax.broadcasted_iota(jnp.int32, (share, width), 1)
    out_ref[0:1, :] = jnp.sum(jnp.where(c == r + piece * share, like, 0.0), axis=0, keepdims=True)
    r = lax.broadcasted_iota(jnp.int32, (muts, total), 0)
    c = lax.broadcasted_iota(jnp.int32, (muts, total), 1)
    at_mut = jnp.sum(jnp.where(c == row_ref[...], scale_row, 0.0), axis=1, keepdims=True)
    out_ref[1:2, 0:muts] = score * as_row(at_mut, muts)


def final_part(feats, share, where, logits, squares, scores, nat, mut_row, msgs, width):
    whole = pl.BlockSpec(memory_space=pltpu.VMEM)
    return pl.pallas_call(
        functools.partial(final_kernel, float(feats), share),
        in_specs=[pl.BlockSpec(memory_space=pltpu.SMEM)] + [whole] * (5 + len(msgs)),
        out_specs=whole,
        out_shape=jax.ShapeDtypeStruct((2, width), F32),
        compiler_params=SMALL,
        name="final_part",
    )(where, logits, squares, scores, nat, mut_row, *msgs)


def total_kernel(*refs):
    like_ref, score_ref = refs[-2:]
    total = functools.reduce(lambda p, q: p + q, [ref[...] for ref in refs[:-2]])
    like_ref[...] = total[0:1, 0 : like_ref.shape[1]]
    score_ref[...] = total[1:2, 0 : score_ref.shape[1]]


def total_part(pieces, rows, muts):
    whole = pl.BlockSpec(memory_space=pltpu.VMEM)
    return pl.pallas_call(
        total_kernel,
        in_specs=[whole] * len(pieces),
        out_specs=[whole] * 2,
        out_shape=[jax.ShapeDtypeStruct((1, rows), F32), jax.ShapeDtypeStruct((1, muts), F32)],
        compiler_params=SMALL,
        name="total_part",
    )(*pieces)


def feature_rows(unembed, norm_gain, rows_wanted, z, m):
    count, shards = lax.axis_size("ctx"), lax.axis_size("mp")
    held = unembed.shape[0]
    scaled = (unembed.astype(F32) * norm_gain[:, None]).astype(BF16)
    if held % rows_wanted != 0:
        every = lax.all_gather(scaled, "mp", axis=0, tiled=True)
        return [lax.dynamic_slice_in_dim(every, z * rows_wanted, rows_wanted, 0)], 0
    ratio = held // rows_wanted
    piece = lax.dynamic_slice_in_dim(scaled, (z % ratio) * rows_wanted, rows_wanted, 0)
    owner = [i // ratio for i in range(count)]
    place = m ^ (z // ratio)
    copies = [piece]
    for k in range(1, shards):
        pairs = [(i * shards + owner[i], i * shards + (owner[i] ^ k)) for i in range(count)]
        copies.append(lax.ppermute(piece, ("ctx", "mp"), pairs))
    return copies, place


def half_kernel(groups, which_ref, weight_ref, *refs):
    out_ref = refs[-1]
    half = refs[0].shape[0] // 2
    rows = pl.ds(pl.multiple_of(which_ref[0] * half, half), half)
    parts, at = [], 0
    for size in groups:
        parts.append(functools.reduce(lambda p, q: p + q, [ref[rows, :] for ref in refs[at : at + size]]))
        at += size
    block = parts[0] if len(parts) == 1 else jnp.concatenate(parts, axis=0)
    out_ref[...] = jnp.dot(block, weight_ref[...], preferred_element_type=F32).astype(out_ref.dtype)


def both_kernel(groups, which_ref, weight_ref, *refs):
    parts, (send_ref, keep_ref) = refs[:-2], refs[-2:]
    half = parts[0].shape[0] // 2
    for out_ref, which in ((send_ref, 1 - which_ref[0]), (keep_ref, which_ref[0])):
        rows = pl.ds(pl.multiple_of(which * half, half), half)
        at = 0
        for k, size in enumerate(groups):
            block = functools.reduce(lambda p, q: p + q, [ref[rows, :] for ref in parts[at : at + size]])
            at += size
            value = jnp.dot(block, weight_ref[...], preferred_element_type=F32)
            out_ref[k * half : (k + 1) * half, :] = value.astype(out_ref.dtype)


def both_parts(which, weight, blocks):
    rows = len(blocks) * (blocks[0][0].shape[0] // 2)
    flat = [part for block in blocks for part in block]
    return pl.pallas_call(
        functools.partial(both_kernel, tuple(len(block) for block in blocks)),
        in_specs=[pl.BlockSpec(memory_space=pltpu.SMEM)] + [in_vmem()] * (1 + len(flat)),
        out_specs=[in_vmem()] * 2,
        out_shape=[jax.ShapeDtypeStruct((rows, weight.shape[1]), dtype) for dtype in (BF16, BF16)],
        compiler_params=SMALL,
        name="both_parts",
    )(which.astype(jnp.int32)[None], weight, *flat)


def fetch_kernel(which_ref, weight_ref, *refs):
    count = (len(refs) - 2) // 2
    terms, out_ref, held, sems = refs[:count], refs[count], refs[count + 1 : -1], refs[-1]
    half = out_ref.shape[0]
    rows = pl.ds(pl.multiple_of(which_ref[0] * half, half), half)
    copies = [pltpu.make_async_copy(term.at[rows, :], here, sems.at[k]) for k, (term, here) in enumerate(zip(terms, held))]
    for copy in copies:
        copy.start()
    for copy in copies:
        copy.wait()
    block = functools.reduce(lambda p, q: p + q, [here[...] for here in held])
    out_ref[...] = jnp.dot(block, weight_ref[...], preferred_element_type=F32).astype(out_ref.dtype)


def fetch_half(which, weight, terms, dtype):
    half, width = terms[0].shape[0] // 2, terms[0].shape[1]
    return pl.pallas_call(
        fetch_kernel,
        in_specs=[pl.BlockSpec(memory_space=pltpu.SMEM), in_vmem()] + [pl.BlockSpec(memory_space=pl.ANY)] * len(terms),
        out_specs=in_vmem(),
        out_shape=jax.ShapeDtypeStruct((half, weight.shape[1]), dtype),
        scratch_shapes=[pltpu.VMEM((half, width), BF16)] * len(terms) + [pltpu.SemaphoreType.DMA((len(terms),))],
        compiler_params=SMALL,
        name="fetch_half",
    )(which.astype(jnp.int32)[None], weight, *terms)


def half_part(which, weight, blocks, dtype):
    rows = len(blocks) * (blocks[0][0].shape[0] // 2)
    flat = [part for block in blocks for part in block]
    return pl.pallas_call(
        functools.partial(half_kernel, tuple(len(block) for block in blocks)),
        in_specs=[pl.BlockSpec(memory_space=pltpu.SMEM)] + [in_vmem()] * (1 + len(flat)),
        out_specs=in_vmem(),
        out_shape=jax.ShapeDtypeStruct((rows, weight.shape[1]), dtype),
        compiler_params=SMALL,
        name="half_part",
    )(which.astype(jnp.int32)[None], weight, *flat)


def project(blocks, weight, m, hurry, last):
    shards, count = lax.axis_size("mp"), len(blocks)
    if shards == 1:
        whole = [functools.reduce(lambda p, q: p + q, block) for block in blocks]
        return jnp.dot(jnp.concatenate(whole, axis=0), weight, preferred_element_type=F32)
    bit, value = 1, None
    while bit < shards:
        upper = (m // bit) % 2
        if value is None and not hurry:
            send, keep = both_parts(upper, weight, blocks)
        elif value is None:
            one = len(blocks) == 1
            send = fetch_half(1 - upper, weight, blocks[0], BF16) if one else half_part(1 - upper, weight, blocks, BF16)
            keep = fetch_half(upper, weight, blocks[0], F32) if one else half_part(upper, weight, blocks, F32 if last else BF16)
        else:
            half = value.shape[0] // count // 2
            pieces = value.reshape(count, 2, half, value.shape[1])
            keep = lax.dynamic_index_in_dim(pieces, upper, 1, False).reshape(count * half, value.shape[1])
            send = lax.dynamic_index_in_dim(pieces, 1 - upper, 1, False).reshape(count * half, value.shape[1])
            send = send.astype(BF16)
        got = swap(send, "mp", bit)
        value = keep.astype(F32) + got.astype(F32)
        value = value if last or 2 * bit >= shards else value.astype(BF16)
        bit *= 2
    return value


def row_piece(m):
    shards = lax.axis_size("mp")
    piece, bit = 0, 1
    while bit < shards:
        piece = piece * 2 + (m // bit) % 2
        bit *= 2
    return piece


def body(streams, short_filter, mode_params, out_weight, norm_gain, unembed, native, mut_pos, mut_ids):
    rows, _ = streams.shape[1:]
    count, shards = lax.axis_size("ctx"), lax.axis_size("mp")
    z = lax.axis_index("ctx")
    quick = count == 4
    modes_t = jnp.swapaxes(mode_params, 1, 2)
    me = z.astype(jnp.int32)[None]
    prod, gate_stream, msg, filt, modes_t = end_part(streams, short_filter, modes_t, native)
    y, gate, start = local_part(filt, modes_t, prod, gate_stream)
    if quick:
        msgs = [msg]
        for k in range(1, count):
            msgs.append(swap(msg, "ctx", k))
        gated, nat_rows = carry_part(me, filt, modes_t, y, gate, start, msgs, False)
    else:
        every = lax.all_gather(msg, "ctx")
        gated, nat_rows = carry_part(me, filt, modes_t, y, gate, start, [every], True)
    gated, nat_rows, native, mut_pos, mut_ids, z, m, norm_gain = lax.optimization_barrier(
        (gated, nat_rows, native, mut_pos, mut_ids, z, lax.axis_index("mp"), norm_gain)
    )
    sources, chosen = feature_rows(unembed, norm_gain, out_weight.shape[1], z, m)
    piece = row_piece(m)
    share = rows // shards
    nat = (nat_rows[:, :rows] * 256.0 + nat_rows[:, rows : 2 * rows]).astype(jnp.int32)
    nat_col = lax.dynamic_slice_in_dim(nat, piece * share, share, 1).reshape(count * share, 1)
    block, inner = mut_pos // rows, mut_pos % rows
    mut_row = jnp.where(inner // share == piece, block * share + inner % share, -1)[:, None]
    mut_col = mut_ids[:, None]

    if quick:
        middle = [(1, 2), (2, 1)]
        beside = swap(gated, "ctx", 1)
        mid_a = lax.ppermute(gated, "ctx", middle)
        mid_b = lax.ppermute(beside, "ctx", middle)
        far_a = swap(mid_a, "ctx", 1)
        far_b = swap(mid_b, "ctx", 1)
        groups = [[[gated], [beside]], [[mid_a, far_a]], [[mid_b, far_b]]]
        low = z < 2
        where = [z, z ^ 1, jnp.where(low, 2, 1), jnp.where(low, 3, 0)]
    else:
        every = lax.all_gather(gated, "ctx")
        groups = [[[every[b]]] for b in range(count)]
        where = list(range(count))
    where = jnp.stack([jnp.asarray(w, jnp.int32) for w in where + [z, chosen]])
    if quick:
        out_weight = bring(gated, out_weight)
    slots = []
    for k, blocks in enumerate(groups):
        slots.append(project(blocks, out_weight, m, k != 1, k == len(groups) - 1))
    early = slots[:-1] if quick else slots
    part, squares, scores, un = logit_part(share, where, early, sources, mut_row, mut_col, nat_col)
    msgs = []
    if quick:
        squares, scores, *msgs = message_part(
            share, where, slots[-1], un, mut_row, mut_col, nat_col, part, squares, scores, count - 1
        )
    if quick:
        for k in range(1, count):
            msgs[k - 1] = swap(msgs[k - 1], "ctx", k)
    else:
        part = lax.psum_scatter(part, "ctx", scatter_dimension=0, tiled=True)
        squares = lax.psum(squares, "ctx")
        scores = lax.psum(scores, "ctx")

    spot = jnp.stack([z, piece]).astype(jnp.int32)
    feats = norm_gain.shape[0] * shards
    span = max(rows, mut_pos.shape[0])
    result = final_part(feats, share, spot, part, squares, scores, nat_col, mut_row, msgs, span)
    pieces = [result] + [swap(result, "mp", k) for k in range(1, shards)]
    like, score = total_part(pieces, rows, mut_pos.shape[0])
    return like[0], score[0]


def solution(mesh):
    in_specs = (
        P(None, ("groups", "ctx"), "mp"),
        P(None, None, "mp"),
        P(None, "mp", None),
        P("mp", "ctx"),
        P("mp"),
        P("mp", None),
        P(("groups", "ctx")),
        P("groups"),
        P("groups"),
    )
    out_specs = (P(("groups", "ctx")), P("groups"))
    return jax.shard_map(body, mesh=mesh, in_specs=in_specs, out_specs=out_specs, check_vma=False)
```

```python
import functools

import jax
import jax.numpy as jnp
from jax import lax
from jax.experimental import pallas as pl
from jax.experimental.pallas import tpu as pltpu
from jax.sharding import PartitionSpec as P


F32 = jnp.float32
BF16 = jnp.bfloat16
LANES = 128
SUBS = 8
EPS = 1e-05


def swap(value, axis, bit):
    count = lax.axis_size(axis)
    return lax.ppermute(value, axis, [(i, i ^ bit) for i in range(count)])


def mix(taps, now, back1, back2):
    return taps[0] * now + taps[1] * back1 + taps[2] * back2


def rounded(value):
    return value.astype(BF16).astype(F32)


def taps_of(filt_ref, stream, cols):
    return [filt_ref[stream, j : j + 1, cols] for j in range(3)]


def lane_slice(tile):
    return pl.ds(pl.multiple_of(tile * LANES, LANES), LANES)


def behind(value):
    sub = lax.broadcasted_iota(jnp.int32, value.shape, 0)
    return jnp.where(sub == 0, 0.0, pltpu.roll(value, 1, 0))


def spread_modes(mode_ref, cols, modes):
    decay = [jnp.broadcast_to(mode_ref[0, m : m + 1, cols], (SUBS, LANES)) for m in range(modes)]
    return decay, [jnp.exp(-d) for d in decay]


def running(state, decay, steps):
    sub = lax.broadcasted_iota(jnp.int32, state.shape, 0)
    for reach in (1, 2, 4):
        power = jnp.exp(-decay * float(steps * reach))
        state = state + jnp.where(sub < reach, 0.0, power * pltpu.roll(state, reach, 0))
    return state


def end_kernel(
    steps, modes, x_any, filt_any, mode_any, nat_any, prod_ref, gate_ref, msg_ref, filt_ref, mode_ref,
    held, nat_ref, xs, sems, side_sems
):
    rows = steps * SUBS
    tiles = held.shape[0]
    base = 2 * modes

    def fetch(tile):
        return pltpu.make_async_copy(x_any.at[1:3, :, lane_slice(tile)], held.at[tile], sems.at[tile])

    sides = [
        pltpu.make_async_copy(src, dst, side_sems.at[k])
        for k, (src, dst) in enumerate(
            ((filt_any, filt_ref), (mode_any, mode_ref), (nat_any, nat_ref), (x_any.at[0], gate_ref))
        )
    ]
    fetch(0).start()
    for side in sides[:3]:
        side.start()

    @pl.loop(1, tiles)
    def _(tile):
        fetch(tile).start()

    sides[3].start()
    for side in sides[:3]:
        side.wait()

    @pl.loop(0, tiles)
    def _(tile):
        cols = lane_slice(tile)
        sub = lax.broadcasted_iota(jnp.int32, (SUBS, LANES), 0)
        decay, fall = spread_modes(mode_ref, cols, modes)
        taps = [taps_of(filt_ref, i, cols) for i in (1, 2)]
        fetch(tile).wait()
        for i in range(2):
            xs[i] = held[tile, i].astype(F32)

        def at(i, t):
            return xs[i, pl.ds(t, SUBS, stride=steps), :]

        back2 = [behind(at(i, steps - 2)) for i in range(2)]
        back1 = [behind(at(i, steps - 1)) for i in range(2)]
        state = [jnp.zeros((SUBS, LANES), F32) for _ in range(modes)]
        for t in range(steps):
            now = [at(i, t) for i in range(2)]
            mixed = [mix(taps[i], now[i], back1[i], back2[i]) for i in range(2)]
            back2, back1 = back1, now
            prod = rounded(mixed[0] * mixed[1])
            if t < 2:
                prod = jnp.where(sub == 0, 0.0, prod)
            prod_ref[t * SUBS : (t + 1) * SUBS, cols] = prod
            state = [f * s + prod for f, s in zip(fall, state)]
        ends = [running(state[m], decay[m], steps)[SUBS - 1 : SUBS, :] for m in range(modes)]
        end = jnp.concatenate(ends, axis=0)
        high = rounded(end)
        edge = [xs[0, 0:2, :], xs[1, 0:2, :], xs[0, rows - 2 : rows, :], xs[1, rows - 2 : rows, :]]
        msg_ref[0 : base + 8, cols] = jnp.concatenate([high, end - high] + edge, axis=0).astype(BF16)

    sides[3].wait()
    width = gate_ref.shape[1]
    ids = nat_ref[...]
    empty = jnp.zeros((1, width - 2 * rows), jnp.int32)
    ids = jnp.concatenate([ids // 256, ids % 256, empty], axis=1).astype(F32)
    head = gate_ref[0:16, :].astype(F32)
    tail = gate_ref[rows - 16 : rows, :].astype(F32)
    other = jnp.concatenate([tail[14:16, :], head[0:2, :], ids, jnp.zeros((3, width), F32)], axis=0)
    msg_ref[base + 8 : base + 16, :] = other.astype(BF16)


def local_kernel(steps, modes, filt_ref, mode_ref, prod_ref, x_ref, y_ref, gate_ref, start_ref, xs, gs):
    @pl.loop(0, x_ref.shape[1] // LANES)
    def _(tile):
        cols = lane_slice(tile)
        decay, fall = spread_modes(mode_ref, cols, modes)
        res = [jnp.broadcast_to(mode_ref[1, m : m + 1, cols], (SUBS, LANES)) for m in range(modes)]
        taps = taps_of(filt_ref, 0, cols)
        xs[...] = x_ref[:, cols].astype(F32)
        back2 = behind(xs[pl.ds(steps - 2, SUBS, stride=steps), :])
        back1 = behind(xs[pl.ds(steps - 1, SUBS, stride=steps), :])
        state = [jnp.zeros((SUBS, LANES), F32) for _ in range(modes)]
        for t in range(steps):
            now = xs[pl.ds(t, SUBS, stride=steps), :]
            gs[pl.ds(t, SUBS, stride=steps), :] = mix(taps, now, back1, back2)
            back2, back1 = back1, now
            prod = prod_ref[t * SUBS : (t + 1) * SUBS, cols]
            state = [f * s + prod for f, s in zip(fall, state)]
            y_ref[t * SUBS : (t + 1) * SUBS, cols] = functools.reduce(
                lambda p, q: p + q, [r * s for r, s in zip(res, state)]
            )
        gate_ref[:, cols] = gs[...].astype(BF16)
        for m in range(modes):
            start_ref[m * SUBS : (m + 1) * SUBS, cols] = behind(running(state[m], decay[m], steps))


SMALL = pltpu.CompilerParams(vmem_limit_bytes=16 * 2**20)


def in_vmem():
    return pl.BlockSpec(memory_space=pltpu.VMEM)


def end_part(streams, filt, modes_t, native):
    rows, width = streams.shape[1:]
    modes = modes_t.shape[1]
    steps = rows // SUBS
    tiles = width // LANES
    msg_rows = 2 * modes + 16
    return pl.pallas_call(
        functools.partial(end_kernel, steps, modes),
        in_specs=[pl.BlockSpec(memory_space=pltpu.HBM)] * 4,
        out_specs=[in_vmem()] * 5,
        out_shape=[
            pltpu.VMEM((rows, width), F32),
            pltpu.VMEM((rows, width), BF16),
            pltpu.VMEM((msg_rows, width), BF16),
            pltpu.VMEM(filt.shape, F32),
            pltpu.VMEM(modes_t.shape, F32),
        ],
        scratch_shapes=[
            pltpu.VMEM((tiles, 2, rows, LANES), BF16),
            pltpu.VMEM((1, rows), jnp.int32),
            pltpu.VMEM((2, rows, LANES), F32),
            pltpu.SemaphoreType.DMA((tiles,)),
            pltpu.SemaphoreType.DMA((4,)),
        ],
        compiler_params=SMALL,
        name="end_part",
    )(*[pltpu.with_memory_space_constraint(v, pltpu.HBM) for v in (streams, filt, modes_t, native[None, :])])


def local_part(filt, modes_t, prod, gate_stream):
    rows, width = prod.shape
    modes = modes_t.shape[1]
    return pl.pallas_call(
        functools.partial(local_kernel, rows // SUBS, modes),
        in_specs=[in_vmem()] * 4,
        out_specs=[in_vmem()] * 3,
        out_shape=[
            pltpu.VMEM((rows, width), F32),
            pltpu.VMEM((rows, width), BF16),
            pltpu.VMEM((modes * SUBS, width), F32),
        ],
        input_output_aliases={2: 0, 3: 1},
        scratch_shapes=[pltpu.VMEM((rows, LANES), F32), pltpu.VMEM((rows, LANES), F32)],
        compiler_params=SMALL,
        name="local_part",
    )(*[pltpu.with_memory_space_constraint(v, pltpu.VMEM) for v in (filt, modes_t, prod, gate_stream)])


def carry_kernel(steps, modes, stacked, count, where_ref, filt_ref, mode_ref, y_ref, gate_ref, start_ref, *rest):
    msg_refs, (out_ref, nat_ref, held, conv) = rest[:-4], rest[-4:]
    me = where_ref[0]
    rows = steps * SUBS
    base = 2 * modes

    @pl.loop(0, y_ref.shape[1] // LANES)
    def _(tile):
        cols = lane_slice(tile)
        sub = lax.broadcasted_iota(jnp.int32, (SUBS, LANES), 0)
        for k in range(count):
            if stacked:
                held[k] = msg_refs[0][k, :, cols].astype(F32)
            else:
                held[me ^ k] = msg_refs[k][:, cols].astype(F32)
        for b in range(count):
            nat_ref[b : b + 1, cols] = held[b, base + 12 : base + 13, :]
        decay = mode_ref[0, :, cols]
        taps = [taps_of(filt_ref, i, cols) for i in range(3)]

        def firsts(own, prior, keep):
            pair = []
            for i, lane in ((1, 0), (2, 2)):
                f0 = own[base + lane : base + lane + 1, :]
                f1 = own[base + lane + 1 : base + lane + 2, :]
                l2 = jnp.where(keep, prior[base + lane + 4 : base + lane + 5, :], 0.0)
                l1 = jnp.where(keep, prior[base + lane + 5 : base + lane + 6, :], 0.0)
                pair.append((mix(taps[i], f0, l1, l2), mix(taps[i], f1, f0, l1)))
            return rounded(pair[0][0] * pair[1][0]), rounded(pair[0][1] * pair[1][1])

        full = jnp.exp(-decay * float(rows))
        near0 = jnp.exp(-decay * float(rows - 1))
        near1 = jnp.exp(-decay * float(rows - 2))

        def advance(b, entering):
            own = held[b]
            p0, p1 = firsts(own, held[jnp.maximum(b - 1, 0)], b > 0)
            end = own[0:modes, :] + own[modes : 2 * modes, :] + near0 * p0 + near1 * p1
            return jnp.where(b < me, full * entering + end, entering)

        entering = jnp.zeros((modes, LANES), F32)
        if count <= 8:
            for b in range(count - 1):
                entering = advance(b, entering)
        else:
            entering = lax.fori_loop(0, count - 1, advance, entering)
        own = held[me]
        prior = held[jnp.maximum(me - 1, 0)]
        p0, p1 = firsts(own, prior, me > 0)
        later = (
            jnp.exp(-decay * float(steps)) * entering
            + jnp.exp(-decay * float(steps - 1)) * p0
            + jnp.exp(-decay * float(steps - 2)) * p1
        )
        shift = float(steps) * jnp.maximum(sub - 1, 0).astype(F32)
        fall, res, flow = [], [], []
        for m in range(modes):
            d = jnp.broadcast_to(decay[m : m + 1, :], (SUBS, LANES))
            r = jnp.broadcast_to(mode_ref[1, m : m + 1, cols], (SUBS, LANES))
            fall.append(jnp.exp(-d))
            res.append(r)
            begin = jnp.where(sub == 0, entering[m : m + 1, :], jnp.exp(-d * shift) * later[m : m + 1, :])
            flow.append(r * (start_ref[m * SUBS : (m + 1) * SUBS, cols] + begin))
        inject = (p0, p1)
        for t in range(steps):
            flow = [f * v for f, v in zip(fall, flow)]
            if t < 2:
                extra = jnp.where(sub == 0, inject[t], 0.0)
                flow = [v + r * extra for v, r in zip(flow, res)]
            conv[pl.ds(t, SUBS, stride=steps), :] = functools.reduce(
                lambda p, q: p + q, flow, y_ref[t * SUBS : (t + 1) * SUBS, cols]
            )
        g0 = own[base + 10 : base + 11, :]
        g1 = own[base + 11 : base + 12, :]
        l2 = jnp.where(me > 0, prior[base + 8 : base + 9, :], 0.0)
        l1 = jnp.where(me > 0, prior[base + 9 : base + 10, :], 0.0)
        head0 = mix(taps[0], g0, l1, l2)
        head1 = mix(taps[0], g1, g0, l1)
        gate = gate_ref[:, cols].astype(F32)
        line = lax.broadcasted_iota(jnp.int32, (16, LANES), 0)
        head = jnp.where(line == 0, rounded(head0), jnp.where(line == 1, rounded(head1), gate[0:16, :]))
        out_ref[0:16, cols] = (head * rounded(conv[0:16, :])).astype(BF16)
        out_ref[16:rows, cols] = (gate[16:rows, :] * rounded(conv[16:rows, :])).astype(BF16)


def carry_part(me, filt, modes_t, y, gate, start, msgs, stacked):
    rows, width = y.shape
    modes = modes_t.shape[1]
    steps = rows // SUBS
    count = msgs[0].shape[0] if stacked else len(msgs)
    msg_rows = msgs[0].shape[-2]
    return pl.pallas_call(
        functools.partial(carry_kernel, steps, modes, stacked, count),
        in_specs=[pl.BlockSpec(memory_space=pltpu.SMEM)] + [in_vmem()] * (5 + len(msgs)),
        out_specs=[in_vmem()] * 2,
        out_shape=[jax.ShapeDtypeStruct((rows, width), BF16), jax.ShapeDtypeStruct((count, width), F32)],
        scratch_shapes=[pltpu.VMEM((count, msg_rows, LANES), F32), pltpu.VMEM((rows, LANES), F32)],
        compiler_params=SMALL,
        cost_estimate=pl.CostEstimate(flops=rows * width * 32, bytes_accessed=rows * width * 8, transcendentals=0),
        name="carry_part",
    )(me, *[pltpu.with_memory_space_constraint(v, pltpu.VMEM) for v in (filt, modes_t, y, gate, start, *msgs)])


def bring_kernel(later_any, src_any, out_ref, sem):
    copy = pltpu.make_async_copy(src_any, out_ref, sem)
    copy.start()
    copy.wait()


def bring(later, weight):
    return pl.pallas_call(
        bring_kernel,
        in_specs=[pl.BlockSpec(memory_space=pl.ANY), pl.BlockSpec(memory_space=pltpu.HBM)],
        out_specs=in_vmem(),
        out_shape=pltpu.VMEM(weight.shape, weight.dtype),
        scratch_shapes=[pltpu.SemaphoreType.DMA],
        compiler_params=SMALL,
        name="bring",
    )(later, pltpu.with_memory_space_constraint(weight, pltpu.HBM))


def as_row(col, width):
    rows = col.shape[0]
    r = lax.broadcasted_iota(jnp.int32, (rows, width), 0)
    c = lax.broadcasted_iota(jnp.int32, (rows, width), 1)
    return jnp.sum(jnp.where(r == c, col, 0.0), axis=0, keepdims=True)


def two_rows(row, width):
    high = rounded(row)
    both = jnp.concatenate([high, row - high], axis=0)
    return jnp.concatenate([both, jnp.zeros((2, width - row.shape[1]), F32)], axis=1)


def logit_kernel(share, given, peers, where_ref, un_ref, row_ref, id_ref, nat_ref, *rest):
    slots = where_ref.shape[0] - 1
    slot_refs, rest = rest[:given], rest[given:]
    part_ref, square_ref, score_ref = rest[:3]
    msg_refs, acc = rest[3 : 3 + peers], rest[-1]
    at = 0
    for slot_ref in slot_refs:
        for k in range(slot_ref.shape[0] // share):
            acc[pl.ds(pl.multiple_of(where_ref[at] * share, share), share), :] = slot_ref[k * share : (k + 1) * share, :]
            at += 1
    values = acc[...]
    total = values.shape[0]
    square = as_row(jnp.sum(values * values, axis=1, keepdims=True), total)
    square_ref[...] = square
    part = jnp.dot(values.astype(BF16), un_ref[...], preferred_element_type=F32)
    part_ref[...] = part
    muts = row_ref.shape[0]
    vocab = part.shape[1]
    high = part.astype(BF16)
    low = (part - high.astype(F32)).astype(BF16)
    words = lax.broadcasted_iota(jnp.int32, (total, vocab), 1)
    both = high.astype(F32) + low.astype(F32)
    native = as_row(jnp.sum(jnp.where(words == nat_ref[...], both, 0.0), axis=1, keepdims=True), total)
    spots = lax.broadcasted_iota(jnp.int32, (muts, total), 1)
    hit = spots == row_ref[...]
    onehot = hit.astype(BF16)
    picked = jnp.dot(onehot, high, preferred_element_type=F32) + jnp.dot(onehot, low, preferred_element_type=F32)
    words = lax.broadcasted_iota(jnp.int32, (muts, vocab), 1)
    chosen = jnp.sum(jnp.where(words == id_ref[...], picked, 0.0), axis=1, keepdims=True)
    base = jnp.sum(jnp.where(hit, native, 0.0), axis=1, keepdims=True)
    score = as_row(chosen - base, muts)
    score_ref[...] = score
    if peers:
        me = where_ref[slots]
        extra = jnp.concatenate(
            [two_rows(square, vocab), two_rows(score, vocab), jnp.zeros((4, vocab), F32)], axis=0
        ).astype(BF16)
        for k in range(1, peers + 1):
            their = part_ref[pl.ds(pl.multiple_of((me ^ k) * share, share), share), :]
            msg_refs[k - 1][0:share, :] = their.astype(BF16)
            msg_refs[k - 1][share : share + 8, :] = extra


def logit_part(share, where, slots, un, mut_row, mut_id, mut_nat, peers):
    wide = slots[0].shape[1]
    total = share * (where.shape[0] - 1)
    vocab = un.shape[1]
    muts = mut_row.shape[0]
    whole = pl.BlockSpec(memory_space=pltpu.VMEM)
    return pl.pallas_call(
        functools.partial(logit_kernel, share, len(slots), peers),
        in_specs=[pl.BlockSpec(memory_space=pltpu.SMEM)] + [whole] * (4 + len(slots)),
        out_specs=[whole] * (3 + peers),
        out_shape=[
            jax.ShapeDtypeStruct((total, vocab), F32),
            jax.ShapeDtypeStruct((1, total), F32),
            jax.ShapeDtypeStruct((1, muts), F32),
        ]
        + [jax.ShapeDtypeStruct((share + 8, vocab), BF16)] * peers,
        scratch_shapes=[pltpu.VMEM((total, wide), F32)],
        compiler_params=SMALL,
        name="logit_part",
    )(where, un, mut_row, mut_id, mut_nat, *slots)


def final_kernel(feats, share, where_ref, log_ref, square_ref, score_ref, nat_ref, row_ref, *rest):
    msg_refs, out_ref = rest[:-1], rest[-1]
    me, piece = where_ref[0], where_ref[1]
    vocab = log_ref.shape[1]
    total = square_ref.shape[1]
    muts = score_ref.shape[1]
    width = out_ref.shape[1]
    if msg_refs:
        logits = log_ref[pl.ds(pl.multiple_of(me * share, share), share), :]
    else:
        logits = log_ref[...]
    square, score = square_ref[...], score_ref[...]
    for msg_ref in msg_refs:
        logits = logits + msg_ref[0:share, :].astype(F32)
        extra = msg_ref[share : share + 8, :].astype(F32)
        square = square + (extra[0:1, 0:total] + extra[1:2, 0:total])
        score = score + (extra[2:3, 0:muts] + extra[3:4, 0:muts])
    scale_row = lax.rsqrt(square / feats + EPS)
    r = lax.broadcasted_iota(jnp.int32, (share, total), 0)
    c = lax.broadcasted_iota(jnp.int32, (share, total), 1)
    scale = jnp.sum(jnp.where(c == r + me * share, scale_row, 0.0), axis=1, keepdims=True)
    logits = logits * scale
    top = jnp.max(logits, axis=1, keepdims=True)
    norm = top + jnp.log(jnp.sum(jnp.exp(logits - top), axis=1, keepdims=True))
    words = lax.broadcasted_iota(jnp.int32, (share, vocab), 1)
    native = nat_ref[pl.ds(pl.multiple_of(me * share, share), share), :]
    like = jnp.sum(jnp.where(words == native, logits, 0.0), axis=1, keepdims=True) - norm
    r = lax.broadcasted_iota(jnp.int32, (share, width), 0)
    c = lax.broadcasted_iota(jnp.int32, (share, width), 1)
    out_ref[0:1, :] = jnp.sum(jnp.where(c == r + piece * share, like, 0.0), axis=0, keepdims=True)
    r = lax.broadcasted_iota(jnp.int32, (muts, total), 0)
    c = lax.broadcasted_iota(jnp.int32, (muts, total), 1)
    at_mut = jnp.sum(jnp.where(c == row_ref[...], scale_row, 0.0), axis=1, keepdims=True)
    out_ref[1:2, 0:muts] = score * as_row(at_mut, muts)


def final_part(feats, share, where, logits, squares, scores, nat, mut_row, msgs, width):
    whole = pl.BlockSpec(memory_space=pltpu.VMEM)
    return pl.pallas_call(
        functools.partial(final_kernel, float(feats), share),
        in_specs=[pl.BlockSpec(memory_space=pltpu.SMEM)] + [whole] * (5 + len(msgs)),
        out_specs=whole,
        out_shape=jax.ShapeDtypeStruct((2, width), F32),
        compiler_params=SMALL,
        name="final_part",
    )(where, logits, squares, scores, nat, mut_row, *msgs)


def total_kernel(*refs):
    like_ref, score_ref = refs[-2:]
    total = functools.reduce(lambda p, q: p + q, [ref[...] for ref in refs[:-2]])
    like_ref[...] = total[0:1, 0 : like_ref.shape[1]]
    score_ref[...] = total[1:2, 0 : score_ref.shape[1]]


def total_part(pieces, rows, muts):
    whole = pl.BlockSpec(memory_space=pltpu.VMEM)
    return pl.pallas_call(
        total_kernel,
        in_specs=[whole] * len(pieces),
        out_specs=[whole] * 2,
        out_shape=[jax.ShapeDtypeStruct((1, rows), F32), jax.ShapeDtypeStruct((1, muts), F32)],
        compiler_params=SMALL,
        name="total_part",
    )(*pieces)


def choose_kernel(place_ref, *refs):
    sources, (out_ref, sem) = refs[:-2], refs[-2:]
    for k, source in enumerate(sources):

        @pl.when(place_ref[0] == k)
        def _():
            copy = pltpu.make_async_copy(source, out_ref, sem)
            copy.start()
            copy.wait()


def choose(place, sources):
    return pl.pallas_call(
        choose_kernel,
        in_specs=[pl.BlockSpec(memory_space=pltpu.SMEM)] + [pl.BlockSpec(memory_space=pltpu.HBM)] * len(sources),
        out_specs=in_vmem(),
        out_shape=pltpu.VMEM(sources[0].shape, sources[0].dtype),
        scratch_shapes=[pltpu.SemaphoreType.DMA],
        compiler_params=SMALL,
        name="choose",
    )(place, *[pltpu.with_memory_space_constraint(v, pltpu.HBM) for v in sources])


def feature_rows(unembed, norm_gain, rows_wanted, z, m):
    count, shards = lax.axis_size("ctx"), lax.axis_size("mp")
    held = unembed.shape[0]
    scaled = (unembed.astype(F32) * norm_gain[:, None]).astype(BF16)
    if held % rows_wanted != 0:
        every = lax.all_gather(scaled, "mp", axis=0, tiled=True)
        return lax.dynamic_slice_in_dim(every, z * rows_wanted, rows_wanted, 0)
    ratio = held // rows_wanted
    piece = lax.dynamic_slice_in_dim(scaled, (z % ratio) * rows_wanted, rows_wanted, 0)
    copies = [piece]
    for k in range(1, shards):
        owner = [i // ratio for i in range(count)]
        pairs = [(i * shards + owner[i], i * shards + (owner[i] ^ k)) for i in range(count)]
        copies.append(lax.ppermute(piece, ("ctx", "mp"), pairs))
    return choose((m ^ (z // ratio)).astype(jnp.int32)[None], copies)


def half_kernel(groups, which_ref, weight_ref, *refs):
    out_ref = refs[-1]
    half = refs[0].shape[0] // 2
    rows = pl.ds(pl.multiple_of(which_ref[0] * half, half), half)
    parts, at = [], 0
    for size in groups:
        parts.append(functools.reduce(lambda p, q: p + q, [ref[rows, :] for ref in refs[at : at + size]]))
        at += size
    block = parts[0] if len(parts) == 1 else jnp.concatenate(parts, axis=0)
    out_ref[...] = jnp.dot(block, weight_ref[...], preferred_element_type=F32).astype(out_ref.dtype)


def both_kernel(groups, which_ref, weight_ref, *refs):
    parts, (send_ref, keep_ref) = refs[:-2], refs[-2:]
    half = parts[0].shape[0] // 2
    for out_ref, which in ((send_ref, 1 - which_ref[0]), (keep_ref, which_ref[0])):
        rows = pl.ds(pl.multiple_of(which * half, half), half)
        at = 0
        for k, size in enumerate(groups):
            block = functools.reduce(lambda p, q: p + q, [ref[rows, :] for ref in parts[at : at + size]])
            at += size
            value = jnp.dot(block, weight_ref[...], preferred_element_type=F32)
            out_ref[k * half : (k + 1) * half, :] = value.astype(out_ref.dtype)


def both_parts(which, weight, blocks):
    rows = len(blocks) * (blocks[0][0].shape[0] // 2)
    flat = [part for block in blocks for part in block]
    return pl.pallas_call(
        functools.partial(both_kernel, tuple(len(block) for block in blocks)),
        in_specs=[pl.BlockSpec(memory_space=pltpu.SMEM)] + [in_vmem()] * (1 + len(flat)),
        out_specs=[in_vmem()] * 2,
        out_shape=[jax.ShapeDtypeStruct((rows, weight.shape[1]), dtype) for dtype in (BF16, F32)],
        compiler_params=SMALL,
        name="both_parts",
    )(which.astype(jnp.int32)[None], weight, *flat)


def half_part(which, weight, blocks, dtype):
    rows = len(blocks) * (blocks[0][0].shape[0] // 2)
    flat = [part for block in blocks for part in block]
    return pl.pallas_call(
        functools.partial(half_kernel, tuple(len(block) for block in blocks)),
        in_specs=[pl.BlockSpec(memory_space=pltpu.SMEM)] + [in_vmem()] * (1 + len(flat)),
        out_specs=in_vmem(),
        out_shape=jax.ShapeDtypeStruct((rows, weight.shape[1]), dtype),
        compiler_params=SMALL,
        name="half_part",
    )(which.astype(jnp.int32)[None], weight, *flat)


def project(blocks, weight, m, hurry):
    shards, count = lax.axis_size("mp"), len(blocks)
    if shards == 1:
        whole = [functools.reduce(lambda p, q: p + q, block) for block in blocks]
        return jnp.dot(jnp.concatenate(whole, axis=0), weight, preferred_element_type=F32)
    bit, value = 1, None
    while bit < shards:
        upper = (m // bit) % 2
        if value is None and not hurry:
            send, keep = both_parts(upper, weight, blocks)
        elif value is None:
            send = half_part(1 - upper, weight, blocks, BF16)
            keep = half_part(upper, weight, blocks, F32)
        else:
            half = value.shape[0] // count // 2
            pieces = value.reshape(count, 2, half, value.shape[1])
            keep = lax.dynamic_index_in_dim(pieces, upper, 1, False).reshape(count * half, value.shape[1])
            send = lax.dynamic_index_in_dim(pieces, 1 - upper, 1, False).reshape(count * half, value.shape[1])
            send = send.astype(BF16)
        got = swap(send, "mp", bit)
        value = keep + got.astype(F32)
        bit *= 2
    return value


def row_piece(m):
    shards = lax.axis_size("mp")
    piece, bit = 0, 1
    while bit < shards:
        piece = piece * 2 + (m // bit) % 2
        bit *= 2
    return piece


def body(streams, short_filter, mode_params, out_weight, norm_gain, unembed, native, mut_pos, mut_ids):
    rows, _ = streams.shape[1:]
    count, shards = lax.axis_size("ctx"), lax.axis_size("mp")
    z = lax.axis_index("ctx")
    quick = count == 4
    modes_t = jnp.swapaxes(mode_params, 1, 2)
    me = z.astype(jnp.int32)[None]
    prod, gate_stream, msg, filt, modes_t = end_part(streams, short_filter, modes_t, native)
    y, gate, start = local_part(filt, modes_t, prod, gate_stream)
    if quick:
        msgs = [msg]
        for k in range(1, count):
            msgs.append(swap(msg, "ctx", k))
        gated, nat_rows = carry_part(me, filt, modes_t, y, gate, start, msgs, False)
    else:
        every = lax.all_gather(msg, "ctx")
        gated, nat_rows = carry_part(me, filt, modes_t, y, gate, start, [every], True)
    gated, nat_rows, native, mut_pos, mut_ids, z, m, norm_gain = lax.optimization_barrier(
        (gated, nat_rows, native, mut_pos, mut_ids, z, lax.axis_index("mp"), norm_gain)
    )
    un = feature_rows(unembed, norm_gain, out_weight.shape[1], z, m)
    piece = row_piece(m)
    share = rows // shards
    nat = (nat_rows[:, :rows] * 256.0 + nat_rows[:, rows : 2 * rows]).astype(jnp.int32)
    nat_col = lax.dynamic_slice_in_dim(nat, piece * share, share, 1).reshape(count * share, 1)
    block, inner = mut_pos // rows, mut_pos % rows
    mut_row = jnp.where(inner // share == piece, block * share + inner % share, -1)[:, None]
    mut_col = mut_ids[:, None]

    if quick:
        middle = [(1, 2), (2, 1)]
        beside = swap(gated, "ctx", 1)
        mid_a = lax.ppermute(gated, "ctx", middle)
        mid_b = lax.ppermute(beside, "ctx", middle)
        far_a = swap(mid_a, "ctx", 1)
        far_b = swap(mid_b, "ctx", 1)
        mid_here = bring(gated, mid_b)
        groups = [[[gated], [beside]], [[mid_a, far_a]], [[mid_here, far_b]]]
        low = z < 2
        where = [z, z ^ 1, jnp.where(low, 2, 1), jnp.where(low, 3, 0)]
    else:
        every = lax.all_gather(gated, "ctx")
        groups = [[[every[b]]] for b in range(count)]
        where = list(range(count))
    where = jnp.stack([jnp.asarray(w, jnp.int32) for w in where + [z]])
    if quick:
        out_weight = bring(gated, out_weight)
    slots = []
    for k, blocks in enumerate(groups):
        slots.append(project(blocks, out_weight, m, k != 1))
    peers = count - 1 if quick else 0
    part, squares, scores, *msgs = logit_part(share, where, slots, un, mut_row, mut_col, nat_col, peers)
    if quick:
        for k in range(1, count):
            msgs[k - 1] = swap(msgs[k - 1], "ctx", k)
    else:
        part = lax.psum_scatter(part, "ctx", scatter_dimension=0, tiled=True)
        squares = lax.psum(squares, "ctx")
        scores = lax.psum(scores, "ctx")

    spot = jnp.stack([z, piece]).astype(jnp.int32)
    feats = norm_gain.shape[0] * shards
    span = max(rows, mut_pos.shape[0])
    result = final_part(feats, share, spot, part, squares, scores, nat_col, mut_row, msgs, span)
    pieces = [result]
    for k in range(1, shards):
        pieces.append(swap(result, "mp", k))
    like, score = total_part(pieces, rows, mut_pos.shape[0])
    return like[0], score[0]


def solution(mesh):
    in_specs = (
        P(None, ("groups", "ctx"), "mp"),
        P(None, None, "mp"),
        P(None, "mp", None),
        P("mp", "ctx"),
        P("mp"),
        P("mp", None),
        P(("groups", "ctx")),
        P("groups"),
        P("groups"),
    )
    out_specs = (P(("groups", "ctx")), P("groups"))
    return jax.shard_map(body, mesh=mesh, in_specs=in_specs, out_specs=out_specs, check_vma=False)
```
